32 devices in a mesh: batch: 8 (over y, x, core), tensor: 4 (over z).
Axes of the slice: x: 2, y: 2, z: 4, core: 2. Of those that a mesh axis runs over, the one named last changes fastest.
Arguments:
- patches: bfloat16 [16384, 48], P(('batch', 'tensor')), may hold values from -6 to 6
- valid_mask: int32 [16384], P('batch'), may hold values 0 or 1
- class_ids: int32 [64], P(('batch', 'tensor')), may hold values from 0 to 999
- embed_weight: bfloat16 [48, 768], replicated, may hold values from -0.875 to 0.875
- embed_bias: float32 [768], replicated, may hold values from -3 to 3
- position_table: bfloat16 [256, 768], replicated, may hold values from -3 to 3
- class_table: bfloat16 [1000, 768], replicated, may hold values from -3 to 3
- attn_gain: float32 [2, 768], replicated, may hold values from 0.5 to 1.5
- attn_offset: float32 [2, 768], replicated, may hold values from -2 to 2
- attend_weight: bfloat16 [2, 3, 768, 768], P(None, None, None, 'tensor'), may hold values from -0.21875 to 0.21875
- merge_weight: bfloat16 [2, 768, 768], P(None, 'tensor'), may hold values from -0.625 to 0.625
- mlp_gain: float32 [2, 768], replicated, may hold values from 0.5 to 1.5
- mlp_offset: float32 [2, 768], replicated, may hold values from -2 to 2
- up_weight: bfloat16 [2, 768, 3072], P(None, None, 'tensor'), may hold values from -0.21875 to 0.21875
- up_bias: float32 [2, 3072], P(None, 'tensor'), may hold values from -3 to 3
- down_weight: bfloat16 [2, 3072, 768], P(None, 'tensor'), may hold values from -0.109375 to 0.109375
- down_bias: float32 [2, 768], replicated, may hold values from -2 to 2
- final_gain: float32 [768], replicated, may hold values from 0.5 to 1.5
- final_offset: float32 [768], replicated, may hold values from -2 to 2
- head_weight: bfloat16 [768, 96], replicated, may hold values from -0.109375 to 0.109375
- head_bias: float32 [96], replicated, may hold values from -2 to 2
- latent_cot: float32 [16384, 48], P(('batch', 'tensor')), may hold values from -6 to 6
- logdet_cot: float32 [64], P(('batch', 'tensor')), may hold values from -0.6 to 0.6
Outputs:
- latents: float32 [16384, 48], P(('batch', 'tensor'))
- log_det: float32 [64], P(('batch', 'tensor'))
- patches_grad: float32 [16384, 48], P(('batch', 'tensor'))
- embed_weight_grad: float32 [48, 768], replicated
- embed_bias_grad: float32 [768], replicated
- position_grad: float32 [256, 768], replicated
- class_grad: float32 [1000, 768], replicated
- attn_gain_grad: float32 [2, 768], replicated
- attn_offset_grad: float32 [2, 768], replicated
- attend_weight_grad: float32 [2, 3, 768, 768], P(None, None, None, 'tensor')
- merge_weight_grad: float32 [2, 768, 768], P(None, 'tensor')
- mlp_gain_grad: float32 [2, 768], replicated
- mlp_offset_grad: float32 [2, 768], replicated
- up_weight_grad: float32 [2, 768, 3072], P(None, None, 'tensor')
- up_bias_grad: float32 [2, 3072], P(None, 'tensor')
- down_weight_grad: float32 [2, 3072, 768], P(None, 'tensor')
- down_bias_grad: float32 [2, 768], replicated
- final_gain_grad: float32 [768], replicated
- final_offset_grad: float32 [768], replicated
- head_weight_grad: float32 [768, 96], replicated
- head_bias_grad: float32 [96], replicated
The draws below stay inside these ranges and needn't reach their ends.
Inputs may be any that keep to these rules, and one draw needn't show every extreme that they name: `valid_mask`: 1 marks a valid patch, 0 a masked one.
All inputs are finite; a program needn't handle non-finite values. No bound on the sum of `valid_mask` on one device may be relied on, other than what follows from the above.
Results may differ from the reference program's by a relative error of at most 0.017.
Values may be sent and summed in bfloat16 or wider, within the bound.
A program may use at most 256 MiB of HBM per device.

```python
import jax
import jax.numpy as jnp
from jax import lax

D = 768
HEADS = 12
HEAD_DIM = 64
FF = 3072
P_SIZE = 256
PV = 48
CLASSES = 1000
NL = 2
IMAGES = 64
TOKENS = 16384


def with_ends(array, rng, low, top_value):
    extent = array.shape
    spot = [jax.random.randint(jax.random.fold_in(rng, axis), (), 0, extent[axis]) for axis in range(len(extent))]
    array = array.at[tuple(spot)].set(low)
    longest = extent.index(max(extent))
    spot[longest] = (spot[longest] + 1) % extent[longest]
    return array.at[tuple(spot)].set(top_value)


def steps_of(key, dims, split, low, largest):
    factor_of = 1.0
    for axis_at, shards_of in split:
        heights = jax.random.uniform(jax.random.fold_in(jax.random.fold_in(key, 6), axis_at), (shards_of,), jnp.float32, low / len(split), largest / len(split))
        factor_of = factor_of * jnp.repeat(jnp.exp(heights), dims[axis_at] // shards_of).reshape((-1,) + (1,) * (len(dims) - 1 - axis_at))
    return factor_of


def scatter_about(stream_key, dims, scale, limit, pieces=(), held_as=jnp.bfloat16):
    loudness = steps_of(stream_key, dims, pieces, -0.22, 0.18) if pieces else 1.0
    result = jax.random.normal(stream_key, dims, jnp.float32) * scale * loudness
    return jnp.minimum(jnp.maximum(result, -limit), limit).astype(held_as)


def setup_inputs(seed: int = 0) -> dict:
    key_list = jax.random.split(jax.random.key(seed), 24)
    return {
        "patches": scatter_about(key_list[0], (TOKENS, PV), 1.0, 6.0, ((0, 32),)),
        "valid_mask": with_ends((jax.random.randint(key_list[1], (TOKENS,), 0, 8) < 7).astype(jnp.int32), jax.random.fold_in(key_list[1], 1), 0, 1),
        "class_ids": with_ends(jax.random.randint(key_list[2], (IMAGES,), 0, CLASSES), jax.random.fold_in(key_list[2], 1), 0, CLASSES - 1).astype(jnp.int32),
        "embed_weight": scatter_about(key_list[3], (PV, D), PV ** -0.5, 0.875),
        "embed_bias": scatter_about(key_list[4], (D,), 0.5, 3.0, (), jnp.float32),
        "position_table": scatter_about(key_list[5], (P_SIZE, D), 0.5, 3.0),
        "class_table": scatter_about(key_list[6], (CLASSES, D), 0.5, 3.0),
        "attn_gain": jnp.clip(1.0 + 0.1 * jax.random.normal(key_list[7], (NL, D), jnp.float32), 0.5, 1.5),
        "attn_offset": scatter_about(key_list[8], (NL, D), 0.3, 2.0, (), jnp.float32),
        "attend_weight": scatter_about(key_list[9], (NL, 3, D, D), D ** -0.5, 0.21875, ((3, 4),)),
        "merge_weight": scatter_about(key_list[10], (NL, D, D), (D // 8) ** -0.5, 0.625, ((1, 4),)),
        "mlp_gain": jnp.clip(1.0 + 0.1 * jax.random.normal(key_list[11], (NL, D), jnp.float32), 0.5, 1.5),
        "mlp_offset": scatter_about(key_list[12], (NL, D), 0.3, 2.0, (), jnp.float32),
        "up_weight": scatter_about(key_list[13], (NL, D, FF), D ** -0.5, 0.21875, ((2, 4),)),
        "up_bias": scatter_about(key_list[14], (NL, FF), 0.5, 3.0, ((1, 4),), jnp.float32),
        "down_weight": scatter_about(key_list[15], (NL, FF, D), FF ** -0.5, 0.109375, ((1, 4),)),
        "down_bias": scatter_about(key_list[16], (NL, D), 0.3, 2.0, (), jnp.float32),
        "final_gain": jnp.clip(1.0 + 0.1 * jax.random.normal(key_list[17], (D,), jnp.float32), 0.5, 1.5),
        "final_offset": scatter_about(key_list[18], (D,), 0.3, 2.0, (), jnp.float32),
        "head_weight": scatter_about(key_list[19], (D, 2 * PV), (4 * D) ** -0.5, 0.109375),
        "head_bias": scatter_about(key_list[20], (2 * PV,), 0.3, 2.0, (), jnp.float32),
        "latent_cot": scatter_about(key_list[21], (TOKENS, PV), 1.0, 6.0, ((0, 32),), jnp.float32),
        "logdet_cot": scatter_about(key_list[22], (IMAGES,), 0.1, 0.6, ((0, 32),), jnp.float32),
    }


@jax.custom_vjp
def low(v):
    return lax.optimization_barrier(v.astype(jnp.bfloat16)).astype(jnp.float32)

@jax.custom_vjp
def low_back(v):
    return v

def low_keep(v):
    return (low(v), None)

def low_pass(kept, grad):
    return (grad,)

def back_keep(v):
    return (v, None)

def back_low(kept, grad):
    return (low(grad),)
low.defvjp(low_keep, low_pass)
low_back.defvjp(back_keep, back_low)
EPSILON = 1e-05
NEGATIVE = -1000000000.0

def matmul(former, latter):
    return jnp.dot(former, latter, precision=lax.Precision.HIGHEST, preferred_element_type=jnp.float32)

def layer_norm(values, norm_gain, norm_offset):
    center = values - lax.optimization_barrier(jnp.mean(values, axis=-1, keepdims=True))
    spread = lax.optimization_barrier(jnp.mean(center * center, axis=-1, keepdims=True))
    return center * lax.rsqrt(spread + EPSILON) * norm_gain + norm_offset

def attention(queries, keys, values, allowed):
    scaling = HEAD_DIM ** (-0.5)
    scores = low_back(jnp.einsum('qhd,khd->hqk', queries, keys, precision=lax.Precision.HIGHEST) * scaling)
    scores = jnp.where(allowed[None], scores, NEGATIVE)
    log_total = jax.nn.logsumexp(scores, axis=-1, keepdims=True)
    probs = low(jnp.exp(scores - log_total))
    return jnp.einsum('hqk,khd->qhd', probs, values, precision=lax.Precision.HIGHEST)

def forward(params, patch_part, valid_part, label_part):
    embed_weight, embed_bias, position_table, class_table, attn_gain, attn_offset, attend_weight, merge_weight, mlp_gain, mlp_offset, up_weight, up_bias, down_weight, down_bias, final_gain, final_offset, head_weight, head_bias = params
    row_count = patch_part.shape[0]
    per_image = row_count // P_SIZE
    hidden = matmul(patch_part, embed_weight) + embed_bias
    hidden = hidden + jnp.tile(position_table, (per_image, 1))
    hidden = hidden + jnp.repeat(class_table[label_part], P_SIZE, axis=0)
    position = jnp.arange(row_count, dtype=jnp.int32)
    image_of = position // P_SIZE
    allowed = (image_of[:, None] == image_of[None, :]) & (position[None, :] <= position[:, None])
    allowed = allowed & ((valid_part[None, :] > 0.5) | (position[None, :] == position[:, None]))
    for layer_index in range(NL):
        normed = low(layer_norm(hidden, attn_gain[layer_index], attn_offset[layer_index]))
        qkv = jnp.einsum('rd,cde->rce', normed, attend_weight[layer_index], precision=lax.Precision.HIGHEST)
        qkv = low(low_back(qkv))
        queries = qkv[:, 0].reshape(row_count, HEADS, HEAD_DIM)
        keys = qkv[:, 1].reshape(row_count, HEADS, HEAD_DIM)
        values = qkv[:, 2].reshape(row_count, HEADS, HEAD_DIM)
        mixed = low(low_back(attention(queries, keys, values, allowed))).reshape(row_count, D)
        hidden = hidden + low_back(matmul(mixed, merge_weight[layer_index]))
        normed = low(layer_norm(hidden, mlp_gain[layer_index], mlp_offset[layer_index]))
        inner = low_back(matmul(normed, up_weight[layer_index]) + up_bias[layer_index])
        active = low(jax.nn.gelu(inner, approximate=False))
        hidden = hidden + low_back(matmul(active, down_weight[layer_index]) + down_bias[layer_index])
    final = low(layer_norm(hidden, final_gain, final_offset))
    head_out = low_back(matmul(final, head_weight) + head_bias)
    starts = (position % P_SIZE == 0)[:, None]
    previous = jnp.concatenate([jnp.zeros((1, 2 * PV), jnp.float32), head_out[:-1]], axis=0)
    previous = jnp.where(starts, 0.0, previous)
    shift_part = previous[:, :PV]
    log_scale = previous[:, PV:]
    live_mask = valid_part[:, None]
    latents = live_mask * (patch_part - shift_part) * jnp.exp(-log_scale) + (1.0 - live_mask) * patch_part
    log_det = -lax.optimization_barrier(jnp.sum((live_mask * log_scale).reshape(per_image, P_SIZE * PV), axis=1))
    return (latents, log_det)

def reference(patches, valid_mask, class_ids, embed_weight, embed_bias, position_table, class_table, attn_gain, attn_offset, attend_weight, merge_weight, mlp_gain, mlp_offset, up_weight, up_bias, down_weight, down_bias, final_gain, final_offset, head_weight, head_bias, latent_cot, logdet_cot):
    params = tuple((entry.astype(jnp.float32) for entry in (embed_weight, embed_bias, position_table, class_table, attn_gain, attn_offset, attend_weight, merge_weight, mlp_gain, mlp_offset, up_weight, up_bias, down_weight, down_bias, final_gain, final_offset, head_weight, head_bias)))
    groups = TOKENS // (2 * P_SIZE)
    patch_groups = patches.astype(jnp.float32).reshape(groups, 2 * P_SIZE, PV)
    valid_groups = valid_mask.astype(jnp.float32).reshape(groups, 2 * P_SIZE)
    label_groups = class_ids.reshape(groups, 2)
    cot_groups = latent_cot.astype(jnp.float32).reshape(groups, 2 * P_SIZE, PV)
    det_groups = logdet_cot.astype(jnp.float32).reshape(groups, 2)

    def scan_step(running, inputs):
        patch_part, valid_part, label_part, cot_part, det_part = inputs

        def apply_block(params_in, patch_in):
            return forward(params_in, patch_in, valid_part, label_part)
        outputs, pullback = jax.vjp(apply_block, params, patch_part)
        grad_params, grad_patch = pullback((cot_part, det_part))
        running = jax.tree.map(lambda earlier, addend: earlier + addend, running, grad_params)
        return (running, (outputs[0], outputs[1], grad_patch))
    zero_init = jax.tree.map(jnp.zeros_like, params)
    totals, stacked = lax.scan(scan_step, zero_init, (patch_groups, valid_groups, label_groups, cot_groups, det_groups))
    latents = stacked[0].reshape(TOKENS, PV)
    log_det = stacked[1].reshape(IMAGES)
    patches_grad = stacked[2].reshape(TOKENS, PV)
    return (latents, log_det, patches_grad, totals[0], totals[1], totals[2], totals[3], totals[4], totals[5], totals[6], totals[7], totals[8], totals[9], totals[10], totals[11], totals[12], totals[13], totals[14], totals[15], totals[16], totals[17])
```

```python
import functools

import jax
import jax.numpy as jnp
from jax import lax
from jax.experimental import pallas as pl
from jax.experimental.pallas import tpu as pltpu
from jax.sharding import PartitionSpec as P

D = 768
HEAD_DIM = 64
P_SIZE = 256
PV = 48
CLASSES = 1000
NL = 2


EPSILON = 1e-05
NEGATIVE = -1000000000.0
HIGHEST = lax.Precision.HIGHEST


def layer_norm(values, norm_gain, norm_offset):
    center = values - jnp.mean(values, axis=-1, keepdims=True)
    spread = jnp.mean(center * center, axis=-1, keepdims=True)
    return center * lax.rsqrt(spread + EPSILON) * norm_gain + norm_offset


def norm_backward(values, norm_gain, norm_offset, upstream):
    outputs, pullback = jax.vjp(layer_norm, values, norm_gain, norm_offset)
    return pullback(upstream)


def gelu_exact(values):
    return jax.nn.gelu(values, approximate=False)


def product(former, latter):
    return jnp.dot(former, latter, preferred_element_type=jnp.float32)


def product_back(former, latter):
    return lax.dot_general(
        former, latter, (((1,), (1,)), ((), ())), preferred_element_type=jnp.float32
    )


def contract_rows(former, latter):
    return lax.dot_general(
        former, latter, (((0,), (0,)), ((), ())), preferred_element_type=jnp.float32
    )


def precise_rows(former, latter):
    return lax.dot_general(
        former,
        latter,
        (((0,), (0,)), ((), ())),
        precision=HIGHEST,
        preferred_element_type=jnp.float32,
    )


def build_allowed(mask_rows, span):
    row_index = lax.broadcasted_iota(jnp.int32, (span, span), 0)
    col_index = lax.broadcasted_iota(jnp.int32, (span, span), 1)
    causal = (row_index // P_SIZE == col_index // P_SIZE) & (col_index <= row_index)
    key_valid = mask_rows.reshape(mask_rows.shape[0] // span, 1, span) > 0
    return causal[None] & (key_valid | (row_index == col_index)[None])


def gather_rows(parts):
    batch_count = lax.axis_size("batch")
    batch_index = lax.axis_index("batch")
    pieces = []
    for part in parts:
        rows = part.shape[0] // batch_count
        pieces.append(lax.dynamic_slice_in_dim(part, batch_index * rows, rows, 0))
    piece = jnp.concatenate(pieces, axis=0)
    group = lax.all_gather(piece, "tensor", axis=0)
    whole = lax.all_gather(group, "batch", axis=0)
    results = []
    begin = 0
    for entry in pieces:
        results.append(whole[:, :, begin : begin + entry.shape[0]])
        begin += entry.shape[0]
    return results


def reduce_rows(parts):
    joined = jnp.concatenate([part.astype(jnp.bfloat16) for part in parts], axis=2)
    over_batch = lax.psum_scatter(joined, "batch", scatter_dimension=0)
    own = lax.psum_scatter(over_batch, "tensor", scatter_dimension=0)
    whole = lax.all_gather(own, "batch", axis=0)
    results = []
    begin = 0
    for part in parts:
        results.append(whole[:, begin : begin + part.shape[2]])
        begin += part.shape[2]
    return results


def to_tensor_major(blocks):
    return jnp.swapaxes(blocks, 0, 1).reshape(-1, blocks.shape[-1])


def to_batch_major(rows):
    batch_count = lax.axis_size("batch")
    tensor_count = lax.axis_size("tensor")
    return jnp.swapaxes(rows.reshape(tensor_count, batch_count, -1, rows.shape[-1]), 0, 1)


def split_blocks(rows):
    batch_count = lax.axis_size("batch")
    tensor_count = lax.axis_size("tensor")
    return rows.reshape(batch_count, tensor_count, -1, rows.shape[-1])


MESH = pl.DeviceIdType.MESH
SWAP_TENSOR = (1, 2, 3)


def place():
    batch_index = lax.axis_index("batch")
    tensor_index = lax.axis_index("tensor")
    return (batch_index // 4, batch_index // 2 % 2, batch_index % 2, tensor_index)


def device_at(y, x, core, z):
    return (y * 4 + x * 2 + core, z)


def flipped(index, bits):
    high, low = index // 2, index % 2
    if bits & 2:
        high = 1 - high
    if bits & 1:
        low = 1 - low
    return high * 2 + low


def greet(devices):
    barrier = pltpu.get_barrier_semaphore()
    for device in devices:
        pl.semaphore_signal(barrier, inc=1, device_id=device, device_id_type=MESH)
    pl.semaphore_wait(barrier, len(devices))


def partners():
    y, x, core, z = place()
    devices = [device_at(y, x, core, flipped(z, bits)) for bits in SWAP_TENSOR]
    devices.append(device_at(y, 1 - x, core, z))
    devices.append(device_at(1 - y, x, core, z))
    devices.append(device_at(y, x, 1 - core, z))
    return devices


def halves(count):
    return (slice(0, (count + 1) // 2), slice((count + 1) // 2, count))


class Copies:
    def __init__(self, send_sems):
        self.send_sems = send_sems
        self.count = 0
        self.sent = []

    def send(self, source, target, recv_sem, device, keep=True):
        copy = pltpu.make_async_remote_copy(
            src_ref=source,
            dst_ref=target,
            send_sem=self.send_sems.at[self.count],
            recv_sem=recv_sem,
            device_id=device,
            device_id_type=MESH,
        )
        self.count += 1
        copy.start()
        if keep:
            self.sent.append(copy)
        return copy

    def finish(self):
        for copy in self.sent:
            copy.wait_send()


def wait_arrival(target, recv_sem, send_sem, device):
    pltpu.make_async_remote_copy(
        src_ref=target,
        dst_ref=target,
        send_sem=send_sem,
        recv_sem=recv_sem,
        device_id=device,
        device_id_type=MESH,
    ).wait_recv()


def spread_piece(ref, lead, b):
    if len(ref.shape) == len(lead) + 4:
        return ref.at[(*lead, slice(None), b)]
    return ref.at[(*lead, b)]


def half_piece(ref, lead, b, side):
    if len(ref.shape) == len(lead) + 4:
        return ref.at[(*lead, halves(ref.shape[len(lead)])[side], b)]
    return ref.at[(*lead, b, halves(ref.shape[len(lead) + 1])[side])]


def gather_kernel(layer_count, *refs):
    per_layer = 4
    units = layer_count * per_layer
    shards = refs[:units]
    bias = refs[units]
    fulls = refs[units + 1 : 2 * units + 1]
    bias_full = refs[2 * units + 1]
    send_sems, z_sems, xy_sems, core_sems, local_sems, bias_sems, spare = refs[2 * units + 2 :]
    y, x, core, z = place()
    b = y * 4 + x * 2 + core
    over_x = y * 4 + (1 - x) * 2 + core
    over_y = (1 - y) * 4 + x * 2 + core
    corner = (1 - y) * 4 + (1 - x) * 2 + core
    at_x = device_at(y, 1 - x, core, z)
    at_y = device_at(1 - y, x, core, z)
    at_core = device_at(y, x, 1 - core, z)
    middle = (z + 1) // 2 % 2
    near = flipped(z, 1)
    across = 3 - z
    far = (z + 2) % 4
    at_near = device_at(y, x, core, near)
    at_across = device_at(y, x, core, across)
    order = (
        near,
        middle * across + (1 - middle) * far,
        middle * far + (1 - middle) * across,
    )
    greet(partners())
    copies = Copies(send_sems)
    conditional = []
    locals_ = []
    for unit in range(units):
        copy = pltpu.make_async_copy(shards[unit], fulls[unit].at[z], local_sems.at[unit])
        copy.start()
        locals_.append(copy)
    copy = pltpu.make_async_copy(bias, bias_full.at[z], local_sems.at[units])
    copy.start()
    locals_.append(copy)
    for entry, bits in enumerate(SWAP_TENSOR):
        copies.send(
            bias,
            bias_full.at[z],
            bias_sems.at[entry],
            device_at(y, x, core, flipped(z, bits)),
        )

    def of_layer(layer):
        return range(layer * per_layer, (layer + 1) * per_layer)

    def send_if_middle(source, target, recv_sem, device):
        slot = send_sems.at[copies.count]
        copies.count += 1
        copy = pltpu.make_async_remote_copy(
            src_ref=source,
            dst_ref=target,
            send_sem=slot,
            recv_sem=recv_sem,
            device_id=device,
            device_id_type=MESH,
        )

        @pl.when(middle == 1)
        def _():
            copy.start()

        conditional.append(copy)

    def begin(layer):
        for unit in of_layer(layer):
            mine = spread_piece(shards[unit], (), b)
            target = spread_piece(fulls[unit], (z,), b)
            copies.send(mine, target, z_sems.at[unit, z], at_near)
            send_if_middle(mine, target, z_sems.at[unit, z], at_across)

    def take_z(layer, step):
        t = order[step]
        for unit in of_layer(layer):
            piece = spread_piece(fulls[unit], (t,), b)
            wait_arrival(piece, z_sems.at[unit, t], spare.at[0], at_near)
            send_if_middle(
                piece, piece, z_sems.at[unit, t], at_across if step == 0 else at_near
            )
        for unit in of_layer(layer):
            piece = spread_piece(fulls[unit], (t,), b)
            copies.send(piece, piece, xy_sems.at[unit, step, 0], at_x)
            copies.send(piece, piece, xy_sems.at[unit, step, 1], at_y)
            copies.send(piece, piece, core_sems.at[unit, step, 0], at_core)

    def take_xy(layer, step):
        t = order[step]
        for unit in of_layer(layer):
            piece = spread_piece(fulls[unit], (t,), over_x)
            wait_arrival(piece, xy_sems.at[unit, step, 0], spare.at[0], at_x)
            first = half_piece(fulls[unit], (t,), over_x, 0)
            copies.send(first, first, xy_sems.at[unit, step, 2], at_y)
            copies.send(piece, piece, core_sems.at[unit, step, 1], at_core)
        for unit in of_layer(layer):
            piece = spread_piece(fulls[unit], (t,), over_y)
            wait_arrival(piece, xy_sems.at[unit, step, 1], spare.at[0], at_y)
            second = half_piece(fulls[unit], (t,), over_y, 1)
            copies.send(second, second, xy_sems.at[unit, step, 3], at_x)
            copies.send(piece, piece, core_sems.at[unit, step, 2], at_core)

    def take_corner(layer, step):
        t = order[step]
        for unit in of_layer(layer):
            first = half_piece(fulls[unit], (t,), corner, 0)
            second = half_piece(fulls[unit], (t,), corner, 1)
            wait_arrival(first, xy_sems.at[unit, step, 2], spare.at[0], at_y)
            wait_arrival(second, xy_sems.at[unit, step, 3], spare.at[0], at_x)
            piece = spread_piece(fulls[unit], (t,), corner)
            copies.send(piece, piece, core_sems.at[unit, step, 3], at_core)

    def take_core(layer, step):
        t = order[step]
        for unit in of_layer(layer):
            for entry, owner in enumerate((b, over_x, over_y, corner)):
                other = owner + 1 - 2 * core
                piece = spread_piece(fulls[unit], (t,), other)
                wait_arrival(piece, core_sems.at[unit, step, entry], spare.at[0], at_core)

    begin(0)
    for layer in range(layer_count):
        take_z(layer, 0)
        take_z(layer, 1)
        if layer:
            take_corner(layer - 1, 1)
        take_xy(layer, 0)
        take_z(layer, 2)
        if layer + 1 < layer_count:
            begin(layer + 1)
        if layer:
            take_corner(layer - 1, 2)
        take_xy(layer, 1)
        take_corner(layer, 0)
        take_xy(layer, 2)
    take_corner(layer_count - 1, 1)
    take_corner(layer_count - 1, 2)
    for layer in range(layer_count):
        for step in range(3):
            take_core(layer, step)
    for entry, bits in enumerate(SWAP_TENSOR):
        wait_arrival(
            bias_full.at[flipped(z, bits)],
            bias_sems.at[entry],
            spare.at[0],
            device_at(y, x, core, flipped(z, bits)),
        )
    for copy in locals_:
        copy.wait()
    copies.finish()

    @pl.when(middle == 1)
    def _():
        for copy in conditional:
            copy.wait_send()


def gather_all(shards, bias):
    units = len(shards)
    outs = [jax.ShapeDtypeStruct((4, *shard.shape), shard.dtype) for shard in shards]
    outs.append(jax.ShapeDtypeStruct((4, *bias.shape), bias.dtype))
    vmem = pl.BlockSpec(memory_space=pltpu.VMEM)
    anywhere = pl.BlockSpec(memory_space=pl.ANY)
    dma = pltpu.SemaphoreType.DMA
    return pl.pallas_call(
        functools.partial(gather_kernel, units // 4),
        out_shape=outs,
        in_specs=[vmem] * (units + 1),
        out_specs=[anywhere] * (units + 1),
        scratch_shapes=[
            dma((3 + units * (2 + 3 * 9),)),
            dma((units, 4)),
            dma((units, 3, 4)),
            dma((units, 3, 4)),
            dma((units + 1,)),
            dma((3,)),
            dma((1,)),
        ],
        compiler_params=pltpu.CompilerParams(collective_id=0, has_side_effects=True),
        name="gather_weights",
    )(*shards, bias)


def add_slab(target, addend):
    target[...] = (target[...].astype(jnp.float32) + addend[...].astype(jnp.float32)).astype(
        target.dtype
    )


ITEM_ORDER = (0, 2, 1, 3)


def reduce_kernel(groups, spread_all, *refs):
    units = sum(len(group) for group in groups)
    grads = refs[:units]
    outs = refs[units : 2 * units]
    own, got_core, got_one, got_two, got_z, result = (
        refs[(2 + entry) * units : (3 + entry) * units] for entry in range(6)
    )
    send_sems, load_sems, step_sems, z_sems, spread_sems, core_sems, all_sems, spare = refs[
        8 * units :
    ]
    y, x, core, z = place()
    at_x = device_at(y, 1 - x, core, z)
    at_y = device_at(1 - y, x, core, z)
    at_core = device_at(y, x, 1 - core, z)
    greet(partners())
    copies = Copies(send_sems)
    conditional = []
    items = [(group, t) for group in groups for t in ITEM_ORDER]
    for group, t in items:
        for unit in group:
            grad = grads[unit]
            copies.send(
                grad.at[t, :, :, :, 1 - core],
                got_core[unit].at[t],
                step_sems.at[unit, 0, t],
                at_core,
            )
            pltpu.make_async_copy(
                grad.at[t, :, :, :, core], own[unit].at[t], load_sems.at[unit, t]
            ).start()

    def take_core_sum(group, t):
        for unit in group:
            grad = grads[unit]
            mine, other = own[unit], got_core[unit]
            pltpu.make_async_copy(
                grad.at[t, :, :, :, core], mine.at[t], load_sems.at[unit, t]
            ).wait()
            wait_arrival(other.at[t], step_sems.at[unit, 0, t], spare.at[0], at_core)
            count = mine.shape[1] * 4

            def body(entry, carry):
                spot = (t, entry // 4, entry // 2 % 2, entry % 2)
                add_slab(mine.at[spot], other.at[spot])
                return carry

            lax.fori_loop(0, count, body, 0)
            if t < 2:
                copies.send(
                    mine.at[t, :, :, 1 - x], got_one[unit].at[t], step_sems.at[unit, 1, t], at_x
                )
            else:
                copies.send(
                    mine.at[t, :, 1 - y], got_one[unit].at[t], step_sems.at[unit, 1, t], at_y
                )

    def take_one(group, t):
        for unit in group:
            mine, other = own[unit], got_one[unit]
            wait_arrival(
                other.at[t], step_sems.at[unit, 1, t], spare.at[0], at_x if t < 2 else at_y
            )
            count = mine.shape[1] * 2

            def body(entry, carry):
                first, second = entry // 2, entry % 2
                if t < 2:
                    add_slab(mine.at[t, first, second, x], other.at[t, first, second])
                else:
                    add_slab(mine.at[t, first, y, second], other.at[t, first, second])
                return carry

            lax.fori_loop(0, count, body, 0)
            if t < 2:
                copies.send(
                    mine.at[t, :, 1 - y, x], got_two[unit].at[t], step_sems.at[unit, 2, t], at_y
                )
            else:
                copies.send(
                    mine.at[t, :, y, 1 - x], got_two[unit].at[t], step_sems.at[unit, 2, t], at_x
                )

    def take_two(group, t):
        for unit in group:
            mine, other = own[unit], got_two[unit]
            wait_arrival(
                other.at[t], step_sems.at[unit, 2, t], spare.at[0], at_y if t < 2 else at_x
            )

            def body(entry, carry):
                add_slab(mine.at[t, entry, y, x], other.at[t, entry])
                return carry

            lax.fori_loop(0, mine.shape[1], body, 0)
            copy = pltpu.make_async_remote_copy(
                src_ref=mine.at[t, :, y, x],
                dst_ref=got_z[unit].at[z],
                send_sem=send_sems.at[copies.count],
                recv_sem=z_sems.at[unit, z],
                device_id=device_at(y, x, core, t),
                device_id_type=MESH,
            )
            copies.count += 1

            @pl.when(z != t)
            def _():
                copy.start()

            conditional.append((t, copy))

    def spot_of(unit, where):
        return outs[unit].at[(z, slice(None), *where)]

    def half_spot(unit, where, side):
        count = outs[unit].shape[1]
        if count > 1:
            return outs[unit].at[(z, halves(count)[side], *where)]
        return outs[unit].at[(z, slice(None), *where, halves(outs[unit].shape[5])[side])]

    def take_z(group):
        for unit in group:
            mine, other, total = own[unit], got_z[unit], result[unit]
            for bits in SWAP_TENSOR:
                t = flipped(z, bits)
                wait_arrival(
                    other.at[t], z_sems.at[unit, t], spare.at[0], device_at(y, x, core, t)
                )

            def body(entry, carry):
                value = mine[z, entry, y, x].astype(jnp.float32)
                for bits in SWAP_TENSOR:
                    value = value + other[flipped(z, bits), entry].astype(jnp.float32)
                total[entry] = value.astype(total.dtype)
                return carry

            lax.fori_loop(0, mine.shape[1], body, 0)
            spot = spot_of(unit, (y, x, core))
            pltpu.make_async_copy(total, spot, load_sems.at[unit, 4]).start()
            copies.send(total, spot, spread_sems.at[unit, 0], at_x)
            copies.send(total, spot, spread_sems.at[unit, 1], at_y)
            copies.send(total, spot, core_sems.at[unit, 0], at_core)

    def take_spread(group):
        for unit in group:
            spot = spot_of(unit, (y, 1 - x, core))
            wait_arrival(spot, spread_sems.at[unit, 0], spare.at[0], at_x)
            first = half_spot(unit, (y, 1 - x, core), 0)
            copies.send(first, first, spread_sems.at[unit, 2], at_y)
            copies.send(spot, spot, core_sems.at[unit, 1], at_core)
            spot = spot_of(unit, (1 - y, x, core))
            wait_arrival(spot, spread_sems.at[unit, 1], spare.at[0], at_y)
            second = half_spot(unit, (1 - y, x, core), 1)
            copies.send(second, second, spread_sems.at[unit, 3], at_x)
            copies.send(spot, spot, core_sems.at[unit, 2], at_core)

    def take_corner(group):
        for unit in group:
            where = (1 - y, 1 - x, core)
            wait_arrival(half_spot(unit, where, 0), spread_sems.at[unit, 2], spare.at[0], at_y)
            wait_arrival(half_spot(unit, where, 1), spread_sems.at[unit, 3], spare.at[0], at_x)
            spot = spot_of(unit, where)
            copies.send(spot, spot, core_sems.at[unit, 3], at_core)

    def take_last(group):
        for unit in group:
            pltpu.make_async_copy(
                result[unit], spot_of(unit, (y, x, core)), load_sems.at[unit, 4]
            ).wait()
            for entry, where in enumerate(((y, x), (y, 1 - x), (1 - y, x), (1 - y, 1 - x))):
                spot = spot_of(unit, (*where, 1 - core))
                wait_arrival(spot, core_sems.at[unit, entry], spare.at[0], at_core)

    def run(step):
        if step < len(items):
            take_core_sum(*items[step])
        if 0 <= step - 1 < len(items):
            take_one(*items[step - 1])
        if 0 <= step - 2 < len(items):
            take_two(*items[step - 2])
        for index, group in enumerate(groups):
            last = 4 * index + 3
            if step == last + 4:
                take_z(group)
            if step == last + 5:
                take_spread(group)
            if step == last + 6:
                take_corner(group)

    for step in range(len(items) + 6):
        run(step)
    for group in groups:
        take_last(group)
    for entry, unit in enumerate(spread_all):
        for bits in SWAP_TENSOR:
            copies.send(
                outs[unit].at[z],
                outs[unit].at[z],
                all_sems.at[entry, bits],
                device_at(y, x, core, flipped(z, bits)),
            )
        for bits in SWAP_TENSOR:
            t = flipped(z, bits)
            wait_arrival(
                outs[unit].at[t], all_sems.at[entry, bits], spare.at[0], device_at(y, x, core, t)
            )
    copies.finish()
    for t, copy in conditional:

        @pl.when(z != t)
        def _(copy=copy):
            copy.wait_send()


def reduce_all(grads, groups, spread_all):
    units = len(grads)
    scratch = []
    for lead in ((4, 2, 2), (4, 2, 2), (4, 2), (4,), (4,), ()):
        for grad in grads:
            count, rows = grad.shape[1], grad.shape[5]
            shape = lead[:1] + (count,) + lead[1:] + (rows, D)
            scratch.append(pltpu.VMEM(shape, jnp.bfloat16))
    dma = pltpu.SemaphoreType.DMA
    anywhere = pl.BlockSpec(memory_space=pl.ANY)
    return pl.pallas_call(
        functools.partial(reduce_kernel, groups, spread_all),
        out_shape=[jax.ShapeDtypeStruct(grad.shape, grad.dtype) for grad in grads],
        in_specs=[anywhere] * units,
        out_specs=[anywhere] * units,
        scratch_shapes=scratch
        + [
            dma((units * 24 + 3 * len(spread_all),)),
            dma((units, 5)),
            dma((units, 3, 4)),
            dma((units, 4)),
            dma((units, 4)),
            dma((units, 4)),
            dma((max(len(spread_all), 1), 4)),
            dma((1,)),
        ],
        compiler_params=pltpu.CompilerParams(
            collective_id=1, has_side_effects=True, vmem_limit_bytes=62 * 1024 * 1024
        ),
        name="reduce_gradients",
    )(*grads)


def fast_mesh():
    return lax.axis_size("batch") == 8 and lax.axis_size("tensor") == 4


def gather_weights(shards, bias):
    if not fast_mesh():
        wholes = [to_tensor_major(blocks) for blocks in gather_rows(shards)]
        return (wholes, lax.all_gather(bias, "tensor", axis=0))
    parts = []
    for shard in shards:
        rows = shard.shape[0]
        parts.append(shard.reshape(8, -1, D) if rows == D else shard.reshape(-1, 8, 8, D))
    results = gather_all(parts, jnp.pad(bias, ((0, 8 - NL), (0, 0))))
    return ([whole.reshape(-1, D) for whole in results[:-1]], results[-1][:, :NL])


def reduce_weights(grads, small):
    if not fast_mesh():
        sums = reduce_rows([to_batch_major(grad) for grad in grads] + [split_blocks(small)])
        small_sum = lax.all_gather(sums[-1], "tensor", axis=1).reshape(-1, D)
        return ([entry.reshape(-1, D) for entry in sums[:-1]], small_sum)
    tensor_index = lax.axis_index("tensor")
    parts = []
    for grad in grads:
        count = 1 if grad.shape[0] == 4 * D else grad.shape[0] // 256
        parts.append(grad.reshape(4, count, 2, 2, 2, -1, D))
    parts.append(small.astype(jnp.bfloat16).reshape(4, 1, 2, 2, 2, -1, D))
    groups = ((4, 5, 6, 7), (0, 1, 2, 3, 8))
    sums = reduce_all(parts, groups, (8,))
    own = [lax.dynamic_index_in_dim(entry, tensor_index, 0, keepdims=False) for entry in sums[:-1]]
    return ([entry.reshape(-1, D) for entry in own], sums[-1].reshape(-1, D))


def head_blocks(qkv_low, tensor_count):
    images = qkv_low.shape[0] // P_SIZE
    blocks = qkv_low.reshape(images, P_SIZE, tensor_count, 3, -1, HEAD_DIM)
    blocks = jnp.transpose(blocks, (3, 0, 2, 4, 1, 5))
    return blocks.reshape(3, images, -1, P_SIZE, HEAD_DIM)


def head_rows(mixed):
    images, heads = mixed.shape[:2]
    return jnp.transpose(mixed, (0, 2, 1, 3)).reshape(images * P_SIZE, heads * HEAD_DIM)


def block_scores(blocks, allowed):
    queries, keys, values = blocks[0], blocks[1], blocks[2]
    scores = jnp.einsum("bhqd,bhkd->bhqk", queries, keys, preferred_element_type=jnp.float32) * (
        HEAD_DIM ** (-0.5)
    )
    scores = jnp.where(allowed[:, None], scores, NEGATIVE)
    return (queries, keys, values, scores)


def attend(blocks, allowed):
    queries, keys, values, scores = block_scores(blocks, allowed)
    log_total = jax.nn.logsumexp(scores, axis=-1, keepdims=True)
    probs_low = jnp.exp(scores - log_total).astype(jnp.bfloat16)
    mixed = jnp.einsum("bhqk,bhkd->bhqd", probs_low, values, preferred_element_type=jnp.float32)
    return (head_rows(mixed.astype(jnp.bfloat16)), log_total)


def attend_back(blocks, allowed, log_total, grad_mixed, tensor_count):
    queries, keys, values, scores = block_scores(blocks, allowed)
    probs_full = jnp.exp(scores - log_total)
    probs_low = probs_full.astype(jnp.bfloat16)
    images = queries.shape[0]
    grad_out = jnp.transpose(grad_mixed.reshape(images, P_SIZE, -1, HEAD_DIM), (0, 2, 1, 3))
    grad_values = jnp.einsum(
        "bhqk,bhqd->bhkd", probs_low, grad_out, preferred_element_type=jnp.float32
    )
    grad_probs = jnp.einsum("bhqd,bhkd->bhqk", grad_out, values, preferred_element_type=jnp.float32)
    inner_sum = jnp.sum(probs_full * grad_probs, axis=-1, keepdims=True)
    grad_scores = (probs_full * (grad_probs - inner_sum)).astype(jnp.bfloat16)
    scaling = HEAD_DIM ** (-0.5)
    grad_queries = (
        jnp.einsum("bhqk,bhkd->bhqd", grad_scores, keys, preferred_element_type=jnp.float32)
        * scaling
    )
    grad_keys = (
        jnp.einsum("bhqk,bhqd->bhkd", grad_scores, queries, preferred_element_type=jnp.float32)
        * scaling
    )
    stacked = jnp.stack([grad_queries, grad_keys, grad_values]).astype(jnp.bfloat16)
    stacked = stacked.reshape(3, images, tensor_count, -1, P_SIZE, HEAD_DIM)
    return jnp.transpose(stacked, (1, 4, 2, 0, 3, 5)).reshape(images * P_SIZE, -1)


def shards(
    patches,
    valid_mask,
    class_ids,
    embed_weight,
    embed_bias,
    position_table,
    class_table,
    attn_gain,
    attn_offset,
    attend_weight,
    merge_weight,
    mlp_gain,
    mlp_offset,
    up_weight,
    up_bias,
    down_weight,
    down_bias,
    final_gain,
    final_offset,
    head_weight,
    head_bias,
    latent_cot,
    logdet_cot,
):
    shard_count = patches.shape[0]
    local_images = shard_count // P_SIZE
    tensor_index = lax.axis_index("tensor")
    tensor_count = lax.axis_size("tensor")
    batch_count = lax.axis_size("batch")
    device_index = lax.axis_index("batch") * tensor_count + tensor_index
    device_count = batch_count * tensor_count
    patch_values = patches.astype(jnp.float32)
    local_valid = lax.dynamic_slice_in_dim(valid_mask, tensor_index * shard_count, shard_count, 0)
    live_mask = local_valid.astype(jnp.float32)[:, None]
    allowed = build_allowed(local_valid, P_SIZE)
    embed_full = embed_weight.astype(jnp.float32)
    shards = []
    for layer_index in range(NL):
        shards.append(jnp.swapaxes(attend_weight[layer_index], 1, 2).reshape(-1, D))
        shards.append(merge_weight[layer_index])
        shards.append(jnp.swapaxes(up_weight[layer_index], 0, 1))
        shards.append(down_weight[layer_index])
    wholes, bias_all = gather_weights(shards, up_bias)
    weights = [
        (*wholes[4 * layer_index : 4 * layer_index + 4], bias_all[:, layer_index].reshape(-1))
        for layer_index in range(NL)
    ]
    choose = class_ids[:, None] == lax.broadcasted_iota(jnp.int32, (local_images, CLASSES), 1)
    class_rows = product(choose.astype(jnp.bfloat16), class_table)
    hidden = product(patches, embed_weight) + embed_bias
    hidden = hidden.reshape(local_images, P_SIZE, D) + position_table.astype(jnp.float32)[None]
    hidden = (hidden + class_rows[:, None]).reshape(shard_count, D)
    stored = []
    for layer_index in range(NL):
        attend_full, merge_full, up_full, down_full, bias_full = weights[layer_index]
        normed = layer_norm(hidden, attn_gain[layer_index], attn_offset[layer_index]).astype(
            jnp.bfloat16
        )
        qkv_low = product_back(normed, attend_full).astype(jnp.bfloat16)
        blocks = head_blocks(qkv_low, tensor_count)
        mixed_low, log_total = attend(blocks, allowed)
        hidden_mid = hidden + product(mixed_low, merge_full)
        normed_mlp = layer_norm(hidden_mid, mlp_gain[layer_index], mlp_offset[layer_index]).astype(
            jnp.bfloat16
        )
        pre_active = product_back(normed_mlp, up_full) + bias_full
        active = gelu_exact(pre_active).astype(jnp.bfloat16)
        stored.append(
            (hidden, normed, blocks, log_total, mixed_low, hidden_mid, normed_mlp, pre_active, active)
        )
        hidden = hidden_mid + (product(active, down_full) + down_bias[layer_index])
    final = layer_norm(hidden, final_gain, final_offset)
    final_low = final.astype(jnp.bfloat16)
    head_out = product(final_low, head_weight) + head_bias
    position = lax.broadcasted_iota(jnp.int32, (shard_count, 1), 0) % P_SIZE
    starts = position == 0
    previous = jnp.concatenate([jnp.zeros((1, 2 * PV), jnp.float32), head_out[:-1]], axis=0)
    previous = jnp.where(starts, 0.0, previous)
    shift_part = previous[:, :PV]
    log_scale = previous[:, PV:]
    scale_factor = jnp.exp(-log_scale)
    latents = (
        live_mask * (patch_values - shift_part) * scale_factor + (1.0 - live_mask) * patch_values
    )
    log_det = -jnp.sum((live_mask * log_scale).reshape(local_images, P_SIZE * PV), axis=1)
    image_cot = jnp.repeat(logdet_cot, P_SIZE)[:, None]
    direct_grad = latent_cot * (live_mask * scale_factor + (1.0 - live_mask))
    grad_shift = -live_mask * latent_cot * scale_factor
    grad_scale = -live_mask * (latent_cot * (patch_values - shift_part) * scale_factor + image_cot)
    grad_previous = jnp.where(starts, 0.0, jnp.concatenate([grad_shift, grad_scale], axis=1))
    grad_head = jnp.concatenate([grad_previous[1:], jnp.zeros((1, 2 * PV), jnp.float32)], axis=0)
    grad_head_low = grad_head.astype(jnp.bfloat16)
    head_weight_grad = contract_rows(grad_head_low, final_low)
    head_bias_grad = jnp.sum(grad_head_low.astype(jnp.float32), axis=0)
    grad_final = product_back(grad_head_low, head_weight)
    grad_hidden, final_gain_grad, final_offset_grad = norm_backward(
        hidden, final_gain, final_offset, grad_final
    )
    rows_of = {}
    split_list = [None] * NL
    for layer_index in reversed(range(NL)):
        hidden_in, normed, blocks, log_total, mixed_low, hidden_mid, normed_mlp, pre_active, active = (
            stored[layer_index]
        )
        attend_full, merge_full, up_full, down_full, bias_full = weights[layer_index]
        grad_out_mlp = grad_hidden.astype(jnp.bfloat16)
        down_bias_grad = jnp.sum(grad_out_mlp.astype(jnp.float32), axis=0)
        down_grad = contract_rows(active, grad_out_mlp)
        grad_active = product_back(grad_out_mlp, down_full)
        outputs, gelu_pull = jax.vjp(gelu_exact, pre_active)
        grad_inner = gelu_pull(grad_active)[0].astype(jnp.bfloat16)
        up_bias_grad = jnp.sum(grad_inner.astype(jnp.float32), axis=0)
        up_grad = contract_rows(grad_inner, normed_mlp)
        grad_normed = product(grad_inner, up_full)
        grad_from, mlp_gain_grad, mlp_offset_grad = norm_backward(
            hidden_mid, mlp_gain[layer_index], mlp_offset[layer_index], grad_normed
        )
        grad_hidden = grad_hidden + grad_from
        grad_out_attn = grad_hidden.astype(jnp.bfloat16)
        merge_grad = contract_rows(mixed_low, grad_out_attn)
        grad_mixed = product_back(grad_out_attn, merge_full).astype(jnp.bfloat16)
        grad_qkv = attend_back(blocks, allowed, log_total, grad_mixed, tensor_count)
        attend_grad = contract_rows(grad_qkv, normed)
        grad_normed = product(grad_qkv, attend_full)
        grad_from, attn_gain_grad, attn_offset_grad = norm_backward(
            hidden_in, attn_gain[layer_index], attn_offset[layer_index], grad_normed
        )
        grad_hidden = grad_hidden + grad_from
        rows_of[layer_index] = [
            attn_gain_grad[None],
            attn_offset_grad[None],
            mlp_gain_grad[None],
            mlp_offset_grad[None],
            down_bias_grad[None],
            up_bias_grad.reshape(-1, D),
        ]
        split_list[layer_index] = [
            grad.astype(jnp.bfloat16) for grad in (attend_grad, merge_grad, up_grad, down_grad)
        ]
    per_image = grad_hidden.reshape(local_images, P_SIZE, D)
    image_count = device_count * local_images
    image_index = device_index * local_images
    image_rows = lax.dynamic_update_slice_in_dim(
        jnp.zeros((image_count, D), jnp.float32), jnp.sum(per_image, axis=1), image_index, 0
    )
    id_rows = jnp.stack([class_ids // 32, class_ids % 32]).astype(jnp.float32)
    id_rows = lax.dynamic_update_slice(jnp.zeros((2, D), jnp.float32), id_rows, (0, image_index))
    small = [
        jnp.sum(per_image, axis=0),
        precise_rows(patch_values, grad_hidden),
        head_weight_grad,
        image_rows,
        jnp.sum(grad_hidden, axis=0)[None],
        final_gain_grad[None],
        final_offset_grad[None],
        jnp.pad(head_bias_grad, (0, D - 2 * PV))[None],
    ]
    for entry in rows_of[0] + rows_of[1]:
        small.append(entry)
    small.append(id_rows)
    lengths = [entry.shape[0] for entry in small]
    joined = jnp.concatenate(small, axis=0)
    joined = jnp.pad(joined, ((0, -joined.shape[0] % (8 * device_count)), (0, 0)))
    sums, small_sum = reduce_weights(split_list[0] + split_list[1], joined)
    for layer_index in range(NL):
        attend_sum, merge_sum, up_sum, down_sum = sums[4 * layer_index : 4 * layer_index + 4]
        split_list[layer_index] = (
            jnp.swapaxes(attend_sum.reshape(3, -1, D), 1, 2).astype(jnp.float32),
            merge_sum.astype(jnp.float32),
            jnp.swapaxes(up_sum, 0, 1).astype(jnp.float32),
            down_sum.astype(jnp.float32),
        )
    patches_grad = direct_grad + lax.dot_general(
        grad_hidden,
        embed_full,
        (((1,), (1,)), ((), ())),
        precision=HIGHEST,
        preferred_element_type=jnp.float32,
    )
    small_sum = small_sum.astype(jnp.float32)
    small_list = []
    begin = 0
    for length in lengths:
        small_list.append(small_sum[begin : begin + length])
        begin += length
    id_sums = small_list[20][:, :image_count].astype(jnp.int32)
    all_ids = id_sums[0] * 32 + id_sums[1]
    choose_all = all_ids[:, None] == lax.broadcasted_iota(
        jnp.int32, (image_count, CLASSES), 1
    )
    class_grad = precise_rows(choose_all.astype(jnp.float32), small_list[3])
    layer_rows = [small_list[8:14], small_list[14:20]]
    own_bias = [
        lax.dynamic_slice_in_dim(
            entry[5].reshape(tensor_count, -1), tensor_index, 1, 0
        )
        for entry in layer_rows
    ]
    split_stack = [jnp.stack([entry[member] for entry in split_list]) for member in range(4)]
    shared_stack = [
        jnp.concatenate([entry[member] for entry in layer_rows], axis=0) for member in range(5)
    ]
    return (
        latents,
        log_det,
        patches_grad,
        small_list[1],
        small_list[4][0],
        small_list[0],
        class_grad,
        shared_stack[0],
        shared_stack[1],
        split_stack[0],
        split_stack[1],
        shared_stack[2],
        shared_stack[3],
        split_stack[2],
        jnp.concatenate(own_bias, axis=0),
        split_stack[3],
        shared_stack[4],
        small_list[5][0],
        small_list[6][0],
        jnp.swapaxes(small_list[2], 0, 1),
        small_list[7][0, : 2 * PV],
    )


def solution(mesh):
    return jax.shard_map(
        shards,
        mesh=mesh,
        in_specs=(
            P(("batch", "tensor"), None),
            P("batch"),
            P(("batch", "tensor")),
            P(),
            P(),
            P(),
            P(),
            P(),
            P(),
            P(None, None, None, "tensor"),
            P(None, "tensor", None),
            P(),
            P(),
            P(None, None, "tensor"),
            P(None, "tensor"),
            P(None, "tensor", None),
            P(),
            P(),
            P(),
            P(),
            P(),
            P(("batch", "tensor"), None),
            P(("batch", "tensor")),
        ),
        out_specs=(
            P(("batch", "tensor"), None),
            P(("batch", "tensor")),
            P(("batch", "tensor"), None),
            P(),
            P(),
            P(),
            P(),
            P(),
            P(),
            P(None, None, None, "tensor"),
            P(None, "tensor", None),
            P(),
            P(),
            P(None, None, "tensor"),
            P(None, "tensor"),
            P(None, "tensor", None),
            P(),
            P(),
            P(),
            P(),
            P(),
        ),
        check_vma=False,
    )
```

```python
import functools

import jax
import jax.numpy as jnp
from jax import lax
from jax.experimental import pallas as pl
from jax.experimental.pallas import tpu as pltpu
from jax.sharding import PartitionSpec as P

D = 768
HEAD_DIM = 64
P_SIZE = 256
PV = 48
CLASSES = 1000
NL = 2


EPSILON = 1e-05
NEGATIVE = -1000000000.0
HIGHEST = lax.Precision.HIGHEST


def layer_norm(values, norm_gain, norm_offset):
    center = values - jnp.mean(values, axis=-1, keepdims=True)
    spread = jnp.mean(center * center, axis=-1, keepdims=True)
    return center * lax.rsqrt(spread + EPSILON) * norm_gain + norm_offset


def norm_backward(values, norm_gain, norm_offset, upstream):
    outputs, pullback = jax.vjp(layer_norm, values, norm_gain, norm_offset)
    return pullback(upstream)


def gelu_parts(values):
    share = 0.5 + 0.5 * lax.erf(values * (0.5**0.5))
    slope = share + values * (jnp.exp(-0.5 * values * values) * ((0.5 / jnp.pi) ** 0.5))
    return (values * share, slope)


def product(former, latter):
    return jnp.dot(former, latter, preferred_element_type=jnp.float32)


def contract_rows(former, latter):
    return lax.dot_general(
        former, latter, (((0,), (0,)), ((), ())), preferred_element_type=jnp.float32
    )


def precise_rows(former, latter):
    return lax.dot_general(
        former,
        latter,
        (((0,), (0,)), ((), ())),
        precision=HIGHEST,
        preferred_element_type=jnp.float32,
    )


def build_allowed(mask_rows, span):
    row_index = lax.broadcasted_iota(jnp.int32, (span, span), 0)
    col_index = lax.broadcasted_iota(jnp.int32, (span, span), 1)
    causal = (row_index // P_SIZE == col_index // P_SIZE) & (col_index <= row_index)
    key_valid = mask_rows.reshape(mask_rows.shape[0] // span, 1, span) > 0
    return causal[None] & (key_valid | (row_index == col_index)[None])


def gather_rows(parts):
    batch_count = lax.axis_size("batch")
    batch_index = lax.axis_index("batch")
    pieces = []
    for part in parts:
        rows = part.shape[0] // batch_count
        pieces.append(lax.dynamic_slice_in_dim(part, batch_index * rows, rows, 0))
    piece = jnp.concatenate(pieces, axis=0)
    group = lax.all_gather(piece, "tensor", axis=0)
    whole = lax.all_gather(group, "batch", axis=0)
    results = []
    begin = 0
    for entry in pieces:
        results.append(whole[:, :, begin : begin + entry.shape[0]])
        begin += entry.shape[0]
    return results


def reduce_rows(parts):
    joined = jnp.concatenate([part.astype(jnp.bfloat16) for part in parts], axis=2)
    over_batch = lax.psum_scatter(joined, "batch", scatter_dimension=0)
    own = lax.psum_scatter(over_batch, "tensor", scatter_dimension=0)
    whole = lax.all_gather(own, "batch", axis=0)
    results = []
    begin = 0
    for part in parts:
        results.append(whole[:, begin : begin + part.shape[2]])
        begin += part.shape[2]
    return results


def to_tensor_major(blocks):
    return jnp.swapaxes(blocks, 0, 1).reshape(-1, blocks.shape[-1])


def to_batch_major(rows):
    batch_count = lax.axis_size("batch")
    tensor_count = lax.axis_size("tensor")
    return jnp.swapaxes(rows.reshape(tensor_count, batch_count, -1, rows.shape[-1]), 0, 1)


def split_blocks(rows):
    batch_count = lax.axis_size("batch")
    tensor_count = lax.axis_size("tensor")
    return rows.reshape(batch_count, tensor_count, -1, rows.shape[-1])


MESH = pl.DeviceIdType.MESH
SWAP_TENSOR = (1, 2, 3)


def place():
    batch_index = lax.axis_index("batch")
    tensor_index = lax.axis_index("tensor")
    return (batch_index // 4, batch_index // 2 % 2, batch_index % 2, tensor_index)


def device_at(y, x, core, z):
    return (y * 4 + x * 2 + core, z)


def flipped(index, bits):
    high, low = index // 2, index % 2
    if bits & 2:
        high = 1 - high
    if bits & 1:
        low = 1 - low
    return high * 2 + low


def greet(devices):
    barrier = pltpu.get_barrier_semaphore()
    for device in devices:
        pl.semaphore_signal(barrier, inc=1, device_id=device, device_id_type=MESH)
    pl.semaphore_wait(barrier, len(devices))


def partners():
    y, x, core, z = place()
    devices = [device_at(y, x, core, flipped(z, bits)) for bits in SWAP_TENSOR]
    devices.append(device_at(y, 1 - x, core, z))
    devices.append(device_at(1 - y, x, core, z))
    devices.append(device_at(y, x, 1 - core, z))
    return devices


def halves(count):
    return (slice(0, (count + 1) // 2), slice((count + 1) // 2, count))


class Copies:
    def __init__(self, send_sems):
        self.send_sems = send_sems
        self.count = 0
        self.sent = []

    def send(self, source, target, recv_sem, device, keep=True):
        copy = pltpu.make_async_remote_copy(
            src_ref=source,
            dst_ref=target,
            send_sem=self.send_sems.at[self.count],
            recv_sem=recv_sem,
            device_id=device,
            device_id_type=MESH,
        )
        self.count += 1
        copy.start()
        if keep:
            self.sent.append(copy)
        return copy

    def finish(self):
        for copy in self.sent:
            copy.wait_send()


def wait_arrival(target, recv_sem, send_sem, device):
    pltpu.make_async_remote_copy(
        src_ref=target,
        dst_ref=target,
        send_sem=send_sem,
        recv_sem=recv_sem,
        device_id=device,
        device_id_type=MESH,
    ).wait_recv()


def spread_piece(ref, lead, b):
    if len(ref.shape) == len(lead) + 4:
        return ref.at[(*lead, slice(None), b)]
    return ref.at[(*lead, b)]


def half_piece(ref, lead, b, side):
    if len(ref.shape) == len(lead) + 4:
        return ref.at[(*lead, halves(ref.shape[len(lead)])[side], b)]
    return ref.at[(*lead, b, halves(ref.shape[len(lead) + 1])[side])]


def gather_kernel(layer_count, *refs):
    per_layer = 4
    units = layer_count * per_layer
    shards = refs[:units]
    bias = refs[units]
    fulls = refs[units + 1 : 2 * units + 1]
    bias_full = refs[2 * units + 1]
    send_sems, z_sems, xy_sems, core_sems, local_sems, bias_sems, spare = refs[2 * units + 2 :]
    y, x, core, z = place()
    b = y * 4 + x * 2 + core
    over_x = y * 4 + (1 - x) * 2 + core
    over_y = (1 - y) * 4 + x * 2 + core
    corner = (1 - y) * 4 + (1 - x) * 2 + core
    at_x = device_at(y, 1 - x, core, z)
    at_y = device_at(1 - y, x, core, z)
    at_core = device_at(y, x, 1 - core, z)
    middle = (z + 1) // 2 % 2
    near = flipped(z, 1)
    across = 3 - z
    far = (z + 2) % 4
    at_near = device_at(y, x, core, near)
    at_across = device_at(y, x, core, across)
    order = (
        near,
        middle * across + (1 - middle) * far,
        middle * far + (1 - middle) * across,
    )
    greet(partners())
    copies = Copies(send_sems)
    conditional = []
    locals_ = []
    for unit in range(units):
        copy = pltpu.make_async_copy(shards[unit], fulls[unit].at[z], local_sems.at[unit])
        copy.start()
        locals_.append(copy)
    copy = pltpu.make_async_copy(bias, bias_full.at[z], local_sems.at[units])
    copy.start()
    locals_.append(copy)
    for entry, bits in enumerate(SWAP_TENSOR):
        copies.send(
            bias,
            bias_full.at[z],
            bias_sems.at[entry],
            device_at(y, x, core, flipped(z, bits)),
        )

    def of_layer(layer):
        return range(layer * per_layer, (layer + 1) * per_layer)

    def send_if_middle(source, target, recv_sem, device):
        slot = send_sems.at[copies.count]
        copies.count += 1
        copy = pltpu.make_async_remote_copy(
            src_ref=source,
            dst_ref=target,
            send_sem=slot,
            recv_sem=recv_sem,
            device_id=device,
            device_id_type=MESH,
        )

        @pl.when(middle == 1)
        def _():
            copy.start()

        conditional.append(copy)

    def begin(layer):
        for unit in of_layer(layer):
            mine = spread_piece(shards[unit], (), b)
            target = spread_piece(fulls[unit], (z,), b)
            copies.send(mine, target, z_sems.at[unit, z], at_near)
            send_if_middle(mine, target, z_sems.at[unit, z], at_across)

    def take_z(layer, step):
        t = order[step]
        for unit in of_layer(layer):
            piece = spread_piece(fulls[unit], (t,), b)
            wait_arrival(piece, z_sems.at[unit, t], spare.at[0], at_near)
            send_if_middle(
                piece, piece, z_sems.at[unit, t], at_across if step == 0 else at_near
            )
        for unit in of_layer(layer):
            piece = spread_piece(fulls[unit], (t,), b)
            copies.send(piece, piece, xy_sems.at[unit, step, 0], at_x)
            copies.send(piece, piece, xy_sems.at[unit, step, 1], at_y)
            copies.send(piece, piece, core_sems.at[unit, step, 0], at_core)

    def take_xy(layer, step):
        t = order[step]
        for unit in of_layer(layer):
            piece = spread_piece(fulls[unit], (t,), over_x)
            wait_arrival(piece, xy_sems.at[unit, step, 0], spare.at[0], at_x)
            first = half_piece(fulls[unit], (t,), over_x, 0)
            copies.send(first, first, xy_sems.at[unit, step, 2], at_y)
            copies.send(piece, piece, core_sems.at[unit, step, 1], at_core)
        for unit in of_layer(layer):
            piece = spread_piece(fulls[unit], (t,), over_y)
            wait_arrival(piece, xy_sems.at[unit, step, 1], spare.at[0], at_y)
            second = half_piece(fulls[unit], (t,), over_y, 1)
            copies.send(second, second, xy_sems.at[unit, step, 3], at_x)
            copies.send(piece, piece, core_sems.at[unit, step, 2], at_core)

    def take_corner(layer, step):
        t = order[step]
        for unit in of_layer(layer):
            first = half_piece(fulls[unit], (t,), corner, 0)
            second = half_piece(fulls[unit], (t,), corner, 1)
            wait_arrival(first, xy_sems.at[unit, step, 2], spare.at[0], at_y)
            wait_arrival(second, xy_sems.at[unit, step, 3], spare.at[0], at_x)
            piece = spread_piece(fulls[unit], (t,), corner)
            copies.send(piece, piece, core_sems.at[unit, step, 3], at_core)

    def take_core(layer, step):
        t = order[step]
        for unit in of_layer(layer):
            for entry, owner in enumerate((b, over_x, over_y, corner)):
                other = owner + 1 - 2 * core
                piece = spread_piece(fulls[unit], (t,), other)
                wait_arrival(piece, core_sems.at[unit, step, entry], spare.at[0], at_core)

    begin(0)
    for layer in range(layer_count):
        take_z(layer, 0)
        take_z(layer, 1)
        if layer:
            take_corner(layer - 1, 1)
        take_xy(layer, 0)
        take_z(layer, 2)
        if layer + 1 < layer_count:
            begin(layer + 1)
        if layer:
            take_corner(layer - 1, 2)
        take_xy(layer, 1)
        take_corner(layer, 0)
        take_xy(layer, 2)
    take_corner(layer_count - 1, 1)
    take_corner(layer_count - 1, 2)
    for layer in range(layer_count):
        for step in range(3):
            take_core(layer, step)
    for entry, bits in enumerate(SWAP_TENSOR):
        wait_arrival(
            bias_full.at[flipped(z, bits)],
            bias_sems.at[entry],
            spare.at[0],
            device_at(y, x, core, flipped(z, bits)),
        )
    for copy in locals_:
        copy.wait()
    copies.finish()

    @pl.when(middle == 1)
    def _():
        for copy in conditional:
            copy.wait_send()


def gather_all(shards, bias):
    units = len(shards)
    outs = [jax.ShapeDtypeStruct((4, *shard.shape), shard.dtype) for shard in shards]
    outs.append(jax.ShapeDtypeStruct((4, *bias.shape), bias.dtype))
    vmem = pl.BlockSpec(memory_space=pltpu.VMEM)
    anywhere = pl.BlockSpec(memory_space=pl.ANY)
    dma = pltpu.SemaphoreType.DMA
    return pl.pallas_call(
        functools.partial(gather_kernel, units // 4),
        out_shape=outs,
        in_specs=[vmem] * (units + 1),
        out_specs=[anywhere] * (units + 1),
        scratch_shapes=[
            dma((3 + units * (2 + 3 * 9),)),
            dma((units, 4)),
            dma((units, 3, 4)),
            dma((units, 3, 4)),
            dma((units + 1,)),
            dma((3,)),
            dma((1,)),
        ],
        compiler_params=pltpu.CompilerParams(collective_id=0, has_side_effects=True),
        name="gather_weights",
    )(*shards, bias)


def add_slab(target, addend):
    target[...] = (target[...].astype(jnp.float32) + addend[...].astype(jnp.float32)).astype(
        target.dtype
    )


ITEM_ORDER = (0, 2, 1, 3)
AHEAD = 3


def reduce_kernel(groups, spread_all, *refs):
    units = sum(len(group) for group in groups)
    grads = refs[:units]
    outs = refs[units : 2 * units]
    own, got_core, got_one, got_two, got_z, result = (
        refs[(2 + entry) * units : (3 + entry) * units] for entry in range(6)
    )
    send_sems, load_sems, step_sems, z_sems, spread_sems, core_sems, all_sems, spare = refs[
        8 * units :
    ]
    y, x, core, z = place()
    at_x = device_at(y, 1 - x, core, z)
    at_y = device_at(1 - y, x, core, z)
    at_core = device_at(y, x, 1 - core, z)
    greet(partners())
    copies = Copies(send_sems)
    conditional = []
    items = [(group, t) for group in groups for t in ITEM_ORDER]

    def load(group, t):
        for unit in group:
            grad = grads[unit]
            copies.send(
                grad.at[t, :, :, :, 1 - core],
                got_core[unit].at[t],
                step_sems.at[unit, 0, t],
                at_core,
            )
            pltpu.make_async_copy(
                grad.at[t, :, :, :, core], own[unit].at[t], load_sems.at[unit, t]
            ).start()

    def take_core_sum(group, t):
        for unit in group:
            grad = grads[unit]
            mine, other = own[unit], got_core[unit]
            pltpu.make_async_copy(
                grad.at[t, :, :, :, core], mine.at[t], load_sems.at[unit, t]
            ).wait()
            wait_arrival(other.at[t], step_sems.at[unit, 0, t], spare.at[0], at_core)
            count = mine.shape[1] * 4

            def body(entry, carry):
                spot = (t, entry // 4, entry // 2 % 2, entry % 2)
                add_slab(mine.at[spot], other.at[spot])
                return carry

            lax.fori_loop(0, count, body, 0)
            if t < 2:
                copies.send(
                    mine.at[t, :, :, 1 - x], got_one[unit].at[t], step_sems.at[unit, 1, t], at_x
                )
            else:
                copies.send(
                    mine.at[t, :, 1 - y], got_one[unit].at[t], step_sems.at[unit, 1, t], at_y
                )

    def take_one(group, t):
        for unit in group:
            mine, other = own[unit], got_one[unit]
            wait_arrival(
                other.at[t], step_sems.at[unit, 1, t], spare.at[0], at_x if t < 2 else at_y
            )
            count = mine.shape[1] * 2

            def body(entry, carry):
                first, second = entry // 2, entry % 2
                if t < 2:
                    add_slab(mine.at[t, first, second, x], other.at[t, first, second])
                else:
                    add_slab(mine.at[t, first, y, second], other.at[t, first, second])
                return carry

            lax.fori_loop(0, count, body, 0)
            if t < 2:
                copies.send(
                    mine.at[t, :, 1 - y, x], got_two[unit].at[t], step_sems.at[unit, 2, t], at_y
                )
            else:
                copies.send(
                    mine.at[t, :, y, 1 - x], got_two[unit].at[t], step_sems.at[unit, 2, t], at_x
                )

    def take_two(group, t):
        for unit in group:
            mine, other = own[unit], got_two[unit]
            wait_arrival(
                other.at[t], step_sems.at[unit, 2, t], spare.at[0], at_y if t < 2 else at_x
            )

            def body(entry, carry):
                add_slab(mine.at[t, entry, y, x], other.at[t, entry])
                return carry

            lax.fori_loop(0, mine.shape[1], body, 0)
            copy = pltpu.make_async_remote_copy(
                src_ref=mine.at[t, :, y, x],
                dst_ref=got_z[unit].at[z],
                send_sem=send_sems.at[copies.count],
                recv_sem=z_sems.at[unit, z],
                device_id=device_at(y, x, core, t),
                device_id_type=MESH,
            )
            copies.count += 1

            @pl.when(z != t)
            def _():
                copy.start()

            conditional.append((t, copy))

    def slot_of(unit):
        return z if unit in spread_all else 0

    def spot_of(unit, where):
        return outs[unit].at[(slot_of(unit), slice(None), *where)]

    def half_spot(unit, where, side):
        count = outs[unit].shape[1]
        if count > 1:
            return outs[unit].at[(slot_of(unit), halves(count)[side], *where)]
        rows = halves(outs[unit].shape[5])[side]
        return outs[unit].at[(slot_of(unit), slice(None), *where, rows)]

    def take_z(group):
        for unit in group:
            mine, other, total = own[unit], got_z[unit], result[unit]
            for bits in SWAP_TENSOR:
                t = flipped(z, bits)
                wait_arrival(
                    other.at[t], z_sems.at[unit, t], spare.at[0], device_at(y, x, core, t)
                )

            def body(entry, carry):
                value = mine[z, entry, y, x].astype(jnp.float32)
                for bits in SWAP_TENSOR:
                    value = value + other[flipped(z, bits), entry].astype(jnp.float32)
                total[entry] = value.astype(total.dtype)
                return carry

            lax.fori_loop(0, mine.shape[1], body, 0)
            spot = spot_of(unit, (y, x, core))
            pltpu.make_async_copy(total, spot, load_sems.at[unit, 4]).start()
            copies.send(total, spot, spread_sems.at[unit, 0], at_x)
            copies.send(total, spot, spread_sems.at[unit, 1], at_y)
            copies.send(total, spot, core_sems.at[unit, 0], at_core)

    def take_spread(group):
        for unit in group:
            spot = spot_of(unit, (y, 1 - x, core))
            wait_arrival(spot, spread_sems.at[unit, 0], spare.at[0], at_x)
            first = half_spot(unit, (y, 1 - x, core), 0)
            copies.send(first, first, spread_sems.at[unit, 2], at_y)
            copies.send(spot, spot, core_sems.at[unit, 1], at_core)
            spot = spot_of(unit, (1 - y, x, core))
            wait_arrival(spot, spread_sems.at[unit, 1], spare.at[0], at_y)
            second = half_spot(unit, (1 - y, x, core), 1)
            copies.send(second, second, spread_sems.at[unit, 3], at_x)
            copies.send(spot, spot, core_sems.at[unit, 2], at_core)

    def take_corner(group):
        for unit in group:
            where = (1 - y, 1 - x, core)
            wait_arrival(half_spot(unit, where, 0), spread_sems.at[unit, 2], spare.at[0], at_y)
            wait_arrival(half_spot(unit, where, 1), spread_sems.at[unit, 3], spare.at[0], at_x)
            spot = spot_of(unit, where)
            copies.send(spot, spot, core_sems.at[unit, 3], at_core)

    def take_last(group):
        for unit in group:
            pltpu.make_async_copy(
                result[unit], spot_of(unit, (y, x, core)), load_sems.at[unit, 4]
            ).wait()
            for entry, where in enumerate(((y, x), (y, 1 - x), (1 - y, x), (1 - y, 1 - x))):
                spot = spot_of(unit, (*where, 1 - core))
                wait_arrival(spot, core_sems.at[unit, entry], spare.at[0], at_core)

    def run(step):
        if step < len(items):
            take_core_sum(*items[step])
        if 0 <= step - 1 < len(items):
            take_one(*items[step - 1])
        if 0 <= step - 2 < len(items):
            take_two(*items[step - 2])
        for index, group in enumerate(groups):
            last = 4 * index + 3
            if step == last + 4:
                take_z(group)
            if step == last + 5:
                take_spread(group)
            if step == last + 6:
                take_corner(group)

    for item in items[:AHEAD]:
        load(*item)
    for step in range(len(items) + 6):
        if step + AHEAD < len(items):
            load(*items[step + AHEAD])
        run(step)
    for group in groups:
        take_last(group)
    for entry, unit in enumerate(spread_all):
        for bits in SWAP_TENSOR:
            copies.send(
                outs[unit].at[z],
                outs[unit].at[z],
                all_sems.at[entry, bits],
                device_at(y, x, core, flipped(z, bits)),
            )
        for bits in SWAP_TENSOR:
            t = flipped(z, bits)
            wait_arrival(
                outs[unit].at[t], all_sems.at[entry, bits], spare.at[0], device_at(y, x, core, t)
            )
    copies.finish()
    for t, copy in conditional:

        @pl.when(z != t)
        def _(copy=copy):
            copy.wait_send()


def reduce_all(grads, groups, spread_all):
    units = len(grads)
    scratch = []
    for lead in ((4, 2, 2), (4, 2, 2), (4, 2), (4,), (4,), ()):
        for grad in grads:
            count, rows = grad.shape[1], grad.shape[5]
            shape = lead[:1] + (count,) + lead[1:] + (rows, D)
            scratch.append(pltpu.VMEM(shape, jnp.bfloat16))
    dma = pltpu.SemaphoreType.DMA
    anywhere = pl.BlockSpec(memory_space=pl.ANY)
    return pl.pallas_call(
        functools.partial(reduce_kernel, groups, spread_all),
        out_shape=[
            jax.ShapeDtypeStruct((4 if unit in spread_all else 1, *grad.shape[1:]), grad.dtype)
            for unit, grad in enumerate(grads)
        ],
        in_specs=[anywhere] * units,
        out_specs=[anywhere] * units,
        scratch_shapes=scratch
        + [
            dma((units * 24 + 3 * len(spread_all),)),
            dma((units, 5)),
            dma((units, 3, 4)),
            dma((units, 4)),
            dma((units, 4)),
            dma((units, 4)),
            dma((max(len(spread_all), 1), 4)),
            dma((1,)),
        ],
        compiler_params=pltpu.CompilerParams(
            collective_id=1, has_side_effects=True, vmem_limit_bytes=62 * 1024 * 1024
        ),
        name="reduce_gradients",
    )(*grads)


def fast_mesh():
    return lax.axis_size("batch") == 8 and lax.axis_size("tensor") == 4


def gather_weights(shards, bias):
    if not fast_mesh():
        wholes = [to_tensor_major(blocks) for blocks in gather_rows(shards)]
        return (wholes, lax.all_gather(bias, "tensor", axis=0))
    parts = []
    for shard in shards:
        rows = shard.shape[0]
        parts.append(shard.reshape(8, -1, D) if rows == D else shard.reshape(-1, 8, 8, D))
    results = gather_all(parts, jnp.pad(bias, ((0, 8 - NL), (0, 0))))
    return ([whole.reshape(-1, D) for whole in results[:-1]], results[-1][:, :NL])


def reduce_weights(split_list, small):
    if not fast_mesh():
        grads = [grad.reshape(-1, D) for grad in split_list[0] + split_list[1]]
        sums = reduce_rows([to_batch_major(grad) for grad in grads] + [split_blocks(small)])
        small_sum = lax.all_gather(sums[-1], "tensor", axis=1).reshape(-1, D)
        return ([entry.reshape(-1, D) for entry in sums[:-1]], small_sum)
    part = small.astype(jnp.bfloat16).reshape(4, 1, 2, 2, 2, -1, D)
    (small_sum,) = reduce_all([part], ((0,),), (0,))
    return (split_list[0] + split_list[1], small_sum.reshape(-1, D))


def back_dot(former, latter):
    return lax.dot_general(
        former, latter, (((1,), (1,)), ((), ())), preferred_element_type=jnp.float32
    )


def row_blocks(count, size, body, carry=0):
    def step(index, carry):
        return body(pl.ds(pl.multiple_of(index * size, size), size), carry)

    return lax.fori_loop(0, count // size, step, carry)


def norm_into(source, gain, offset, target):
    def body(rows, carry):
        target[rows] = layer_norm(source[rows], gain, offset).astype(target.dtype)
        return carry

    row_blocks(source.shape[0], 128, body)


def norm_back_into(grad, source, upstream, gain):
    def body(rows, carry):
        gain_sum, offset_sum = carry
        values, above = source[rows], upstream[rows]
        center = values - jnp.mean(values, axis=-1, keepdims=True)
        spread = jnp.mean(center * center, axis=-1, keepdims=True)
        scale = lax.rsqrt(spread + EPSILON)
        normal = center * scale
        part = above * gain
        gain_sum = gain_sum + jnp.sum(above * normal, axis=0, keepdims=True)
        offset_sum = offset_sum + jnp.sum(above, axis=0, keepdims=True)
        inner = jnp.mean(part, axis=-1, keepdims=True)
        along = jnp.mean(part * normal, axis=-1, keepdims=True)
        grad[rows] = grad[rows] + scale * (part - inner - normal * along)
        return (gain_sum, offset_sum)

    zero = jnp.zeros((1, D), jnp.float32)
    return row_blocks(source.shape[0], 128, body, (zero, zero))


def head_probs(qkv, allowed, t, rows, image, head):
    span = qkv.shape[2] // 3
    queries, keys, values = (
        qkv[t, rows, c * span + head * HEAD_DIM : c * span + (head + 1) * HEAD_DIM]
        for c in range(3)
    )
    scores = back_dot(queries, keys) * (HEAD_DIM ** (-0.5))
    scores = jnp.where(allowed[image] > 0, scores, NEGATIVE)
    top = jnp.max(scores, axis=-1, keepdims=True)
    powers = jnp.exp(scores - top)
    total = jnp.sum(powers, axis=-1, keepdims=True)
    return (queries, keys, values, powers * (1.0 / total))


def each_image(qkv, body, begin=0, end=4):
    images = qkv.shape[1] // P_SIZE

    def step(index, carry):
        t, image = index // images, index % images
        body(t, image, pl.ds(pl.multiple_of(image * P_SIZE, P_SIZE), P_SIZE))
        return carry

    lax.fori_loop(begin * images, end * images, step, 0)


def attend_into(qkv, allowed, mixed):
    def body(t, image, rows):
        blocks = []
        for head in range(qkv.shape[2] // (3 * HEAD_DIM)):
            queries, keys, values, probs = head_probs(qkv, allowed, t, rows, image, head)
            blocks.append(product(probs.astype(jnp.bfloat16), values))
        mixed[t, rows] = jnp.concatenate(blocks, axis=1).astype(mixed.dtype)

    each_image(qkv, body)


def attend_back_into(qkv, allowed, grad_mixed, grad_qkv, begin=0, end=4):
    def body(t, image, rows):
        parts = ([], [], [])
        for head in range(qkv.shape[2] // (3 * HEAD_DIM)):
            queries, keys, values, probs = head_probs(qkv, allowed, t, rows, image, head)
            above = grad_mixed[t, rows, head * HEAD_DIM : (head + 1) * HEAD_DIM]
            grad_values = contract_rows(probs.astype(jnp.bfloat16), above)
            grad_probs = back_dot(above, values)
            inner = jnp.sum(probs * grad_probs, axis=-1, keepdims=True)
            grad_scores = (probs * (grad_probs - inner)).astype(jnp.bfloat16)
            scaling = HEAD_DIM ** (-0.5)
            parts[0].append(product(grad_scores, keys) * scaling)
            parts[1].append(contract_rows(grad_scores, queries) * scaling)
            parts[2].append(grad_values)
        grad_qkv[t, rows] = jnp.concatenate(parts[0] + parts[1] + parts[2], axis=1).astype(
            grad_qkv.dtype
        )

    each_image(qkv, body, begin, end)


def each_part(body, count=4):
    def step(t, carry):
        body(t)
        return carry

    lax.fori_loop(0, count, step, 0)


def layer_forward_chunks(
    hidden, allowed, gains, weights, bias, normed, qkv, mixed, hidden_mid, normed_mlp, slope, active,
    hidden_next,
):
    attend_w, merge_w, up_w, down_w = weights

    def start():
        norm_into(hidden, gains[0:1], gains[1:2], normed)

        def project(t):
            qkv[t] = back_dot(normed[...], attend_w[t]).astype(qkv.dtype)

        each_part(project)

    def attention():
        attend_into(qkv, allowed, mixed)

    def merge():
        total = hidden[...]
        for t in range(4):
            total = total + product(mixed[t], merge_w[t])
        hidden_mid[...] = total
        norm_into(hidden_mid, gains[2:3], gains[3:4], normed_mlp)

    def up(t):
        inner = product(normed_mlp[...], up_w[t]) + bias[pl.ds(t, 1)]
        value, rise = gelu_parts(inner)
        active[t] = value.astype(active.dtype)
        slope[t] = rise.astype(slope.dtype)

    def down():
        total = hidden_mid[...] + gains[4:5]
        for t in range(4):
            total = total + product(active[t], down_w[t])
        hidden_next[...] = total

    return [start, attention, merge, lambda: each_part(up), down]


def layer_forward_kernel(*refs):
    hidden, allowed, gains, bias = refs[:4]
    weights = refs[4:8]
    for chunk in layer_forward_chunks(hidden, allowed, gains, weights, bias, *refs[8:]):
        chunk()


def layer_shapes(rows, heads):
    low, full = jnp.bfloat16, jnp.float32
    return [
        jax.ShapeDtypeStruct((rows, D), low),
        jax.ShapeDtypeStruct((4, rows, heads * 3 * HEAD_DIM), low),
        jax.ShapeDtypeStruct((4, rows, heads * HEAD_DIM), low),
        jax.ShapeDtypeStruct((rows, D), full),
        jax.ShapeDtypeStruct((rows, D), low),
        jax.ShapeDtypeStruct((4, rows, D), low),
        jax.ShapeDtypeStruct((4, rows, D), low),
        jax.ShapeDtypeStruct((rows, D), full),
    ]


VMEM_LIMIT = 62 * 1024 * 1024


def layer_forward(hidden, allowed, gains, bias, weights):
    rows, heads = hidden.shape[0], weights[0].shape[1] // (3 * HEAD_DIM)
    vmem = pl.BlockSpec(memory_space=pltpu.VMEM)
    outs = layer_shapes(rows, heads)
    return pl.pallas_call(
        layer_forward_kernel,
        out_shape=outs,
        in_specs=[vmem] * 8,
        out_specs=[vmem] * len(outs),
        compiler_params=pltpu.CompilerParams(vmem_limit_bytes=VMEM_LIMIT),
        name="layer_forward",
    )(hidden, allowed, gains, bias, *weights)


def layer_backward_chunks(
    grad, allowed, gains, weights, stored, low, grad_inner, grad_mixed, grad_qkv, upstream, rows_out,
    attend_grad, merge_grad, up_grad, down_grad,
):
    attend_w, merge_w, up_w, down_w = weights
    hidden, normed, qkv, mixed, hidden_mid, normed_mlp, slope, active = stored

    def start():
        low[...] = grad[...].astype(low.dtype)
        rows_out[4:5] = jnp.sum(low[...].astype(jnp.float32), axis=0, keepdims=True)
        upstream[...] = jnp.zeros_like(upstream)

    def mlp(t):
        inner = (back_dot(low[...], down_w[t]) * slope[t]).astype(jnp.bfloat16)
        grad_inner[...] = inner
        rows_out[pl.ds(8 + t, 1)] = jnp.sum(inner.astype(jnp.float32), axis=0, keepdims=True)
        up_grad[t] = contract_rows(normed_mlp[...], grad_inner[...]).astype(jnp.bfloat16)
        down_grad[t] = contract_rows(active[t], low[...]).astype(jnp.bfloat16)
        upstream[...] += back_dot(grad_inner[...], up_w[t])

    def middle():
        sums = norm_back_into(grad, hidden_mid, upstream, gains[2:3])
        rows_out[2:3], rows_out[3:4] = sums
        low[...] = grad[...].astype(low.dtype)

        def part(t):
            merge_grad[t] = contract_rows(mixed[t], low[...]).astype(jnp.bfloat16)
            grad_mixed[t] = back_dot(low[...], merge_w[t]).astype(jnp.bfloat16)

        each_part(part)

    def attention():
        attend_back_into(qkv, allowed, grad_mixed, grad_qkv)

    def finish():
        upstream[...] = jnp.zeros_like(upstream)

        def part(t):
            attend_grad[t] = contract_rows(grad_qkv[t], normed[...]).astype(jnp.bfloat16)
            upstream[...] += product(grad_qkv[t], attend_w[t])

        each_part(part)
        sums = norm_back_into(grad, hidden, upstream, gains[0:1])
        rows_out[0:1], rows_out[1:2] = sums

    return [start, lambda: each_part(mlp), middle, attention, finish]


def layer_backward_kernel(*refs):
    grad_in, allowed, gains = refs[:3]
    weights, stored = refs[3:7], refs[7:15]
    grad, rows_out, attend_grad, merge_grad, up_grad, down_grad = refs[15:21]
    low, grad_inner, grad_mixed, grad_qkv, upstream = refs[21:]
    grad[...] = grad_in[...]
    rows_out[...] = jnp.zeros_like(rows_out)
    for chunk in layer_backward_chunks(
        grad, allowed, gains, weights, stored, low, grad_inner, grad_mixed, grad_qkv, upstream,
        rows_out, attend_grad, merge_grad, up_grad, down_grad,
    ):
        chunk()


def layer_backward(grad, allowed, gains, weights, stored):
    rows, heads = grad.shape[0], weights[0].shape[1] // (3 * HEAD_DIM)
    vmem = pl.BlockSpec(memory_space=pltpu.VMEM)
    low, full = jnp.bfloat16, jnp.float32
    outs = [jax.ShapeDtypeStruct((rows, D), full), jax.ShapeDtypeStruct((16, D), full)]
    outs += [jax.ShapeDtypeStruct(weight.shape, low) for weight in weights]
    return pl.pallas_call(
        layer_backward_kernel,
        out_shape=outs,
        in_specs=[vmem] * 15,
        out_specs=[vmem] * len(outs),
        scratch_shapes=[
            pltpu.VMEM((rows, D), low),
            pltpu.VMEM((rows, D), low),
            pltpu.VMEM((4, rows, heads * HEAD_DIM), low),
            pltpu.VMEM((4, rows, heads * 3 * HEAD_DIM), low),
            pltpu.VMEM((rows, D), full),
        ],
        compiler_params=pltpu.CompilerParams(vmem_limit_bytes=VMEM_LIMIT),
        name="layer_backward",
    )(grad, allowed, gains, *weights, *stored)


MLP_GROUP, ATTEND_GROUP = (2, 3), (0, 1)


def layer_back_kernel(*refs):
    grad_in, hidden, hidden_mid, normed, normed_mlp, slope, active, up_w, down_w = refs[:9]
    qkv, mixed, allowed, gains, attend_w, merge_w = refs[9:15]
    grad, rows_out = refs[15:17]
    outs = refs[17:21]
    grads, got_core, got_one, got_two, got_z, result = (
        refs[21 + 4 * entry : 25 + 4 * entry] for entry in range(6)
    )
    low, grad_inner, grad_mixed, grad_qkv, upstream, values, rounded = refs[45:52]
    slopes, actives, ups, downs = refs[52:56]
    send_sems, step_sems, z_sems, spread_sems, core_sems, spare, load_sems, stream_sems = refs[56:]
    y, x, core, z = place()
    at_x = device_at(y, 1 - x, core, z)
    at_y = device_at(1 - y, x, core, z)
    at_core = device_at(y, x, 1 - core, z)

    def load(source, target, sem):
        copy = pltpu.make_async_copy(source, target, load_sems.at[sem])
        copy.start()
        return copy

    def stream(step):
        t, slot = ITEM_ORDER[step], step % 2
        pairs = ((down_w, downs), (slope, slopes), (active, actives), (up_w, ups))
        copies = []
        for entry, (source, target) in enumerate(pairs):
            copy = pltpu.make_async_copy(
                source.at[t], target.at[slot], stream_sems.at[slot, entry]
            )
            copy.start()
            copies.append(copy)
        return copies

    first_loads = [load(grad_in, grad, 0)]
    streams = [stream(0), stream(1)]
    first_loads += [load(normed_mlp, rounded, 1), load(hidden_mid, values, 2)]
    greet(partners())
    copies = Copies(send_sems)
    conditional = []
    items = [(group, t) for group in (MLP_GROUP, ATTEND_GROUP) for t in ITEM_ORDER]

    def put(unit, t, value):
        target = grads[unit]
        target[t] = value.reshape(target.shape[1:]).astype(target.dtype)

    def share(k):
        group, t = items[k]
        for unit in group:
            copies.send(
                grads[unit].at[t, :, :, :, 1 - core],
                got_core[unit].at[t],
                step_sems.at[unit, 0, t],
                at_core,
            )

    def core_sum(k):
        group, t = items[k]
        for unit in group:
            mine, other = grads[unit], got_core[unit]
            wait_arrival(other.at[t], step_sems.at[unit, 0, t], spare.at[0], at_core)

            def body(entry, carry):
                spot = (t, entry // 4, entry // 2 % 2, entry % 2)
                add_slab(mine.at[(*spot, core)], other.at[spot])
                return carry

            lax.fori_loop(0, mine.shape[1] * 4, body, 0)
            if t < 2:
                source, device = mine.at[t, :, :, 1 - x, core], at_x
            else:
                source, device = mine.at[t, :, 1 - y, :, core], at_y
            copies.send(source, got_one[unit].at[t], step_sems.at[unit, 1, t], device)

    def one(k):
        group, t = items[k]
        for unit in group:
            mine, other = grads[unit], got_one[unit]
            wait_arrival(
                other.at[t], step_sems.at[unit, 1, t], spare.at[0], at_x if t < 2 else at_y
            )

            def body(entry, carry):
                first, second = entry // 2, entry % 2
                spot = (t, first, second, x, core) if t < 2 else (t, first, y, second, core)
                add_slab(mine.at[spot], other.at[t, first, second])
                return carry

            lax.fori_loop(0, mine.shape[1] * 2, body, 0)
            if t < 2:
                source, device = mine.at[t, :, 1 - y, x, core], at_y
            else:
                source, device = mine.at[t, :, y, 1 - x, core], at_x
            copies.send(source, got_two[unit].at[t], step_sems.at[unit, 2, t], device)

    def two(k):
        group, t = items[k]
        for unit in group:
            mine, other = grads[unit], got_two[unit]
            wait_arrival(
                other.at[t], step_sems.at[unit, 2, t], spare.at[0], at_y if t < 2 else at_x
            )

            def body(entry, carry):
                add_slab(mine.at[t, entry, y, x, core], other.at[t, entry])
                return carry

            lax.fori_loop(0, mine.shape[1], body, 0)
            copy = pltpu.make_async_remote_copy(
                src_ref=mine.at[t, :, y, x, core],
                dst_ref=got_z[unit].at[z],
                send_sem=send_sems.at[copies.count],
                recv_sem=z_sems.at[unit, z],
                device_id=device_at(y, x, core, t),
                device_id_type=MESH,
            )
            copies.count += 1

            @pl.when(z != t)
            def _():
                copy.start()

            conditional.append((t, copy))

    def spot_of(unit, where):
        return outs[unit].at[(slice(None), *where)]

    def half_spot(unit, where, side):
        count = outs[unit].shape[0]
        if count > 1:
            return outs[unit].at[(halves(count)[side], *where)]
        return outs[unit].at[(slice(None), *where, halves(outs[unit].shape[4])[side])]

    def over_z(group):
        for unit in group:
            mine, other, total = grads[unit], got_z[unit], result[unit]
            for bits in SWAP_TENSOR:
                t = flipped(z, bits)
                wait_arrival(
                    other.at[t], z_sems.at[unit, t], spare.at[0], device_at(y, x, core, t)
                )

            def body(entry, carry):
                value = mine[z, entry, y, x, core].astype(jnp.float32)
                for bits in SWAP_TENSOR:
                    value = value + other[flipped(z, bits), entry].astype(jnp.float32)
                total[entry] = value.astype(total.dtype)
                return carry

            lax.fori_loop(0, mine.shape[1], body, 0)
            spot = spot_of(unit, (y, x, core))
            pltpu.make_async_copy(total, spot, load_sems.at[3 + unit]).start()
            copies.send(total, spot, spread_sems.at[unit, 0], at_x)
            copies.send(total, spot, spread_sems.at[unit, 1], at_y)
            copies.send(total, spot, core_sems.at[unit, 0], at_core)

    def spread(group):
        for unit in group:
            spot = spot_of(unit, (y, 1 - x, core))
            wait_arrival(spot, spread_sems.at[unit, 0], spare.at[0], at_x)
            first = half_spot(unit, (y, 1 - x, core), 0)
            copies.send(first, first, spread_sems.at[unit, 2], at_y)
            copies.send(spot, spot, core_sems.at[unit, 1], at_core)
            spot = spot_of(unit, (1 - y, x, core))
            wait_arrival(spot, spread_sems.at[unit, 1], spare.at[0], at_y)
            second = half_spot(unit, (1 - y, x, core), 1)
            copies.send(second, second, spread_sems.at[unit, 3], at_x)
            copies.send(spot, spot, core_sems.at[unit, 2], at_core)

    def corner(group):
        for unit in group:
            where = (1 - y, 1 - x, core)
            wait_arrival(half_spot(unit, where, 0), spread_sems.at[unit, 2], spare.at[0], at_y)
            wait_arrival(half_spot(unit, where, 1), spread_sems.at[unit, 3], spare.at[0], at_x)
            spot = spot_of(unit, where)
            copies.send(spot, spot, core_sems.at[unit, 3], at_core)

    def finish(group):
        for unit in group:
            pltpu.make_async_copy(
                result[unit], spot_of(unit, (y, x, core)), load_sems.at[3 + unit]
            ).wait()
            for entry, where in enumerate(((y, x), (y, 1 - x), (1 - y, x), (1 - y, 1 - x))):
                spot = spot_of(unit, (*where, 1 - core))
                wait_arrival(spot, core_sems.at[unit, entry], spare.at[0], at_core)

    def mlp(step):
        t, slot = ITEM_ORDER[step], step % 2
        for copy in streams[step]:
            copy.wait()
        inner = (back_dot(low[...], downs[slot]) * slopes[slot]).astype(jnp.bfloat16)
        grad_inner[...] = inner
        rows_out[8 + t : 9 + t] = jnp.sum(inner.astype(jnp.float32), axis=0, keepdims=True)
        put(2, t, contract_rows(rounded[...], grad_inner[...]))
        put(3, t, contract_rows(actives[slot], low[...]))
        upstream[...] += back_dot(grad_inner[...], ups[slot])
        if step < 2:
            streams.append(stream(step + 2))
        share(step)

    def project(step):
        t = ITEM_ORDER[step]
        put(0, t, contract_rows(grad_qkv[t], rounded[...]))
        upstream[...] += product(grad_qkv[t], attend_w[t])
        share(4 + step)

    rows_out[...] = jnp.zeros_like(rows_out)
    for copy in first_loads:
        copy.wait()
    low[...] = grad[...].astype(low.dtype)
    rows_out[4:5] = jnp.sum(low[...].astype(jnp.float32), axis=0, keepdims=True)
    upstream[...] = jnp.zeros_like(upstream)
    mlp(0)
    mlp(1)
    core_sum(0)
    mlp(2)
    core_sum(1)
    mlp(3)
    core_sum(2)
    one(0)
    rows_out[2:3], rows_out[3:4] = norm_back_into(grad, values, upstream, gains[2:3])
    later_loads = [load(hidden, values, 2), load(normed, rounded, 1)]
    low[...] = grad[...].astype(low.dtype)
    for t in range(4):
        put(1, t, contract_rows(mixed[t], low[...]))
        grad_mixed[t] = back_dot(low[...], merge_w[t]).astype(grad_mixed.dtype)
    core_sum(3)
    one(1)
    attend_back_into(qkv, allowed, grad_mixed, grad_qkv, 0, 2)
    one(2)
    two(0)
    attend_back_into(qkv, allowed, grad_mixed, grad_qkv, 2, 4)
    one(3)
    two(1)
    upstream[...] = jnp.zeros_like(upstream)
    for copy in later_loads:
        copy.wait()
    project(0)
    project(1)
    core_sum(4)
    two(2)
    project(2)
    core_sum(5)
    two(3)
    project(3)
    core_sum(6)
    one(4)
    rows_out[0:1], rows_out[1:2] = norm_back_into(grad, values, upstream, gains[0:1])
    core_sum(7)
    one(5)
    over_z(MLP_GROUP)
    two(4)
    one(6)
    two(5)
    one(7)
    spread(MLP_GROUP)
    two(6)
    corner(MLP_GROUP)
    two(7)
    over_z(ATTEND_GROUP)
    spread(ATTEND_GROUP)
    corner(ATTEND_GROUP)
    finish(MLP_GROUP)
    finish(ATTEND_GROUP)
    copies.finish()
    for t, copy in conditional:

        @pl.when(z != t)
        def _(copy=copy):
            copy.wait_send()


def owner_shape(weight):
    count = 1 if weight.shape[1] == D else weight.shape[1] // 64
    return (count, 2, 2, 2, weight.shape[1] // (8 * count), D)


def layer_back_reduce(layer_index, grad, allowed, gains, weights, stored):
    hidden, normed, qkv, mixed, hidden_mid, normed_mlp, slope, active = stored
    attend_w, merge_w, up_w, down_w = weights
    rows, heads = grad.shape[0], attend_w.shape[1] // (3 * HEAD_DIM)
    low, full = jnp.bfloat16, jnp.float32
    vmem = pl.BlockSpec(memory_space=pltpu.VMEM)
    anywhere = pl.BlockSpec(memory_space=pl.ANY)
    shapes = [owner_shape(weight) for weight in weights]
    scratch = []
    for lead in ((4, 2, 2, 2), (4, 2, 2), (4, 2), (4,), (4,), ()):
        for shape in shapes:
            whole = lead[:1] + shape[:1] + lead[1:] + shape[4:]
            scratch.append(pltpu.VMEM(whole, low))
    dma = pltpu.SemaphoreType.DMA
    scratch += [
        pltpu.VMEM((rows, D), low),
        pltpu.VMEM((rows, D), low),
        pltpu.VMEM((4, rows, heads * HEAD_DIM), low),
        pltpu.VMEM((4, rows, heads * 3 * HEAD_DIM), low),
        pltpu.VMEM((rows, D), full),
        pltpu.VMEM((rows, D), full),
        pltpu.VMEM((rows, D), low),
        pltpu.VMEM((2, rows, D), slope.dtype),
        pltpu.VMEM((2, rows, D), low),
        pltpu.VMEM((2, D, D), low),
        pltpu.VMEM((2, D, D), low),
        dma((4 * 24,)),
        dma((4, 3, 4)),
        dma((4, 4)),
        dma((4, 4)),
        dma((4, 4)),
        dma((1,)),
        dma((7,)),
        dma((2, 4)),
    ]
    outs = [jax.ShapeDtypeStruct((rows, D), full), jax.ShapeDtypeStruct((16, D), full)]
    outs += [jax.ShapeDtypeStruct(shape, low) for shape in shapes]
    after, rows_out, *sums = pl.pallas_call(
        layer_back_kernel,
        out_shape=outs,
        in_specs=[anywhere] * 9 + [vmem] * 6,
        out_specs=[vmem] * 2 + [anywhere] * 4,
        scratch_shapes=scratch,
        compiler_params=pltpu.CompilerParams(
            collective_id=2 + layer_index, has_side_effects=True, vmem_limit_bytes=BACK_LIMIT
        ),
        name="layer_back_reduce",
    )(
        grad, hidden, hidden_mid, normed, normed_mlp, slope, active, up_w, down_w,
        qkv, mixed, allowed, gains, attend_w, merge_w,
    )
    return (after, rows_out, [entry.reshape(-1, D) for entry in sums])


BACK_LIMIT = 66 * 1000 * 1000


def shards(
    patches,
    valid_mask,
    class_ids,
    embed_weight,
    embed_bias,
    position_table,
    class_table,
    attn_gain,
    attn_offset,
    attend_weight,
    merge_weight,
    mlp_gain,
    mlp_offset,
    up_weight,
    up_bias,
    down_weight,
    down_bias,
    final_gain,
    final_offset,
    head_weight,
    head_bias,
    latent_cot,
    logdet_cot,
):
    shard_count = patches.shape[0]
    local_images = shard_count // P_SIZE
    tensor_index = lax.axis_index("tensor")
    tensor_count = lax.axis_size("tensor")
    batch_count = lax.axis_size("batch")
    device_index = lax.axis_index("batch") * tensor_count + tensor_index
    device_count = batch_count * tensor_count
    patch_values = patches.astype(jnp.float32)
    local_valid = lax.dynamic_slice_in_dim(valid_mask, tensor_index * shard_count, shard_count, 0)
    live_mask = local_valid.astype(jnp.float32)[:, None]
    allowed = build_allowed(local_valid, P_SIZE).astype(jnp.float32)
    embed_full = embed_weight.astype(jnp.float32)
    shards = []
    for layer_index in range(NL):
        shards.append(jnp.swapaxes(attend_weight[layer_index], 1, 2).reshape(-1, D))
        shards.append(merge_weight[layer_index])
        shards.append(up_weight[layer_index])
        shards.append(down_weight[layer_index])
    wholes, bias_all = gather_weights(shards, up_bias)
    layers = []
    for layer_index in range(NL):
        weights = [
            whole.reshape(tensor_count, -1, D)
            for whole in wholes[4 * layer_index : 4 * layer_index + 4]
        ]
        gains = jnp.stack(
            [attn_gain[layer_index], attn_offset[layer_index], mlp_gain[layer_index]]
            + [mlp_offset[layer_index], down_bias[layer_index]]
        )
        layers.append((gains, bias_all[:, layer_index], weights))
    choose = class_ids[:, None] == lax.broadcasted_iota(jnp.int32, (local_images, CLASSES), 1)
    class_rows = product(choose.astype(jnp.bfloat16), class_table)
    hidden = product(patches, embed_weight) + embed_bias
    hidden = hidden.reshape(local_images, P_SIZE, D) + position_table.astype(jnp.float32)[None]
    hidden = (hidden + class_rows[:, None]).reshape(shard_count, D)
    stored = []
    for layer_index in range(NL):
        gains, bias, weights = layers[layer_index]
        *kept, after = layer_forward(hidden, allowed, gains, bias, weights)
        stored.append((hidden, *kept))
        hidden = after
    final = layer_norm(hidden, final_gain, final_offset)
    final_low = final.astype(jnp.bfloat16)
    head_out = product(final_low, head_weight) + head_bias
    position = lax.broadcasted_iota(jnp.int32, (shard_count, 1), 0) % P_SIZE
    starts = position == 0
    previous = jnp.concatenate([jnp.zeros((1, 2 * PV), jnp.float32), head_out[:-1]], axis=0)
    previous = jnp.where(starts, 0.0, previous)
    shift_part = previous[:, :PV]
    log_scale = previous[:, PV:]
    scale_factor = jnp.exp(-log_scale)
    latents = (
        live_mask * (patch_values - shift_part) * scale_factor + (1.0 - live_mask) * patch_values
    )
    log_det = -jnp.sum((live_mask * log_scale).reshape(local_images, P_SIZE * PV), axis=1)
    image_cot = jnp.repeat(logdet_cot, P_SIZE)[:, None]
    direct_grad = latent_cot * (live_mask * scale_factor + (1.0 - live_mask))
    grad_shift = -live_mask * latent_cot * scale_factor
    grad_scale = -live_mask * (latent_cot * (patch_values - shift_part) * scale_factor + image_cot)
    grad_previous = jnp.where(starts, 0.0, jnp.concatenate([grad_shift, grad_scale], axis=1))
    grad_head = jnp.concatenate([grad_previous[1:], jnp.zeros((1, 2 * PV), jnp.float32)], axis=0)
    grad_head_low = grad_head.astype(jnp.bfloat16)
    head_weight_grad = contract_rows(grad_head_low, final_low)
    head_bias_grad = jnp.sum(grad_head_low.astype(jnp.float32), axis=0)
    grad_final = back_dot(grad_head_low, head_weight)
    grad_hidden, final_gain_grad, final_offset_grad = norm_backward(
        hidden, final_gain, final_offset, grad_final
    )
    rows_of = {}
    split_list = [None] * NL
    for layer_index in reversed(range(NL)):
        gains, bias, weights = layers[layer_index]
        if fast_mesh():
            grad_hidden, rows_of[layer_index], split_list[layer_index] = layer_back_reduce(
                layer_index, grad_hidden, allowed, gains, weights, stored[layer_index]
            )
        else:
            grad_hidden, rows_of[layer_index], *split_list[layer_index] = layer_backward(
                grad_hidden, allowed, gains, weights, stored[layer_index]
            )
    per_image = grad_hidden.reshape(local_images, P_SIZE, D)
    image_count = device_count * local_images
    image_index = device_index * local_images
    image_rows = lax.dynamic_update_slice_in_dim(
        jnp.zeros((image_count, D), jnp.float32), jnp.sum(per_image, axis=1), image_index, 0
    )
    id_rows = jnp.stack([class_ids // 32, class_ids % 32]).astype(jnp.float32)
    id_rows = lax.dynamic_update_slice(jnp.zeros((2, D), jnp.float32), id_rows, (0, image_index))
    small = [
        jnp.sum(per_image, axis=0),
        precise_rows(patch_values, grad_hidden),
        head_weight_grad,
        image_rows,
        jnp.sum(grad_hidden, axis=0)[None],
        final_gain_grad[None],
        final_offset_grad[None],
        jnp.pad(head_bias_grad, (0, D - 2 * PV))[None],
    ]
    small += [rows_of[0], rows_of[1], id_rows]
    lengths = [entry.shape[0] for entry in small]
    joined = jnp.concatenate(small, axis=0)
    joined = jnp.pad(joined, ((0, -joined.shape[0] % (8 * device_count)), (0, 0)))
    sums, small_sum = reduce_weights(split_list, joined)
    for layer_index in range(NL):
        attend_sum, merge_sum, up_sum, down_sum = sums[4 * layer_index : 4 * layer_index + 4]
        split_list[layer_index] = (
            jnp.swapaxes(attend_sum.reshape(3, -1, D), 1, 2).astype(jnp.float32),
            merge_sum.astype(jnp.float32),
            up_sum.astype(jnp.float32),
            down_sum.astype(jnp.float32),
        )
    patches_grad = direct_grad + lax.dot_general(
        grad_hidden,
        embed_full,
        (((1,), (1,)), ((), ())),
        precision=HIGHEST,
        preferred_element_type=jnp.float32,
    )
    small_sum = small_sum.astype(jnp.float32)
    small_list = []
    begin = 0
    for length in lengths:
        small_list.append(small_sum[begin : begin + length])
        begin += length
    id_sums = small_list[10][:, :image_count].astype(jnp.int32)
    all_ids = id_sums[0] * 32 + id_sums[1]
    choose_all = all_ids[:, None] == lax.broadcasted_iota(
        jnp.int32, (image_count, CLASSES), 1
    )
    class_grad = precise_rows(choose_all.astype(jnp.float32), small_list[3])
    layer_rows = small_list[8:10]
    own_bias = [lax.dynamic_slice_in_dim(entry, 8 + tensor_index, 1, 0) for entry in layer_rows]
    split_stack = [jnp.stack([entry[member] for entry in split_list]) for member in range(4)]
    shared_stack = [
        jnp.stack([entry[member] for entry in layer_rows]) for member in range(5)
    ]
    return (
        latents,
        log_det,
        patches_grad,
        small_list[1],
        small_list[4][0],
        small_list[0],
        class_grad,
        shared_stack[0],
        shared_stack[1],
        split_stack[0],
        split_stack[1],
        shared_stack[2],
        shared_stack[3],
        split_stack[2],
        jnp.concatenate(own_bias, axis=0),
        split_stack[3],
        shared_stack[4],
        small_list[5][0],
        small_list[6][0],
        jnp.swapaxes(small_list[2], 0, 1),
        small_list[7][0, : 2 * PV],
    )


def solution(mesh):
    return jax.shard_map(
        shards,
        mesh=mesh,
        in_specs=(
            P(("batch", "tensor"), None),
            P("batch"),
            P(("batch", "tensor")),
            P(),
            P(),
            P(),
            P(),
            P(),
            P(),
            P(None, None, None, "tensor"),
            P(None, "tensor", None),
            P(),
            P(),
            P(None, None, "tensor"),
            P(None, "tensor"),
            P(None, "tensor", None),
            P(),
            P(),
            P(),
            P(),
            P(),
            P(("batch", "tensor"), None),
            P(("batch", "tensor")),
        ),
        out_specs=(
            P(("batch", "tensor"), None),
            P(("batch", "tensor")),
            P(("batch", "tensor"), None),
            P(),
            P(),
            P(),
            P(),
            P(),
            P(),
            P(None, None, None, "tensor"),
            P(None, "tensor", None),
            P(),
            P(),
            P(None, None, "tensor"),
            P(None, "tensor"),
            P(None, "tensor", None),
            P(),
            P(),
            P(),
            P(),
            P(),
        ),
        check_vma=False,
    )
```

```python
import functools

import jax
import jax.numpy as jnp
from jax import lax
from jax.experimental import pallas as pl
from jax.experimental.pallas import tpu as pltpu
from jax.sharding import PartitionSpec as P

D = 768
HEAD_DIM = 64
P_SIZE = 256
PV = 48
CLASSES = 1000
NL = 2


EPSILON = 1e-05
NEGATIVE = -1000000000.0
HIGHEST = lax.Precision.HIGHEST


def layer_norm(values, norm_gain, norm_offset):
    center = values - jnp.mean(values, axis=-1, keepdims=True)
    spread = jnp.mean(center * center, axis=-1, keepdims=True)
    return center * lax.rsqrt(spread + EPSILON) * norm_gain + norm_offset


def norm_backward(values, norm_gain, norm_offset, upstream):
    outputs, pullback = jax.vjp(layer_norm, values, norm_gain, norm_offset)
    return pullback(upstream)


def gelu_parts(values):
    share = 0.5 + 0.5 * lax.erf(values * (0.5**0.5))
    slope = share + values * (jnp.exp(-0.5 * values * values) * ((0.5 / jnp.pi) ** 0.5))
    return (values * share, slope)


def product(former, latter):
    return jnp.dot(former, latter, preferred_element_type=jnp.float32)


def contract_rows(former, latter):
    return lax.dot_general(
        former, latter, (((0,), (0,)), ((), ())), preferred_element_type=jnp.float32
    )


def precise_rows(former, latter):
    return lax.dot_general(
        former,
        latter,
        (((0,), (0,)), ((), ())),
        precision=HIGHEST,
        preferred_element_type=jnp.float32,
    )


def build_allowed(mask_rows, span):
    row_index = lax.broadcasted_iota(jnp.int32, (span, span), 0)
    col_index = lax.broadcasted_iota(jnp.int32, (span, span), 1)
    causal = (row_index // P_SIZE == col_index // P_SIZE) & (col_index <= row_index)
    key_valid = mask_rows.reshape(mask_rows.shape[0] // span, 1, span) > 0
    return causal[None] & (key_valid | (row_index == col_index)[None])


def gather_rows(parts):
    batch_count = lax.axis_size("batch")
    batch_index = lax.axis_index("batch")
    pieces = []
    for part in parts:
        rows = part.shape[0] // batch_count
        pieces.append(lax.dynamic_slice_in_dim(part, batch_index * rows, rows, 0))
    piece = jnp.concatenate(pieces, axis=0)
    group = lax.all_gather(piece, "tensor", axis=0)
    whole = lax.all_gather(group, "batch", axis=0)
    results = []
    begin = 0
    for entry in pieces:
        results.append(whole[:, :, begin : begin + entry.shape[0]])
        begin += entry.shape[0]
    return results


def reduce_rows(parts):
    joined = jnp.concatenate([part.astype(jnp.bfloat16) for part in parts], axis=2)
    over_batch = lax.psum_scatter(joined, "batch", scatter_dimension=0)
    own = lax.psum_scatter(over_batch, "tensor", scatter_dimension=0)
    whole = lax.all_gather(own, "batch", axis=0)
    results = []
    begin = 0
    for part in parts:
        results.append(whole[:, begin : begin + part.shape[2]])
        begin += part.shape[2]
    return results


def to_tensor_major(blocks):
    return jnp.swapaxes(blocks, 0, 1).reshape(-1, blocks.shape[-1])


def to_batch_major(rows):
    batch_count = lax.axis_size("batch")
    tensor_count = lax.axis_size("tensor")
    return jnp.swapaxes(rows.reshape(tensor_count, batch_count, -1, rows.shape[-1]), 0, 1)


def split_blocks(rows):
    batch_count = lax.axis_size("batch")
    tensor_count = lax.axis_size("tensor")
    return rows.reshape(batch_count, tensor_count, -1, rows.shape[-1])


MESH = pl.DeviceIdType.MESH
SWAP_TENSOR = (1, 2, 3)


def place():
    batch_index = lax.axis_index("batch")
    tensor_index = lax.axis_index("tensor")
    return (batch_index // 4, batch_index // 2 % 2, batch_index % 2, tensor_index)


def device_at(y, x, core, z):
    return (y * 4 + x * 2 + core, z)


def flipped(index, bits):
    high, low = index // 2, index % 2
    if bits & 2:
        high = 1 - high
    if bits & 1:
        low = 1 - low
    return high * 2 + low


def greet(devices):
    barrier = pltpu.get_barrier_semaphore()
    for device in devices:
        pl.semaphore_signal(barrier, inc=1, device_id=device, device_id_type=MESH)
    pl.semaphore_wait(barrier, len(devices))


def partners():
    y, x, core, z = place()
    devices = [device_at(y, x, core, flipped(z, bits)) for bits in SWAP_TENSOR]
    devices.append(device_at(y, 1 - x, core, z))
    devices.append(device_at(1 - y, x, core, z))
    devices.append(device_at(y, x, 1 - core, z))
    return devices


def halves(count):
    return (slice(0, (count + 1) // 2), slice((count + 1) // 2, count))


class Copies:
    def __init__(self, send_sems):
        self.send_sems = send_sems
        self.count = 0
        self.sent = []

    def send(self, source, target, recv_sem, device, keep=True):
        copy = pltpu.make_async_remote_copy(
            src_ref=source,
            dst_ref=target,
            send_sem=self.send_sems.at[self.count],
            recv_sem=recv_sem,
            device_id=device,
            device_id_type=MESH,
        )
        self.count += 1
        copy.start()
        if keep:
            self.sent.append(copy)
        return copy

    def finish(self):
        for copy in self.sent:
            copy.wait_send()


def wait_arrival(target, recv_sem, send_sem, device):
    pltpu.make_async_remote_copy(
        src_ref=target,
        dst_ref=target,
        send_sem=send_sem,
        recv_sem=recv_sem,
        device_id=device,
        device_id_type=MESH,
    ).wait_recv()


def spread_piece(ref, lead, b):
    if len(ref.shape) == len(lead) + 4:
        return ref.at[(*lead, slice(None), b)]
    return ref.at[(*lead, b)]


def half_piece(ref, lead, b, side):
    if len(ref.shape) == len(lead) + 4:
        return ref.at[(*lead, halves(ref.shape[len(lead)])[side], b)]
    return ref.at[(*lead, b, halves(ref.shape[len(lead) + 1])[side])]


GROUP = 2


def forward_kernel(*refs):
    units = 4 * NL
    shards = refs[:units]
    bias, patches, embed_w, embed_b, table, class_rows, valid = refs[units : units + 7]
    gains = refs[units + 7 : units + 7 + NL]
    outs = refs[units + 7 + NL :]
    fulls, bias_full, hidden_out = outs[:units], outs[units], outs[units + 1]
    kept = [outs[units + 2 + 8 * layer : units + 10 + 8 * layer] for layer in range(NL)]
    rest = outs[units + 2 + 8 * NL :]
    weights, (bias_v, allowed, hidden_a, hidden_b) = rest[:4], rest[4:8]
    stores = rest[8:15]
    send_sems, z_sems, xy_sems, core_sems, local_sems, bias_sems, spare = rest[15:22]
    weight_sems, keep_sems = rest[22:]
    y, x, core, z = place()
    b = y * 4 + x * 2 + core
    over_x = y * 4 + (1 - x) * 2 + core
    over_y = (1 - y) * 4 + x * 2 + core
    corner = (1 - y) * 4 + (1 - x) * 2 + core
    at_x = device_at(y, 1 - x, core, z)
    at_y = device_at(1 - y, x, core, z)
    at_core = device_at(y, x, 1 - core, z)
    middle = (z + 1) // 2 % 2
    near = flipped(z, 1)
    across = 3 - z
    far = (z + 2) % 4
    at_near = device_at(y, x, core, near)
    at_across = device_at(y, x, core, across)
    order = (
        near,
        middle * across + (1 - middle) * far,
        middle * far + (1 - middle) * across,
    )
    greet(partners())
    copies = Copies(send_sems)
    conditional = []
    local_of = {}
    for unit in range(units):
        copy = pltpu.make_async_copy(shards[unit], fulls[unit].at[z], local_sems.at[unit])
        copy.start()
        local_of[unit] = copy
    local_bias = pltpu.make_async_copy(bias, bias_full.at[z], local_sems.at[units])
    local_bias.start()
    for entry, bits in enumerate(SWAP_TENSOR):
        copies.send(
            bias,
            bias_full.at[z],
            bias_sems.at[entry],
            device_at(y, x, core, flipped(z, bits)),
        )

    def of_layer(layer):
        return range(layer * GROUP, (layer + 1) * GROUP)

    def send_if_middle(source, target, recv_sem, device):
        slot = send_sems.at[copies.count]
        copies.count += 1
        copy = pltpu.make_async_remote_copy(
            src_ref=source,
            dst_ref=target,
            send_sem=slot,
            recv_sem=recv_sem,
            device_id=device,
            device_id_type=MESH,
        )

        @pl.when(middle == 1)
        def _():
            copy.start()

        conditional.append(copy)

    def take_bias():
        for entry, bits in enumerate(SWAP_TENSOR):
            t = flipped(z, bits)
            wait_arrival(
                bias_full.at[t], bias_sems.at[entry], spare.at[0], device_at(y, x, core, t)
            )
        local_bias.wait()
        copy = pltpu.make_async_copy(bias_full, bias_v, weight_sems.at[units])
        copy.start()
        copy.wait()

    def begin(layer):
        for unit in of_layer(layer):
            mine = spread_piece(shards[unit], (), b)
            target = spread_piece(fulls[unit], (z,), b)
            copies.send(mine, target, z_sems.at[unit, z], at_near)
            send_if_middle(mine, target, z_sems.at[unit, z], at_across)

    def take_z(layer, step):
        t = order[step]
        for unit in of_layer(layer):
            piece = spread_piece(fulls[unit], (t,), b)
            wait_arrival(piece, z_sems.at[unit, t], spare.at[0], at_near)
            send_if_middle(
                piece, piece, z_sems.at[unit, t], at_across if step == 0 else at_near
            )
        for unit in of_layer(layer):
            piece = spread_piece(fulls[unit], (t,), b)
            copies.send(piece, piece, xy_sems.at[unit, step, 0], at_x)
            copies.send(piece, piece, xy_sems.at[unit, step, 1], at_y)
            copies.send(piece, piece, core_sems.at[unit, step, 0], at_core)

    def take_xy(layer, step):
        t = order[step]
        for unit in of_layer(layer):
            piece = spread_piece(fulls[unit], (t,), over_x)
            wait_arrival(piece, xy_sems.at[unit, step, 0], spare.at[0], at_x)
            first = half_piece(fulls[unit], (t,), over_x, 0)
            copies.send(first, first, xy_sems.at[unit, step, 2], at_y)
            copies.send(piece, piece, core_sems.at[unit, step, 1], at_core)
        for unit in of_layer(layer):
            piece = spread_piece(fulls[unit], (t,), over_y)
            wait_arrival(piece, xy_sems.at[unit, step, 1], spare.at[0], at_y)
            second = half_piece(fulls[unit], (t,), over_y, 1)
            copies.send(second, second, xy_sems.at[unit, step, 3], at_x)
            copies.send(piece, piece, core_sems.at[unit, step, 2], at_core)

    def take_corner(layer, step):
        t = order[step]
        for unit in of_layer(layer):
            first = half_piece(fulls[unit], (t,), corner, 0)
            second = half_piece(fulls[unit], (t,), corner, 1)
            wait_arrival(first, xy_sems.at[unit, step, 2], spare.at[0], at_y)
            wait_arrival(second, xy_sems.at[unit, step, 3], spare.at[0], at_x)
            piece = spread_piece(fulls[unit], (t,), corner)
            copies.send(piece, piece, core_sems.at[unit, step, 3], at_core)

    def take_core_step(layer, step):
        t = order[step]
        for unit in of_layer(layer):
            for entry, owner in enumerate((b, over_x, over_y, corner)):
                other = owner + 1 - 2 * core
                piece = spread_piece(fulls[unit], (t,), other)
                wait_arrival(piece, core_sems.at[unit, step, entry], spare.at[0], at_core)

    pending = {}

    def keep(entry, layer, source, target):
        copy = pltpu.make_async_copy(source, target, keep_sems.at[layer, entry])
        copy.start()
        pending[entry] = copy

    def free(*entries):
        for entry in entries:
            if entry in pending:
                pending.pop(entry).wait()

    def fetch(group):
        take_core(group)
        copies = []
        for unit in of_layer(group):
            if unit in local_of:
                local_of.pop(unit).wait()
            target = weights[unit % 4]
            copy = pltpu.make_async_copy(
                fulls[unit].reshape(target.shape), target, weight_sems.at[unit]
            )
            copy.start()
            copies.append(copy)
        return copies

    def take_core(group):
        for step in range(3):
            take_core_step(group, step)

    def embed():
        row_index = lax.broadcasted_iota(jnp.int32, (P_SIZE, P_SIZE), 0)
        col_index = lax.broadcasted_iota(jnp.int32, (P_SIZE, P_SIZE), 1)
        for image in range(patches.shape[0] // P_SIZE):
            key_valid = jnp.where(row_index == col_index, 1.0, valid[image : image + 1])
            allowed[image] = jnp.where(col_index <= row_index, key_valid, 0.0)
            rows = slice(image * P_SIZE, (image + 1) * P_SIZE)
            value = product(patches[rows], embed_w[...]) + embed_b[...]
            value = value + table[...].astype(jnp.float32)
            hidden_a[rows] = value + class_rows[image : image + 1]
        keep(7, 0, hidden_a, hidden_out)

    normed, qkv, mixed, hidden_mid, normed_mlp, slope, active = stores
    attend_w, merge_w, up_w, down_w = weights

    def chunks(group):
        layer = group // 2
        gain, outputs = gains[layer], kept[layer]
        before, after = (hidden_a, hidden_b) if layer % 2 == 0 else (hidden_b, hidden_a)

        def start():
            free(0, 1)
            norm_into(before, gain[0:1], gain[1:2], normed)

            def project(t):
                qkv[t] = back_dot(normed[...], attend_w[t]).astype(qkv.dtype)

            each_part(project)
            keep(0, layer, normed, outputs[0])
            keep(1, layer, qkv, outputs[1])

        def attend_first():
            free(2)
            attend_into(qkv, allowed, mixed, 0, 2)

        def attend_second():
            attend_into(qkv, allowed, mixed, 2, 4)
            keep(2, layer, mixed, outputs[2])

        def merge():
            free(3, 4)
            total = before[...]
            for t in range(4):
                total = total + product(mixed[t], merge_w[t])
            hidden_mid[...] = total
            norm_into(hidden_mid, gain[2:3], gain[3:4], normed_mlp)
            keep(3, layer, hidden_mid, outputs[3])
            keep(4, layer, normed_mlp, outputs[4])

        def up(t):
            inner = product(normed_mlp[...], up_w[t]) + bias_v[t, layer : layer + 1]
            value, rise = gelu_parts(inner)
            active[t] = value.astype(active.dtype)
            slope[t] = rise.astype(slope.dtype)

        def up_first():
            free(5, 6)
            each_part(up, 0, 2)

        def up_second():
            each_part(up, 2, 4)
            keep(5, layer, slope, outputs[5])
            keep(6, layer, active, outputs[6])

        def down():
            free(7 if layer % 2 else 8)
            total = hidden_mid[...] + gain[4:5]
            for t in range(4):
                total = total + product(active[t], down_w[t])
            after[...] = total
            keep(8 - layer % 2, layer, after, outputs[7])

        def nothing():
            pass

        if group % 2 == 0:
            return [start, attend_first, attend_second, merge]
        return [up_first, up_second, down, nothing]

    groups = units // GROUP
    begin(0)
    embed()
    work = None
    for group in range(groups):
        take_z(group, 0)
        if work:
            work[1]()
        take_z(group, 1)
        if work:
            work[2]()
        if group:
            take_corner(group - 1, 1)
        if work:
            work[3]()
        take_xy(group, 0)
        take_z(group, 2)
        if group + 1 < groups:
            begin(group + 1)
        if group:
            take_corner(group - 1, 2)
        take_xy(group, 1)
        loads = fetch(group - 1) if group else ()
        if group == 1:
            take_bias()
        take_corner(group, 0)
        for copy in loads:
            copy.wait()
        work = chunks(group - 1) if group else None
        if work:
            work[0]()
        take_xy(group, 2)
    take_corner(groups - 1, 1)
    if work:
        work[1]()
    take_corner(groups - 1, 2)
    if work:
        work[2]()
        work[3]()
    for copy in fetch(groups - 1):
        copy.wait()
    for chunk in chunks(groups - 1):
        chunk()
    free(*list(pending))
    copies.finish()

    @pl.when(middle == 1)
    def _():
        for copy in conditional:
            copy.wait_send()


def forward_all(shards, bias, embedding, valid, gains):
    units = len(shards)
    rows = embedding[0].shape[0]
    heads = shards[0].size // (3 * HEAD_DIM * D)
    low, full = jnp.bfloat16, jnp.float32
    outs = [jax.ShapeDtypeStruct((4, *shard.shape), shard.dtype) for shard in shards]
    outs.append(jax.ShapeDtypeStruct((4, *bias.shape), bias.dtype))
    outs.append(jax.ShapeDtypeStruct((rows, D), full))
    shapes = layer_shapes(rows, heads)
    outs += shapes * NL
    vmem = pl.BlockSpec(memory_space=pltpu.VMEM)
    anywhere = pl.BlockSpec(memory_space=pl.ANY)
    dma = pltpu.SemaphoreType.DMA
    inputs = [*shards, bias, *embedding, valid, *gains]
    scratch = [pltpu.VMEM((4, shard.size // D, D), low) for shard in shards[:4]]
    scratch.append(pltpu.VMEM((4, *bias.shape), full))
    scratch.append(pltpu.VMEM((rows // P_SIZE, P_SIZE, P_SIZE), full))
    scratch += [pltpu.VMEM((rows, D), full)] * 2
    scratch += [pltpu.VMEM(shape.shape, shape.dtype) for shape in shapes[:7]]
    return pl.pallas_call(
        forward_kernel,
        out_shape=outs,
        in_specs=[vmem] * len(inputs),
        out_specs=[anywhere] * len(outs),
        scratch_shapes=scratch
        + [
            dma((3 + units * (2 + 3 * 9),)),
            dma((units, 4)),
            dma((units, 3, 4)),
            dma((units, 3, 4)),
            dma((units + 1,)),
            dma((3,)),
            dma((1,)),
            dma((units + 1,)),
            dma((NL, 9)),
        ],
        compiler_params=pltpu.CompilerParams(
            collective_id=0, has_side_effects=True, vmem_limit_bytes=BACK_LIMIT
        ),
        name="gather_forward",
    )(*inputs)


def add_slab(target, addend):
    target[...] = (target[...].astype(jnp.float32) + addend[...].astype(jnp.float32)).astype(
        target.dtype
    )


ITEM_ORDER = (0, 2, 1, 3)


def fast_mesh():
    return lax.axis_size("batch") == 8 and lax.axis_size("tensor") == 4


def forward_layers(shards, bias, embedding, valid, allowed, gains):
    if not fast_mesh():
        tensor_count = lax.axis_size("tensor")
        wholes = [
            to_tensor_major(blocks).reshape(tensor_count, -1, D) for blocks in gather_rows(shards)
        ]
        bias_all = lax.all_gather(bias, "tensor", axis=0)
        patches, embed_weight, embed_bias, table, class_rows = embedding
        hidden = product(patches, embed_weight) + embed_bias
        hidden = hidden.reshape(-1, P_SIZE, D) + table.astype(jnp.float32)[None]
        hidden = (hidden + class_rows[:, None]).reshape(-1, D)
        stored = []
        for layer_index in range(NL):
            weights = wholes[4 * layer_index : 4 * layer_index + 4]
            *kept, after = layer_forward(
                hidden, allowed, gains[layer_index], bias_all[:, layer_index], weights
            )
            stored.append((hidden, *kept))
            hidden = after
        return (wholes, stored, hidden)
    parts = [
        shard.reshape((8, -1, D) if shard.shape[0] == D else (-1, 8, 8, D)) for shard in shards
    ]
    results = forward_all(parts, jnp.pad(bias, ((0, 8 - NL), (0, 0))), embedding, valid, gains)
    units = len(shards)
    wholes = [whole.reshape(4, -1, D) for whole in results[:units]]
    hidden = results[units + 1]
    stored = []
    for layer_index in range(NL):
        *kept, after = results[units + 2 + 8 * layer_index : units + 10 + 8 * layer_index]
        stored.append((hidden, *kept))
        hidden = after
    return (wholes, stored, hidden)


def back_dot(former, latter):
    return lax.dot_general(
        former, latter, (((1,), (1,)), ((), ())), preferred_element_type=jnp.float32
    )


def row_blocks(count, size, body, carry=0):
    def step(index, carry):
        return body(pl.ds(pl.multiple_of(index * size, size), size), carry)

    return lax.fori_loop(0, count // size, step, carry)


def norm_into(source, gain, offset, target):
    def body(rows, carry):
        target[rows] = layer_norm(source[rows], gain, offset).astype(target.dtype)
        return carry

    row_blocks(source.shape[0], 128, body)


def norm_back_into(grad, source, upstream, gain):
    def body(rows, carry):
        gain_sum, offset_sum = carry
        values, above = source[rows], upstream[rows]
        center = values - jnp.mean(values, axis=-1, keepdims=True)
        spread = jnp.mean(center * center, axis=-1, keepdims=True)
        scale = lax.rsqrt(spread + EPSILON)
        normal = center * scale
        part = above * gain
        gain_sum = gain_sum + jnp.sum(above * normal, axis=0, keepdims=True)
        offset_sum = offset_sum + jnp.sum(above, axis=0, keepdims=True)
        inner = jnp.mean(part, axis=-1, keepdims=True)
        along = jnp.mean(part * normal, axis=-1, keepdims=True)
        grad[rows] = grad[rows] + scale * (part - inner - normal * along)
        return (gain_sum, offset_sum)

    zero = jnp.zeros((1, D), jnp.float32)
    return row_blocks(source.shape[0], 128, body, (zero, zero))


def head_probs(qkv, allowed, t, rows, image, head):
    span = qkv.shape[2] // 3
    queries, keys, values = (
        qkv[t, rows, c * span + head * HEAD_DIM : c * span + (head + 1) * HEAD_DIM]
        for c in range(3)
    )
    scores = back_dot(queries, keys) * (HEAD_DIM ** (-0.5))
    scores = jnp.where(allowed[image] > 0, scores, NEGATIVE)
    top = jnp.max(scores, axis=-1, keepdims=True)
    powers = jnp.exp(scores - top)
    total = jnp.sum(powers, axis=-1, keepdims=True)
    return (queries, keys, values, powers * (1.0 / total))


def each_image(qkv, body, begin=0, end=4):
    images = qkv.shape[1] // P_SIZE

    def step(index, carry):
        t, image = index // images, index % images
        body(t, image, pl.ds(pl.multiple_of(image * P_SIZE, P_SIZE), P_SIZE))
        return carry

    lax.fori_loop(begin * images, end * images, step, 0)


def attend_into(qkv, allowed, mixed, begin=0, end=4):
    def body(t, image, rows):
        blocks = []
        for head in range(qkv.shape[2] // (3 * HEAD_DIM)):
            queries, keys, values, probs = head_probs(qkv, allowed, t, rows, image, head)
            blocks.append(product(probs.astype(jnp.bfloat16), values))
        mixed[t, rows] = jnp.concatenate(blocks, axis=1).astype(mixed.dtype)

    each_image(qkv, body, begin, end)


def attend_back_into(qkv, allowed, grad_mixed, grad_qkv, begin=0, end=4):
    def body(t, image, rows):
        parts = ([], [], [])
        for head in range(qkv.shape[2] // (3 * HEAD_DIM)):
            queries, keys, values, probs = head_probs(qkv, allowed, t, rows, image, head)
            above = grad_mixed[t, rows, head * HEAD_DIM : (head + 1) * HEAD_DIM]
            grad_values = contract_rows(probs.astype(jnp.bfloat16), above)
            grad_probs = back_dot(above, values)
            inner = jnp.sum(probs * grad_probs, axis=-1, keepdims=True)
            grad_scores = (probs * (grad_probs - inner)).astype(jnp.bfloat16)
            scaling = HEAD_DIM ** (-0.5)
            parts[0].append(product(grad_scores, keys) * scaling)
            parts[1].append(contract_rows(grad_scores, queries) * scaling)
            parts[2].append(grad_values)
        grad_qkv[t, rows] = jnp.concatenate(parts[0] + parts[1] + parts[2], axis=1).astype(
            grad_qkv.dtype
        )

    each_image(qkv, body, begin, end)


def each_part(body, begin=0, end=4):
    def step(t, carry):
        body(t)
        return carry

    lax.fori_loop(begin, end, step, 0)


def layer_forward_chunks(
    hidden, allowed, gains, weights, bias, normed, qkv, mixed, hidden_mid, normed_mlp, slope, active,
    hidden_next,
):
    attend_w, merge_w, up_w, down_w = weights

    def start():
        norm_into(hidden, gains[0:1], gains[1:2], normed)

        def project(t):
            qkv[t] = back_dot(normed[...], attend_w[t]).astype(qkv.dtype)

        each_part(project)

    def attention():
        attend_into(qkv, allowed, mixed)

    def merge():
        total = hidden[...]
        for t in range(4):
            total = total + product(mixed[t], merge_w[t])
        hidden_mid[...] = total
        norm_into(hidden_mid, gains[2:3], gains[3:4], normed_mlp)

    def up(t):
        inner = product(normed_mlp[...], up_w[t]) + bias[pl.ds(t, 1)]
        value, rise = gelu_parts(inner)
        active[t] = value.astype(active.dtype)
        slope[t] = rise.astype(slope.dtype)

    def down():
        total = hidden_mid[...] + gains[4:5]
        for t in range(4):
            total = total + product(active[t], down_w[t])
        hidden_next[...] = total

    return [start, attention, merge, lambda: each_part(up), down]


def layer_forward_kernel(*refs):
    hidden, allowed, gains, bias = refs[:4]
    weights = refs[4:8]
    for chunk in layer_forward_chunks(hidden, allowed, gains, weights, bias, *refs[8:]):
        chunk()


def layer_shapes(rows, heads):
    low, full = jnp.bfloat16, jnp.float32
    return [
        jax.ShapeDtypeStruct((rows, D), low),
        jax.ShapeDtypeStruct((4, rows, heads * 3 * HEAD_DIM), low),
        jax.ShapeDtypeStruct((4, rows, heads * HEAD_DIM), low),
        jax.ShapeDtypeStruct((rows, D), full),
        jax.ShapeDtypeStruct((rows, D), low),
        jax.ShapeDtypeStruct((4, rows, D), low),
        jax.ShapeDtypeStruct((4, rows, D), low),
        jax.ShapeDtypeStruct((rows, D), full),
    ]


VMEM_LIMIT = 62 * 1024 * 1024


def layer_forward(hidden, allowed, gains, bias, weights):
    rows, heads = hidden.shape[0], weights[0].shape[1] // (3 * HEAD_DIM)
    vmem = pl.BlockSpec(memory_space=pltpu.VMEM)
    outs = layer_shapes(rows, heads)
    return pl.pallas_call(
        layer_forward_kernel,
        out_shape=outs,
        in_specs=[vmem] * 8,
        out_specs=[vmem] * len(outs),
        compiler_params=pltpu.CompilerParams(vmem_limit_bytes=VMEM_LIMIT),
        name="layer_forward",
    )(hidden, allowed, gains, bias, *weights)


def layer_backward_chunks(
    grad, allowed, gains, weights, stored, low, grad_inner, grad_mixed, grad_qkv, upstream, rows_out,
    attend_grad, merge_grad, up_grad, down_grad,
):
    attend_w, merge_w, up_w, down_w = weights
    hidden, normed, qkv, mixed, hidden_mid, normed_mlp, slope, active = stored

    def start():
        low[...] = grad[...].astype(low.dtype)
        rows_out[4:5] = jnp.sum(low[...].astype(jnp.float32), axis=0, keepdims=True)
        upstream[...] = jnp.zeros_like(upstream)

    def mlp(t):
        inner = (back_dot(low[...], down_w[t]) * slope[t]).astype(jnp.bfloat16)
        grad_inner[...] = inner
        rows_out[pl.ds(8 + t, 1)] = jnp.sum(inner.astype(jnp.float32), axis=0, keepdims=True)
        up_grad[t] = contract_rows(normed_mlp[...], grad_inner[...]).astype(jnp.bfloat16)
        down_grad[t] = contract_rows(active[t], low[...]).astype(jnp.bfloat16)
        upstream[...] += back_dot(grad_inner[...], up_w[t])

    def middle():
        sums = norm_back_into(grad, hidden_mid, upstream, gains[2:3])
        rows_out[2:3], rows_out[3:4] = sums
        low[...] = grad[...].astype(low.dtype)

        def part(t):
            merge_grad[t] = contract_rows(mixed[t], low[...]).astype(jnp.bfloat16)
            grad_mixed[t] = back_dot(low[...], merge_w[t]).astype(jnp.bfloat16)

        each_part(part)

    def attention():
        attend_back_into(qkv, allowed, grad_mixed, grad_qkv)

    def finish():
        upstream[...] = jnp.zeros_like(upstream)

        def part(t):
            attend_grad[t] = contract_rows(grad_qkv[t], normed[...]).astype(jnp.bfloat16)
            upstream[...] += product(grad_qkv[t], attend_w[t])

        each_part(part)
        sums = norm_back_into(grad, hidden, upstream, gains[0:1])
        rows_out[0:1], rows_out[1:2] = sums

    return [start, lambda: each_part(mlp), middle, attention, finish]


def layer_backward_kernel(*refs):
    grad_in, allowed, gains = refs[:3]
    weights, stored = refs[3:7], refs[7:15]
    grad, rows_out, attend_grad, merge_grad, up_grad, down_grad = refs[15:21]
    low, grad_inner, grad_mixed, grad_qkv, upstream = refs[21:]
    grad[...] = grad_in[...]
    rows_out[...] = jnp.zeros_like(rows_out)
    for chunk in layer_backward_chunks(
        grad, allowed, gains, weights, stored, low, grad_inner, grad_mixed, grad_qkv, upstream,
        rows_out, attend_grad, merge_grad, up_grad, down_grad,
    ):
        chunk()


def layer_backward(grad, allowed, gains, weights, stored):
    rows, heads = grad.shape[0], weights[0].shape[1] // (3 * HEAD_DIM)
    vmem = pl.BlockSpec(memory_space=pltpu.VMEM)
    low, full = jnp.bfloat16, jnp.float32
    outs = [jax.ShapeDtypeStruct((rows, D), full), jax.ShapeDtypeStruct((16, D), full)]
    outs += [jax.ShapeDtypeStruct(weight.shape, low) for weight in weights]
    return pl.pallas_call(
        layer_backward_kernel,
        out_shape=outs,
        in_specs=[vmem] * 15,
        out_specs=[vmem] * len(outs),
        scratch_shapes=[
            pltpu.VMEM((rows, D), low),
            pltpu.VMEM((rows, D), low),
            pltpu.VMEM((4, rows, heads * HEAD_DIM), low),
            pltpu.VMEM((4, rows, heads * 3 * HEAD_DIM), low),
            pltpu.VMEM((rows, D), full),
        ],
        compiler_params=pltpu.CompilerParams(vmem_limit_bytes=VMEM_LIMIT),
        name="layer_backward",
    )(grad, allowed, gains, *weights, *stored)


ATTEND_GROUP, MLP_GROUP, SMALL_GROUP, LATE_GROUP = (0, 1), (2, 3), (4,), (5, 6)
OF_UNIT = (0, 1, 2, 3, 4, 0, 1)
POSITION_ROW, EMBED_ROW, LAYER_ROW, IMAGE_ROW, OTHER_ROW, SMALL_ROWS = 0, 256, 304, 320, 384, 512


def layer_back_kernel(last, *refs):
    grad_in, hidden, hidden_mid, normed, normed_mlp, slope, active, up_w, down_w = refs[:9]
    qkv, mixed, allowed, gains, attend_w, merge_w = refs[9:15]
    refs = refs[15:]
    if last:
        late, extra, patches = refs[:2], refs[2], refs[3]
        refs = refs[4:]
    grad, rows_out = refs[:2]
    refs = refs[2:]
    if last:
        outs = [refs[unit] for unit in range(7)]
        refs = refs[7:]
        units = 5
    else:
        outs = [None, None, *refs[:2]]
        raw = refs[2:4]
        refs = refs[4:]
        units = 4
    groups = []
    for entry in range(6):
        found = list(refs[:units])
        refs = refs[units:]
        if last:
            found += [found[0], found[1]]
        groups.append(found)
    grads, got_core, got_one, got_two, got_z, result = groups
    if last:
        got_z[5:], result[5:], small_v = refs[:2], refs[2:4], refs[4]
        refs = refs[5:]
    low, grad_inner, grad_mixed, grad_qkv, upstream, values, rounded = refs[:7]
    slopes, actives, ups, downs = refs[7:11]
    send_sems, step_sems, z_sems, spread_sems, core_sems, spare, load_sems, stream_sems = refs[11:19]
    total_sems = refs[19]
    if last:
        all_sems = refs[20]
    y, x, core, z = place()
    at_x = device_at(y, 1 - x, core, z)
    at_y = device_at(1 - y, x, core, z)
    at_core = device_at(y, x, 1 - core, z)

    def load(source, target, sem):
        copy = pltpu.make_async_copy(source, target, load_sems.at[sem])
        copy.start()
        return copy

    def stream(step):
        t, slot = ITEM_ORDER[step], step % 2
        pairs = ((down_w, downs), (slope, slopes), (active, actives), (up_w, ups))
        copies = []
        for entry, (source, target) in enumerate(pairs):
            copy = pltpu.make_async_copy(
                source.at[t], target.at[slot], stream_sems.at[slot, entry]
            )
            copy.start()
            copies.append(copy)
        return copies

    first_loads = [load(grad_in, grad, 0)]
    streams = [stream(0), stream(1)]
    first_loads += [load(normed_mlp, rounded, 1), load(hidden_mid, values, 2)]
    greet(partners())
    copies = Copies(send_sems)
    sent_of = {unit: [] for unit in range(len(grads))}
    conditional_of = {unit: [] for unit in range(len(grads))}

    def send_own(unit, *args):
        sent_of[unit].append(copies.send(*args))

    def put(unit, t, value):
        target = grads[unit]
        target[t] = value.reshape(target.shape[1:]).astype(target.dtype)

    def share(group, step):
        t = ITEM_ORDER[step]
        for unit in group:
            source = grads[unit] if unit < 5 else late[unit - 5]
            copies.send(
                source.at[t, :, :, :, 1 - core],
                got_core[unit].at[t],
                step_sems.at[unit, 0, t],
                at_core,
            )

    def core_sum(group, step):
        t = ITEM_ORDER[step]
        for unit in group:
            mine, other = grads[unit], got_core[unit]
            wait_arrival(other.at[t], step_sems.at[unit, 0, t], spare.at[0], at_core)

            for spot in ((0, 0), (0, 1), (1, 0), (1, 1)):
                where = (t, slice(None), *spot)
                add_slab(mine.at[(*where, core)], other.at[where])
            if t < 2:
                source, device = mine.at[t, :, :, 1 - x, core], at_x
            else:
                source, device = mine.at[t, :, 1 - y, :, core], at_y
            send_own(unit, source, got_one[unit].at[t], step_sems.at[unit, 1, t], device, False)

    def one(group, step):
        t = ITEM_ORDER[step]
        for unit in group:
            mine, other = grads[unit], got_one[unit]
            wait_arrival(
                other.at[t], step_sems.at[unit, 1, t], spare.at[0], at_x if t < 2 else at_y
            )

            for entry in range(2):
                spot = (entry, x, core) if t < 2 else (y, entry, core)
                add_slab(mine.at[(t, slice(None), *spot)], other.at[t, :, entry])
            if t < 2:
                source, device = mine.at[t, :, 1 - y, x, core], at_y
            else:
                source, device = mine.at[t, :, y, 1 - x, core], at_x
            send_own(unit, source, got_two[unit].at[t], step_sems.at[unit, 2, t], device, False)

    def two(group, step):
        t = ITEM_ORDER[step]
        for unit in group:
            mine, other = grads[unit], got_two[unit]
            wait_arrival(
                other.at[t], step_sems.at[unit, 2, t], spare.at[0], at_y if t < 2 else at_x
            )

            add_slab(mine.at[t, :, y, x, core], other.at[t])
            copy = pltpu.make_async_remote_copy(
                src_ref=mine.at[t, :, y, x, core],
                dst_ref=got_z[unit].at[z],
                send_sem=send_sems.at[copies.count],
                recv_sem=z_sems.at[unit, z],
                device_id=device_at(y, x, core, t),
                device_id_type=MESH,
            )
            copies.count += 1

            @pl.when(z != t)
            def _():
                copy.start()

            conditional_of[unit].append((t, copy))

    def place_of(unit):
        return outs[unit].at[z] if unit in SMALL_GROUP else outs[unit]

    def spot_of(unit, where):
        return place_of(unit).at[(slice(None), *where)]

    def half_spot(unit, where, side):
        spot = place_of(unit)
        count = spot.shape[0]
        if count > 1:
            return spot.at[(halves(count)[side], *where)]
        return spot.at[(slice(None), *where, halves(spot.shape[4])[side])]

    def over_z(group):
        for unit in group:
            mine, other, total = grads[unit], got_z[unit], result[unit]
            for bits in SWAP_TENSOR:
                t = flipped(z, bits)
                wait_arrival(
                    other.at[t], z_sems.at[unit, t], spare.at[0], device_at(y, x, core, t)
                )

            value = mine[z, :, y, x, core].astype(jnp.float32)
            for bits in SWAP_TENSOR:
                value = value + other[flipped(z, bits)].astype(jnp.float32)
            total[...] = value.astype(total.dtype)
            spot = spot_of(unit, (y, x, core))
            pltpu.make_async_copy(total, spot, total_sems.at[unit]).start()
            copies.send(total, spot, spread_sems.at[unit, 0], at_x)
            copies.send(total, spot, spread_sems.at[unit, 1], at_y)
            copies.send(total, spot, core_sems.at[unit, 0], at_core)

    def spread(group):
        for unit in group:
            spot = spot_of(unit, (y, 1 - x, core))
            wait_arrival(spot, spread_sems.at[unit, 0], spare.at[0], at_x)
            first = half_spot(unit, (y, 1 - x, core), 0)
            copies.send(first, first, spread_sems.at[unit, 2], at_y)
            copies.send(spot, spot, core_sems.at[unit, 1], at_core)
            spot = spot_of(unit, (1 - y, x, core))
            wait_arrival(spot, spread_sems.at[unit, 1], spare.at[0], at_y)
            second = half_spot(unit, (1 - y, x, core), 1)
            copies.send(second, second, spread_sems.at[unit, 3], at_x)
            copies.send(spot, spot, core_sems.at[unit, 2], at_core)

    def corner(group):
        for unit in group:
            where = (1 - y, 1 - x, core)
            wait_arrival(half_spot(unit, where, 0), spread_sems.at[unit, 2], spare.at[0], at_y)
            wait_arrival(half_spot(unit, where, 1), spread_sems.at[unit, 3], spare.at[0], at_x)
            spot = spot_of(unit, where)
            copies.send(spot, spot, core_sems.at[unit, 3], at_core)

    def finish(group):
        for unit in group:
            pltpu.make_async_copy(
                result[unit], spot_of(unit, (y, x, core)), total_sems.at[unit]
            ).wait()
            for entry, where in enumerate(((y, x), (y, 1 - x), (1 - y, x), (1 - y, 1 - x))):
                if entry == 0 and unit in settled:
                    continue
                spot = spot_of(unit, (*where, 1 - core))
                wait_arrival(spot, core_sems.at[unit, entry], spare.at[0], at_core)

    def settle(group):
        for unit in group:
            for copy in sent_of.pop(unit):
                copy.wait_send()
            for t, copy in conditional_of.pop(unit):

                @pl.when(z != t)
                def _(copy=copy):
                    copy.wait_send()

            wait_arrival(
                spot_of(unit, (y, x, 1 - core)), core_sems.at[unit, 0], spare.at[0], at_core
            )
            settled.append(unit)

    def mlp(step):
        t, slot = ITEM_ORDER[step], step % 2
        for copy in streams[step]:
            copy.wait()
        inner = (back_dot(low[...], downs[slot]) * slopes[slot]).astype(jnp.bfloat16)
        grad_inner[...] = inner
        rows_out[8 + t : 9 + t] = jnp.sum(inner.astype(jnp.float32), axis=0, keepdims=True)
        put(2, t, contract_rows(rounded[...], grad_inner[...]))
        put(3, t, contract_rows(actives[slot], low[...]))
        upstream[...] += back_dot(grad_inner[...], ups[slot])
        if step < 2:
            streams.append(stream(step + 2))
        share(MLP_GROUP, step)

    def project(step):
        t = ITEM_ORDER[step]
        put(0, t, contract_rows(grad_qkv[t], rounded[...]))
        put(1, t, contract_rows(mixed[t], low[...]))
        upstream[...] += product(grad_qkv[t], attend_w[t])
        if last:
            share(ATTEND_GROUP, step)
            return
        for unit in ATTEND_GROUP:
            copy = pltpu.make_async_copy(
                grads[unit].at[t], raw[unit].at[t], step_sems.at[unit, 0, t]
            )
            copy.start()
            left.append(copy)

    def collect_small():
        rows_out[5:6] = jnp.sum(grad[...], axis=0, keepdims=True)
        small_v[LAYER_ROW : LAYER_ROW + 16] = rows_out[...]
        images = grad.shape[0] // P_SIZE
        total = grad[:P_SIZE]
        for image in range(1, images):
            total = total + grad[image * P_SIZE : (image + 1) * P_SIZE]
        small_v[POSITION_ROW : POSITION_ROW + P_SIZE] = total
        first = grad[...].astype(jnp.bfloat16)
        second = (grad[...] - first.astype(jnp.float32)).astype(jnp.bfloat16)
        small_v[EMBED_ROW : EMBED_ROW + PV] = contract_rows(patches[...], first) + contract_rows(
            patches[...], second
        )
        device_index = lax.axis_index("batch") * 4 + z
        for image in range(images):
            rows = grad[image * P_SIZE : (image + 1) * P_SIZE]
            spot = IMAGE_ROW + device_index * images + image
            small_v[pl.ds(spot, 1)] = jnp.sum(rows, axis=0, keepdims=True)
        for t in range(4):
            part = small_v.shape[0] // 4
            put(4, t, small_v[t * part : (t + 1) * part])

    left = []
    settled = []
    rows_out[...] = jnp.zeros_like(rows_out)
    if last:
        for step in range(4):
            share(LATE_GROUP, step)
        late_loads = [load(late[entry], grads[entry], 8 + entry) for entry in range(2)]
        late_loads.append(load(extra, small_v, 7))
    for copy in first_loads:
        copy.wait()
    low[...] = grad[...].astype(low.dtype)
    rows_out[4:5] = jnp.sum(low[...].astype(jnp.float32), axis=0, keepdims=True)
    upstream[...] = jnp.zeros_like(upstream)
    mlp(0)
    if last:
        for copy in late_loads:
            copy.wait()
        core_sum(LATE_GROUP, 0)
        core_sum(LATE_GROUP, 1)
    mlp(1)
    core_sum(MLP_GROUP, 0)
    if last:
        core_sum(LATE_GROUP, 2)
        core_sum(LATE_GROUP, 3)
    mlp(2)
    core_sum(MLP_GROUP, 1)
    if last:
        one(LATE_GROUP, 0)
        one(LATE_GROUP, 1)
    mlp(3)
    core_sum(MLP_GROUP, 2)
    if last:
        one(LATE_GROUP, 2)
        one(LATE_GROUP, 3)
        two(LATE_GROUP, 0)
        two(LATE_GROUP, 1)
    rows_out[2:3], rows_out[3:4] = norm_back_into(grad, values, upstream, gains[2:3])
    later_loads = [load(hidden, values, 2), load(normed, rounded, 1)]
    low[...] = grad[...].astype(low.dtype)
    for t in range(4):
        grad_mixed[t] = back_dot(low[...], merge_w[t]).astype(grad_mixed.dtype)
    core_sum(MLP_GROUP, 3)
    one(MLP_GROUP, 0)
    if last:
        two(LATE_GROUP, 2)
        two(LATE_GROUP, 3)
    attend_back_into(qkv, allowed, grad_mixed, grad_qkv, 0, 2)
    one(MLP_GROUP, 1)
    two(MLP_GROUP, 0)
    if last:
        over_z(LATE_GROUP)
    attend_back_into(qkv, allowed, grad_mixed, grad_qkv, 2, 4)
    one(MLP_GROUP, 2)
    two(MLP_GROUP, 1)
    if last:
        spread(LATE_GROUP)
        settle(LATE_GROUP)
    upstream[...] = jnp.zeros_like(upstream)
    for copy in later_loads:
        copy.wait()
    project(0)
    one(MLP_GROUP, 3)
    project(1)
    if last:
        core_sum(ATTEND_GROUP, 0)
    two(MLP_GROUP, 2)
    project(2)
    if last:
        core_sum(ATTEND_GROUP, 1)
    two(MLP_GROUP, 3)
    project(3)
    if last:
        core_sum(ATTEND_GROUP, 2)
        one(ATTEND_GROUP, 0)
    rows_out[0:1], rows_out[1:2] = norm_back_into(grad, values, upstream, gains[0:1])
    over_z(MLP_GROUP)
    if last:
        collect_small()
        for step in range(4):
            share(SMALL_GROUP, step)
        core_sum(ATTEND_GROUP, 3)
        one(ATTEND_GROUP, 1)
        corner(LATE_GROUP)
        two(ATTEND_GROUP, 0)
        for step in range(4):
            core_sum(SMALL_GROUP, step)
        one(ATTEND_GROUP, 2)
        two(ATTEND_GROUP, 1)
        spread(MLP_GROUP)
        one(ATTEND_GROUP, 3)
        two(ATTEND_GROUP, 2)
        for step in range(4):
            one(SMALL_GROUP, step)
        two(ATTEND_GROUP, 3)
        corner(MLP_GROUP)
        for step in range(4):
            two(SMALL_GROUP, step)
        over_z(ATTEND_GROUP)
        over_z(SMALL_GROUP)
        spread(ATTEND_GROUP)
        spread(SMALL_GROUP)
        corner(ATTEND_GROUP)
        corner(SMALL_GROUP)
        finish(SMALL_GROUP)
        (unit,) = SMALL_GROUP
        for bits in SWAP_TENSOR:
            at_t = device_at(y, x, core, flipped(z, bits))
            copies.send(outs[unit].at[z], outs[unit].at[z], all_sems.at[bits], at_t)
        finish(LATE_GROUP)
        finish(MLP_GROUP)
        finish(ATTEND_GROUP)
        for bits in SWAP_TENSOR:
            t = flipped(z, bits)
            wait_arrival(
                outs[unit].at[t], all_sems.at[bits], spare.at[0], device_at(y, x, core, t)
            )
    else:
        spread(MLP_GROUP)
        corner(MLP_GROUP)
        finish(MLP_GROUP)
    for copy in left:
        copy.wait()
    copies.finish()
    for unit in sent_of:
        for copy in sent_of[unit]:
            copy.wait_send()
        for t, copy in conditional_of[unit]:

            @pl.when(z != t)
            def _(copy=copy):
                copy.wait_send()


def owner_shape(weight):
    count = 1 if weight.shape[1] == D else weight.shape[1] // 64
    return (count, 2, 2, 2, weight.shape[1] // (8 * count), D)


def layer_back_reduce(layer_index, grad, allowed, gains, weights, stored, late=(), extra=None, patches=None):
    hidden, normed, qkv, mixed, hidden_mid, normed_mlp, slope, active = stored
    attend_w, merge_w, up_w, down_w = weights
    last = layer_index == 0
    rows, heads = grad.shape[0], attend_w.shape[1] // (3 * HEAD_DIM)
    low, full = jnp.bfloat16, jnp.float32
    vmem = pl.BlockSpec(memory_space=pltpu.VMEM)
    anywhere = pl.BlockSpec(memory_space=pl.ANY)
    shapes = [owner_shape(weight) for weight in weights]
    if last:
        shapes.append((1, 2, 2, 2, SMALL_ROWS // 32, D))
    scratch = []
    for lead in ((4, 2, 2, 2), (4, 2, 2), (4, 2), (4,), (4,), ()):
        for shape in shapes:
            whole = lead[:1] + shape[:1] + lead[1:] + shape[4:]
            scratch.append(pltpu.VMEM(whole, low))
    count = 7 if last else 4
    if last:
        scratch += [pltpu.VMEM((4, *shape[:1], *shape[4:]), low) for shape in shapes[:2]]
        scratch += [pltpu.VMEM(shape[:1] + shape[4:], low) for shape in shapes[:2]]
        scratch.append(pltpu.VMEM((SMALL_ROWS, D), full))
    dma = pltpu.SemaphoreType.DMA
    scratch += [
        pltpu.VMEM((rows, D), low),
        pltpu.VMEM((rows, D), low),
        pltpu.VMEM((4, rows, heads * HEAD_DIM), low),
        pltpu.VMEM((4, rows, heads * 3 * HEAD_DIM), low),
        pltpu.VMEM((rows, D), full),
        pltpu.VMEM((rows, D), full),
        pltpu.VMEM((rows, D), low),
        pltpu.VMEM((2, rows, D), slope.dtype),
        pltpu.VMEM((2, rows, D), low),
        pltpu.VMEM((2, D, D), low),
        pltpu.VMEM((2, D, D), low),
        dma((count * 24 + 3,)),
        dma((count, 3, 4)),
        dma((count, 4)),
        dma((count, 4)),
        dma((count, 4)),
        dma((1,)),
        dma((10,)),
        dma((2, 4)),
        dma((count,)),
    ]
    if last:
        scratch.append(dma((4,)))
    outs = [jax.ShapeDtypeStruct((rows, D), full), jax.ShapeDtypeStruct((16, D), full)]
    sums = [jax.ShapeDtypeStruct(shape, low) for shape in shapes]
    parts = [jax.ShapeDtypeStruct((4, *shape), low) for shape in shapes]
    if last:
        outs += sums[:4] + [parts[4]] + sums[:2]
    else:
        outs += sums[2:4] + parts[:2]
    inputs = [grad, hidden, hidden_mid, normed, normed_mlp, slope, active, up_w, down_w]
    specs = [anywhere] * 9 + [vmem] * 6
    inputs += [qkv, mixed, allowed, gains, attend_w, merge_w]
    if last:
        inputs += [*late, extra, patches]
        specs += [anywhere] * 3 + [vmem]
    return pl.pallas_call(
        functools.partial(layer_back_kernel, last),
        out_shape=outs,
        in_specs=specs,
        out_specs=[vmem] * 2 + [anywhere] * (len(outs) - 2),
        scratch_shapes=scratch,
        compiler_params=pltpu.CompilerParams(
            collective_id=2 + layer_index, has_side_effects=True, vmem_limit_bytes=BACK_LIMIT
        ),
        name="layer_back_reduce",
    )(*inputs)


BACK_LIMIT = 66 * 1000 * 1000


def shards(
    patches,
    valid_mask,
    class_ids,
    embed_weight,
    embed_bias,
    position_table,
    class_table,
    attn_gain,
    attn_offset,
    attend_weight,
    merge_weight,
    mlp_gain,
    mlp_offset,
    up_weight,
    up_bias,
    down_weight,
    down_bias,
    final_gain,
    final_offset,
    head_weight,
    head_bias,
    latent_cot,
    logdet_cot,
):
    shard_count = patches.shape[0]
    local_images = shard_count // P_SIZE
    tensor_index = lax.axis_index("tensor")
    tensor_count = lax.axis_size("tensor")
    batch_count = lax.axis_size("batch")
    device_index = lax.axis_index("batch") * tensor_count + tensor_index
    device_count = batch_count * tensor_count
    patch_values = patches.astype(jnp.float32)
    local_valid = lax.dynamic_slice_in_dim(valid_mask, tensor_index * shard_count, shard_count, 0)
    live_mask = local_valid.astype(jnp.float32)[:, None]
    allowed = build_allowed(local_valid, P_SIZE).astype(jnp.float32)
    embed_full = embed_weight.astype(jnp.float32)
    shards = []
    for layer_index in range(NL):
        shards.append(jnp.swapaxes(attend_weight[layer_index], 1, 2).reshape(-1, D))
        shards.append(merge_weight[layer_index])
        shards.append(up_weight[layer_index])
        shards.append(down_weight[layer_index])
    gains = [
        jnp.stack(
            [attn_gain[layer_index], attn_offset[layer_index], mlp_gain[layer_index]]
            + [mlp_offset[layer_index], down_bias[layer_index]]
        )
        for layer_index in range(NL)
    ]
    choose = class_ids[:, None] == lax.broadcasted_iota(jnp.int32, (local_images, CLASSES), 1)
    class_rows = product(choose.astype(jnp.bfloat16), class_table)
    embedding = (patches, embed_weight, embed_bias[None], position_table, class_rows)
    valid_rows = local_valid.astype(jnp.float32).reshape(local_images, P_SIZE)
    wholes, stored, hidden = forward_layers(
        shards, up_bias, embedding, valid_rows, allowed, gains
    )
    final = layer_norm(hidden, final_gain, final_offset)
    final_low = final.astype(jnp.bfloat16)
    head_out = product(final_low, head_weight) + head_bias
    position = lax.broadcasted_iota(jnp.int32, (shard_count, 1), 0) % P_SIZE
    starts = position == 0
    previous = jnp.concatenate([jnp.zeros((1, 2 * PV), jnp.float32), head_out[:-1]], axis=0)
    previous = jnp.where(starts, 0.0, previous)
    shift_part = previous[:, :PV]
    log_scale = previous[:, PV:]
    scale_factor = jnp.exp(-log_scale)
    latents = (
        live_mask * (patch_values - shift_part) * scale_factor + (1.0 - live_mask) * patch_values
    )
    log_det = -jnp.sum((live_mask * log_scale).reshape(local_images, P_SIZE * PV), axis=1)
    image_cot = jnp.repeat(logdet_cot, P_SIZE)[:, None]
    direct_grad = latent_cot * (live_mask * scale_factor + (1.0 - live_mask))
    grad_shift = -live_mask * latent_cot * scale_factor
    grad_scale = -live_mask * (latent_cot * (patch_values - shift_part) * scale_factor + image_cot)
    grad_previous = jnp.where(starts, 0.0, jnp.concatenate([grad_shift, grad_scale], axis=1))
    grad_head = jnp.concatenate([grad_previous[1:], jnp.zeros((1, 2 * PV), jnp.float32)], axis=0)
    grad_head_low = grad_head.astype(jnp.bfloat16)
    head_weight_grad = contract_rows(grad_head_low, final_low)
    head_bias_grad = jnp.sum(grad_head_low.astype(jnp.float32), axis=0)
    grad_final = back_dot(grad_head_low, head_weight)
    grad_hidden, final_gain_grad, final_offset_grad = norm_backward(
        hidden, final_gain, final_offset, grad_final
    )
    image_count = device_count * local_images
    image_index = device_index * local_images
    id_rows = jnp.stack([class_ids // 32, class_ids % 32]).astype(jnp.float32)
    id_rows = lax.dynamic_update_slice(jnp.zeros((2, D), jnp.float32), id_rows, (0, image_index))
    other = [
        head_weight_grad,
        final_gain_grad[None],
        final_offset_grad[None],
        jnp.pad(head_bias_grad, (0, D - 2 * PV))[None],
        id_rows,
    ]
    if fast_mesh():
        grad_hidden, layer_rows, up_sum, down_sum, *late = layer_back_reduce(
            1, grad_hidden, allowed, gains[1], wholes[4:], stored[1]
        )
        other = jnp.concatenate([jnp.zeros((OTHER_ROW, D), jnp.float32), layer_rows] + other)
        other = jnp.pad(other, ((0, SMALL_ROWS - other.shape[0]), (0, 0)))
        grad_hidden, layer_rows, *sums = layer_back_reduce(
            0, grad_hidden, allowed, gains[0], wholes[:4], stored[0], late, other, patches
        )
        small_sum = sums[4].reshape(-1, D)
        sums = [entry.reshape(-1, D) for entry in sums[:4] + sums[5:] + [up_sum, down_sum]]
    else:
        rows_of = {}
        split_list = [None] * NL
        for layer_index in reversed(range(NL)):
            weights = wholes[4 * layer_index : 4 * layer_index + 4]
            grad_hidden, rows_of[layer_index], *split_list[layer_index] = layer_backward(
                grad_hidden, allowed, gains[layer_index], weights, stored[layer_index]
            )
        per_image = grad_hidden.reshape(local_images, P_SIZE, D)
        image_rows = lax.dynamic_update_slice_in_dim(
            jnp.zeros((image_count, D), jnp.float32), jnp.sum(per_image, axis=1), image_index, 0
        )
        first_rows = lax.dynamic_update_slice_in_dim(
            rows_of[0], jnp.sum(grad_hidden, axis=0)[None], 5, 0
        )
        small = [
            jnp.sum(per_image, axis=0),
            precise_rows(patch_values, grad_hidden),
            first_rows,
            image_rows,
            rows_of[1],
        ]
        joined = jnp.concatenate(small + other, axis=0)
        joined = jnp.pad(joined, ((0, -joined.shape[0] % (8 * device_count)), (0, 0)))
        grads = [grad.reshape(-1, D) for grad in split_list[0] + split_list[1]]
        sums = reduce_rows([to_batch_major(grad) for grad in grads] + [split_blocks(joined)])
        small_sum = lax.all_gather(sums[-1], "tensor", axis=1).reshape(-1, D)
        sums = [entry.reshape(-1, D) for entry in sums[:-1]]
    split_list = [None] * NL
    for layer_index in range(NL):
        attend_sum, merge_sum, up_sum, down_sum = sums[4 * layer_index : 4 * layer_index + 4]
        split_list[layer_index] = (
            jnp.swapaxes(attend_sum.reshape(3, -1, D), 1, 2).astype(jnp.float32),
            merge_sum.astype(jnp.float32),
            up_sum.astype(jnp.float32),
            down_sum.astype(jnp.float32),
        )
    patches_grad = direct_grad + lax.dot_general(
        grad_hidden,
        embed_full,
        (((1,), (1,)), ((), ())),
        precision=HIGHEST,
        preferred_element_type=jnp.float32,
    )
    small_sum = small_sum.astype(jnp.float32)
    other_row = IMAGE_ROW + image_count
    row = other_row + 16 + 2 * PV
    id_sums = small_sum[row + 3 : row + 5, :image_count].astype(jnp.int32)
    all_ids = id_sums[0] * 32 + id_sums[1]
    choose_all = all_ids[:, None] == lax.broadcasted_iota(
        jnp.int32, (image_count, CLASSES), 1
    )
    class_grad = precise_rows(
        choose_all.astype(jnp.float32), small_sum[IMAGE_ROW:other_row]
    )
    layer_rows = [small_sum[LAYER_ROW : LAYER_ROW + 16], small_sum[other_row : other_row + 16]]
    own_bias = [lax.dynamic_slice_in_dim(entry, 8 + tensor_index, 1, 0) for entry in layer_rows]
    split_stack = [jnp.stack([entry[member] for entry in split_list]) for member in range(4)]
    shared_stack = [
        jnp.stack([entry[member] for entry in layer_rows]) for member in range(5)
    ]
    return (
        latents,
        log_det,
        patches_grad,
        small_sum[EMBED_ROW : EMBED_ROW + PV],
        layer_rows[0][5],
        small_sum[:P_SIZE],
        class_grad,
        shared_stack[0],
        shared_stack[1],
        split_stack[0],
        split_stack[1],
        shared_stack[2],
        shared_stack[3],
        split_stack[2],
        jnp.concatenate(own_bias, axis=0),
        split_stack[3],
        shared_stack[4],
        small_sum[row],
        small_sum[row + 1],
        jnp.swapaxes(small_sum[other_row + 16 : row], 0, 1),
        small_sum[row + 2, : 2 * PV],
    )


def solution(mesh):
    return jax.shard_map(
        shards,
        mesh=mesh,
        in_specs=(
            P(("batch", "tensor"), None),
            P("batch"),
            P(("batch", "tensor")),
            P(),
            P(),
            P(),
            P(),
            P(),
            P(),
            P(None, None, None, "tensor"),
            P(None, "tensor", None),
            P(),
            P(),
            P(None, None, "tensor"),
            P(None, "tensor"),
            P(None, "tensor", None),
            P(),
            P(),
            P(),
            P(),
            P(),
            P(("batch", "tensor"), None),
            P(("batch", "tensor")),
        ),
        out_specs=(
            P(("batch", "tensor"), None),
            P(("batch", "tensor")),
            P(("batch", "tensor"), None),
            P(),
            P(),
            P(),
            P(),
            P(),
            P(),
            P(None, None, None, "tensor"),
            P(None, "tensor", None),
            P(),
            P(),
            P(None, None, "tensor"),
            P(None, "tensor"),
            P(None, "tensor", None),
            P(),
            P(),
            P(),
            P(),
            P(),
        ),
        check_vma=False,
    )
```

```python
import functools

import jax
import jax.numpy as jnp
from jax import lax
from jax.experimental import pallas as pl
from jax.experimental.pallas import tpu as pltpu
from jax.sharding import PartitionSpec as P

D = 768
HEAD_DIM = 64
P_SIZE = 256
PV = 48
CLASSES = 1000
NL = 2


EPSILON = 1e-05
NEGATIVE = -1000000000.0
HIGHEST = lax.Precision.HIGHEST


def layer_norm(values, norm_gain, norm_offset):
    center = values - jnp.mean(values, axis=-1, keepdims=True)
    spread = jnp.mean(center * center, axis=-1, keepdims=True)
    return center * lax.rsqrt(spread + EPSILON) * norm_gain + norm_offset


def norm_backward(values, norm_gain, norm_offset, upstream):
    outputs, pullback = jax.vjp(layer_norm, values, norm_gain, norm_offset)
    return pullback(upstream)


def gelu_parts(values):
    share = 0.5 + 0.5 * lax.erf(values * (0.5**0.5))
    slope = share + values * (jnp.exp(-0.5 * values * values) * ((0.5 / jnp.pi) ** 0.5))
    return (values * share, slope)


def product(former, latter):
    return jnp.dot(former, latter, preferred_element_type=jnp.float32)


def contract_rows(former, latter):
    return lax.dot_general(
        former, latter, (((0,), (0,)), ((), ())), preferred_element_type=jnp.float32
    )


def precise_rows(former, latter):
    return lax.dot_general(
        former,
        latter,
        (((0,), (0,)), ((), ())),
        precision=HIGHEST,
        preferred_element_type=jnp.float32,
    )


def build_allowed(mask_rows, span):
    row_index = lax.broadcasted_iota(jnp.int32, (span, span), 0)
    col_index = lax.broadcasted_iota(jnp.int32, (span, span), 1)
    causal = (row_index // P_SIZE == col_index // P_SIZE) & (col_index <= row_index)
    key_valid = mask_rows.reshape(mask_rows.shape[0] // span, 1, span) > 0
    return causal[None] & (key_valid | (row_index == col_index)[None])


def gather_rows(parts):
    batch_count = lax.axis_size("batch")
    batch_index = lax.axis_index("batch")
    pieces = []
    for part in parts:
        rows = part.shape[0] // batch_count
        pieces.append(lax.dynamic_slice_in_dim(part, batch_index * rows, rows, 0))
    piece = jnp.concatenate(pieces, axis=0)
    group = lax.all_gather(piece, "tensor", axis=0)
    whole = lax.all_gather(group, "batch", axis=0)
    results = []
    begin = 0
    for entry in pieces:
        results.append(whole[:, :, begin : begin + entry.shape[0]])
        begin += entry.shape[0]
    return results


def reduce_rows(parts):
    joined = jnp.concatenate([part.astype(jnp.bfloat16) for part in parts], axis=2)
    over_batch = lax.psum_scatter(joined, "batch", scatter_dimension=0)
    own = lax.psum_scatter(over_batch, "tensor", scatter_dimension=0)
    whole = lax.all_gather(own, "batch", axis=0)
    results = []
    begin = 0
    for part in parts:
        results.append(whole[:, begin : begin + part.shape[2]])
        begin += part.shape[2]
    return results


def to_tensor_major(blocks):
    return jnp.swapaxes(blocks, 0, 1).reshape(-1, blocks.shape[-1])


def to_batch_major(rows):
    batch_count = lax.axis_size("batch")
    tensor_count = lax.axis_size("tensor")
    return jnp.swapaxes(rows.reshape(tensor_count, batch_count, -1, rows.shape[-1]), 0, 1)


def split_blocks(rows):
    batch_count = lax.axis_size("batch")
    tensor_count = lax.axis_size("tensor")
    return rows.reshape(batch_count, tensor_count, -1, rows.shape[-1])


MESH = pl.DeviceIdType.MESH
SWAP_TENSOR = (1, 2, 3)


def place():
    batch_index = lax.axis_index("batch")
    tensor_index = lax.axis_index("tensor")
    return (batch_index // 4, batch_index // 2 % 2, batch_index % 2, tensor_index)


def device_at(y, x, core, z):
    return (y * 4 + x * 2 + core, z)


def flipped(index, bits):
    high, low = index // 2, index % 2
    if bits & 2:
        high = 1 - high
    if bits & 1:
        low = 1 - low
    return high * 2 + low


def greet(devices):
    barrier = pltpu.get_barrier_semaphore()
    for device in devices:
        pl.semaphore_signal(barrier, inc=1, device_id=device, device_id_type=MESH)
    pl.semaphore_wait(barrier, len(devices))


def partners():
    y, x, core, z = place()
    devices = [device_at(y, x, core, flipped(z, bits)) for bits in SWAP_TENSOR]
    devices.append(device_at(y, 1 - x, core, z))
    devices.append(device_at(1 - y, x, core, z))
    devices.append(device_at(y, x, 1 - core, z))
    return devices


def halves(count):
    return (slice(0, (count + 1) // 2), slice((count + 1) // 2, count))


class Copies:
    def __init__(self, send_sems):
        self.send_sems = send_sems
        self.count = 0
        self.sent = []

    def send(self, source, target, recv_sem, device, keep=True):
        copy = pltpu.make_async_remote_copy(
            src_ref=source,
            dst_ref=target,
            send_sem=self.send_sems.at[self.count],
            recv_sem=recv_sem,
            device_id=device,
            device_id_type=MESH,
        )
        self.count += 1
        copy.start()
        if keep:
            self.sent.append(copy)
        return copy

    def finish(self):
        for copy in self.sent:
            copy.wait_send()


def wait_arrival(target, recv_sem, send_sem, device):
    pltpu.make_async_remote_copy(
        src_ref=target,
        dst_ref=target,
        send_sem=send_sem,
        recv_sem=recv_sem,
        device_id=device,
        device_id_type=MESH,
    ).wait_recv()


def spread_piece(ref, lead, b):
    if len(ref.shape) == len(lead) + 4:
        return ref.at[(*lead, slice(None), b)]
    return ref.at[(*lead, b)]


def half_piece(ref, lead, b, side):
    if len(ref.shape) == len(lead) + 4:
        return ref.at[(*lead, halves(ref.shape[len(lead)])[side], b)]
    return ref.at[(*lead, b, halves(ref.shape[len(lead) + 1])[side])]


WEIGHT_GROUPS = ((0, 1), (2, 3), (4, 5), (6,), (7,))


def forward_kernel(*refs):
    units = 4 * NL
    shards = refs[:units]
    bias, patches, embed_w, embed_b, table, class_rows, valid = refs[units : units + 7]
    gains = refs[units + 7 : units + 7 + NL]
    outs = refs[units + 7 + NL :]
    fulls, bias_full, hidden_out = outs[:units], outs[units], outs[units + 1]
    kept = [outs[units + 2 + 8 * layer : units + 10 + 8 * layer] for layer in range(NL)]
    rest = outs[units + 2 + 8 * NL :]
    weights, (bias_v, allowed, hidden_a, hidden_b) = rest[:4], rest[4:8]
    stores = rest[8:15]
    send_sems, z_sems, xy_sems, core_sems, local_sems, bias_sems, spare = rest[15:22]
    weight_sems, keep_sems = rest[22:]
    y, x, core, z = place()
    b = y * 4 + x * 2 + core
    over_x = y * 4 + (1 - x) * 2 + core
    over_y = (1 - y) * 4 + x * 2 + core
    corner = (1 - y) * 4 + (1 - x) * 2 + core
    at_x = device_at(y, 1 - x, core, z)
    at_y = device_at(1 - y, x, core, z)
    at_core = device_at(y, x, 1 - core, z)
    middle = (z + 1) // 2 % 2
    near = flipped(z, 1)
    across = 3 - z
    far = (z + 2) % 4
    at_near = device_at(y, x, core, near)
    at_across = device_at(y, x, core, across)
    order = (
        near,
        middle * across + (1 - middle) * far,
        middle * far + (1 - middle) * across,
    )
    greet(partners())
    copies = Copies(send_sems)
    conditional = []
    local_of = {}
    for unit in range(units):
        copy = pltpu.make_async_copy(shards[unit], fulls[unit].at[z], local_sems.at[unit])
        copy.start()
        local_of[unit] = copy
    local_bias = pltpu.make_async_copy(bias, bias_full.at[z], local_sems.at[units])
    local_bias.start()
    for entry, bits in enumerate(SWAP_TENSOR):
        copies.send(
            bias,
            bias_full.at[z],
            bias_sems.at[entry],
            device_at(y, x, core, flipped(z, bits)),
        )

    def of_layer(layer):
        return WEIGHT_GROUPS[layer]

    def send_if_middle(source, target, recv_sem, device):
        slot = send_sems.at[copies.count]
        copies.count += 1
        copy = pltpu.make_async_remote_copy(
            src_ref=source,
            dst_ref=target,
            send_sem=slot,
            recv_sem=recv_sem,
            device_id=device,
            device_id_type=MESH,
        )

        @pl.when(middle == 1)
        def _():
            copy.start()

        conditional.append(copy)

    def take_bias():
        for entry, bits in enumerate(SWAP_TENSOR):
            t = flipped(z, bits)
            wait_arrival(
                bias_full.at[t], bias_sems.at[entry], spare.at[0], device_at(y, x, core, t)
            )
        local_bias.wait()
        copy = pltpu.make_async_copy(bias_full, bias_v, weight_sems.at[units])
        copy.start()
        copy.wait()

    def begin(layer):
        for unit in of_layer(layer):
            mine = spread_piece(shards[unit], (), b)
            target = spread_piece(fulls[unit], (z,), b)
            copies.send(mine, target, z_sems.at[unit, z], at_near)
            send_if_middle(mine, target, z_sems.at[unit, z], at_across)

    def take_z(layer, step):
        t = order[step]
        for unit in of_layer(layer):
            piece = spread_piece(fulls[unit], (t,), b)
            wait_arrival(piece, z_sems.at[unit, t], spare.at[0], at_near)
            send_if_middle(
                piece, piece, z_sems.at[unit, t], at_across if step == 0 else at_near
            )
        for unit in of_layer(layer):
            piece = spread_piece(fulls[unit], (t,), b)
            copies.send(piece, piece, xy_sems.at[unit, step, 0], at_x)
            copies.send(piece, piece, xy_sems.at[unit, step, 1], at_y)
            copies.send(piece, piece, core_sems.at[unit, step, 0], at_core)

    def take_xy(layer, step):
        t = order[step]
        for unit in of_layer(layer):
            piece = spread_piece(fulls[unit], (t,), over_x)
            wait_arrival(piece, xy_sems.at[unit, step, 0], spare.at[0], at_x)
            first = half_piece(fulls[unit], (t,), over_x, 0)
            copies.send(first, first, xy_sems.at[unit, step, 2], at_y)
            copies.send(piece, piece, core_sems.at[unit, step, 1], at_core)
        for unit in of_layer(layer):
            piece = spread_piece(fulls[unit], (t,), over_y)
            wait_arrival(piece, xy_sems.at[unit, step, 1], spare.at[0], at_y)
            second = half_piece(fulls[unit], (t,), over_y, 1)
            copies.send(second, second, xy_sems.at[unit, step, 3], at_x)
            copies.send(piece, piece, core_sems.at[unit, step, 2], at_core)

    def take_corner(layer, step):
        t = order[step]
        for unit in of_layer(layer):
            first = half_piece(fulls[unit], (t,), corner, 0)
            second = half_piece(fulls[unit], (t,), corner, 1)
            wait_arrival(first, xy_sems.at[unit, step, 2], spare.at[0], at_y)
            wait_arrival(second, xy_sems.at[unit, step, 3], spare.at[0], at_x)
            piece = spread_piece(fulls[unit], (t,), corner)
            copies.send(piece, piece, core_sems.at[unit, step, 3], at_core)

    def take_core_step(layer, step):
        t = order[step]
        for unit in of_layer(layer):
            for entry, owner in enumerate((b, over_x, over_y, corner)):
                other = owner + 1 - 2 * core
                piece = spread_piece(fulls[unit], (t,), other)
                wait_arrival(piece, core_sems.at[unit, step, entry], spare.at[0], at_core)

    pending = {}

    def keep(entry, layer, source, target):
        copy = pltpu.make_async_copy(source, target, keep_sems.at[layer, entry])
        copy.start()
        pending[entry] = copy

    def free(*entries):
        for entry in entries:
            if entry in pending:
                pending.pop(entry).wait()

    def fetch(group):
        take_core(group)
        copies = []
        for unit in of_layer(group):
            if unit in local_of:
                local_of.pop(unit).wait()
            target = weights[unit % 4]
            copy = pltpu.make_async_copy(
                fulls[unit].reshape(target.shape), target, weight_sems.at[unit]
            )
            copy.start()
            copies.append(copy)
        return copies

    def take_core(group):
        for step in range(3):
            take_core_step(group, step)

    def embed():
        row_index = lax.broadcasted_iota(jnp.int32, (P_SIZE, P_SIZE), 0)
        col_index = lax.broadcasted_iota(jnp.int32, (P_SIZE, P_SIZE), 1)
        for image in range(patches.shape[0] // P_SIZE):
            key_valid = jnp.where(row_index == col_index, 1.0, valid[image : image + 1])
            allowed[image] = jnp.where(col_index <= row_index, key_valid, 0.0)
            rows = slice(image * P_SIZE, (image + 1) * P_SIZE)
            value = product(patches[rows], embed_w[...]) + embed_b[...]
            value = value + table[...].astype(jnp.float32)
            hidden_a[rows] = value + class_rows[image : image + 1]
        keep(7, 0, hidden_a, hidden_out)

    normed, qkv, mixed, hidden_mid, normed_mlp, slope, active = stores
    attend_w, merge_w, up_w, down_w = weights

    def chunks(group):
        layer = WEIGHT_GROUPS[group][0] // 4
        kinds = [unit % 4 for unit in WEIGHT_GROUPS[group]]
        gain, outputs = gains[layer], kept[layer]
        before, after = (hidden_a, hidden_b) if layer % 2 == 0 else (hidden_b, hidden_a)

        def start():
            free(0, 1)
            norm_into(before, gain[0:1], gain[1:2], normed)

            def project(t):
                qkv[t] = back_dot(normed[...], attend_w[t]).astype(qkv.dtype)

            each_part(project)
            keep(0, layer, normed, outputs[0])
            keep(1, layer, qkv, outputs[1])

        def attend_first():
            free(2)
            attend_into(qkv, allowed, mixed, 0, 2)

        def attend_second():
            attend_into(qkv, allowed, mixed, 2, 4)
            keep(2, layer, mixed, outputs[2])

        def merge():
            free(3, 4)
            total = before[...]
            for t in range(4):
                total = total + product(mixed[t], merge_w[t])
            hidden_mid[...] = total
            norm_into(hidden_mid, gain[2:3], gain[3:4], normed_mlp)
            keep(3, layer, hidden_mid, outputs[3])
            keep(4, layer, normed_mlp, outputs[4])

        def up(t):
            inner = product(normed_mlp[...], up_w[t]) + bias_v[t, layer : layer + 1]
            value, rise = gelu_parts(inner)
            active[t] = value.astype(active.dtype)
            slope[t] = rise.astype(slope.dtype)

        def up_first():
            free(5, 6)
            each_part(up, 0, 2)

        def up_second():
            each_part(up, 2, 4)
            keep(5, layer, slope, outputs[5])
            keep(6, layer, active, outputs[6])

        def down():
            free(7 if layer % 2 else 8)
            total = hidden_mid[...] + gain[4:5]
            for t in range(4):
                total = total + product(active[t], down_w[t])
            after[...] = total
            keep(8 - layer % 2, layer, after, outputs[7])

        def nothing():
            pass

        steps = [start, attend_first, attend_second, merge] if 0 in kinds else []
        if 2 in kinds:
            steps += [up_first, up_second]
        if 3 in kinds:
            steps.append(down)
        return steps + [nothing] * (4 - len(steps))

    groups = len(WEIGHT_GROUPS)
    begin(0)
    embed()
    work = None
    for group in range(groups):
        take_z(group, 0)
        if work:
            work[1]()
        take_z(group, 1)
        if work:
            work[2]()
        if group:
            take_corner(group - 1, 1)
        if work:
            work[3]()
        take_xy(group, 0)
        take_z(group, 2)
        if group + 1 < groups:
            begin(group + 1)
        if group:
            take_corner(group - 1, 2)
        take_xy(group, 1)
        loads = fetch(group - 1) if group else ()
        if group == 1:
            take_bias()
        take_corner(group, 0)
        for copy in loads:
            copy.wait()
        work = chunks(group - 1) if group else None
        if work:
            work[0]()
        take_xy(group, 2)
    take_corner(groups - 1, 1)
    if work:
        work[1]()
    take_corner(groups - 1, 2)
    if work:
        work[2]()
        work[3]()
    for copy in fetch(groups - 1):
        copy.wait()
    for chunk in chunks(groups - 1):
        chunk()
    free(*list(pending))
    copies.finish()

    @pl.when(middle == 1)
    def _():
        for copy in conditional:
            copy.wait_send()


def forward_all(shards, bias, embedding, valid, gains):
    units = len(shards)
    rows = embedding[0].shape[0]
    heads = shards[0].size // (3 * HEAD_DIM * D)
    low, full = jnp.bfloat16, jnp.float32
    outs = [jax.ShapeDtypeStruct((4, *shard.shape), shard.dtype) for shard in shards]
    outs.append(jax.ShapeDtypeStruct((4, *bias.shape), bias.dtype))
    outs.append(jax.ShapeDtypeStruct((rows, D), full))
    shapes = layer_shapes(rows, heads)
    outs += shapes * NL
    vmem = pl.BlockSpec(memory_space=pltpu.VMEM)
    anywhere = pl.BlockSpec(memory_space=pl.ANY)
    dma = pltpu.SemaphoreType.DMA
    inputs = [*shards, bias, *embedding, valid, *gains]
    scratch = [pltpu.VMEM((4, shard.size // D, D), low) for shard in shards[:4]]
    scratch.append(pltpu.VMEM((4, *bias.shape), full))
    scratch.append(pltpu.VMEM((rows // P_SIZE, P_SIZE, P_SIZE), full))
    scratch += [pltpu.VMEM((rows, D), full)] * 2
    scratch += [pltpu.VMEM(shape.shape, shape.dtype) for shape in shapes[:7]]
    return pl.pallas_call(
        forward_kernel,
        out_shape=outs,
        in_specs=[vmem] * len(inputs),
        out_specs=[anywhere] * len(outs),
        scratch_shapes=scratch
        + [
            dma((3 + units * (2 + 3 * 9),)),
            dma((units, 4)),
            dma((units, 3, 4)),
            dma((units, 3, 4)),
            dma((units + 1,)),
            dma((3,)),
            dma((1,)),
            dma((units + 1,)),
            dma((NL, 9)),
        ],
        compiler_params=pltpu.CompilerParams(
            collective_id=0, has_side_effects=True, vmem_limit_bytes=BACK_LIMIT
        ),
        name="gather_forward",
    )(*inputs)


def add_slab(target, addend):
    target[...] = (target[...].astype(jnp.float32) + addend[...].astype(jnp.float32)).astype(
        target.dtype
    )


ITEM_ORDER = (3, 0, 2, 1)


def fast_mesh():
    return lax.axis_size("batch") == 8 and lax.axis_size("tensor") == 4


def forward_layers(shards, bias, embedding, valid, allowed, gains):
    if not fast_mesh():
        tensor_count = lax.axis_size("tensor")
        wholes = [
            to_tensor_major(blocks).reshape(tensor_count, -1, D) for blocks in gather_rows(shards)
        ]
        bias_all = lax.all_gather(bias, "tensor", axis=0)
        patches, embed_weight, embed_bias, table, class_rows = embedding
        hidden = product(patches, embed_weight) + embed_bias
        hidden = hidden.reshape(-1, P_SIZE, D) + table.astype(jnp.float32)[None]
        hidden = (hidden + class_rows[:, None]).reshape(-1, D)
        stored = []
        for layer_index in range(NL):
            weights = wholes[4 * layer_index : 4 * layer_index + 4]
            *kept, after = layer_forward(
                hidden, allowed, gains[layer_index], bias_all[:, layer_index], weights
            )
            stored.append((hidden, *kept))
            hidden = after
        return (wholes, stored, hidden)
    parts = [
        shard.reshape((8, -1, D) if shard.shape[0] == D else (-1, 8, 8, D)) for shard in shards
    ]
    results = forward_all(parts, jnp.pad(bias, ((0, 8 - NL), (0, 0))), embedding, valid, gains)
    units = len(shards)
    wholes = [whole.reshape(4, -1, D) for whole in results[:units]]
    hidden = results[units + 1]
    stored = []
    for layer_index in range(NL):
        *kept, after = results[units + 2 + 8 * layer_index : units + 10 + 8 * layer_index]
        stored.append((hidden, *kept))
        hidden = after
    return (wholes, stored, hidden)


def back_dot(former, latter):
    return lax.dot_general(
        former, latter, (((1,), (1,)), ((), ())), preferred_element_type=jnp.float32
    )


def row_blocks(count, size, body, carry=0):
    def step(index, carry):
        return body(pl.ds(pl.multiple_of(index * size, size), size), carry)

    return lax.fori_loop(0, count // size, step, carry)


def norm_into(source, gain, offset, target):
    def body(rows, carry):
        target[rows] = layer_norm(source[rows], gain, offset).astype(target.dtype)
        return carry

    row_blocks(source.shape[0], 128, body)


def norm_back_into(grad, source, upstream, gain):
    def body(rows, carry):
        gain_sum, offset_sum = carry
        values, above = source[rows], upstream[rows]
        center = values - jnp.mean(values, axis=-1, keepdims=True)
        spread = jnp.mean(center * center, axis=-1, keepdims=True)
        scale = lax.rsqrt(spread + EPSILON)
        normal = center * scale
        part = above * gain
        gain_sum = gain_sum + jnp.sum(above * normal, axis=0, keepdims=True)
        offset_sum = offset_sum + jnp.sum(above, axis=0, keepdims=True)
        inner = jnp.mean(part, axis=-1, keepdims=True)
        along = jnp.mean(part * normal, axis=-1, keepdims=True)
        grad[rows] = grad[rows] + scale * (part - inner - normal * along)
        return (gain_sum, offset_sum)

    zero = jnp.zeros((1, D), jnp.float32)
    return row_blocks(source.shape[0], 128, body, (zero, zero))


def head_probs(qkv, allowed, t, rows, image, head):
    span = qkv.shape[2] // 3
    queries, keys, values = (
        qkv[t, rows, c * span + head * HEAD_DIM : c * span + (head + 1) * HEAD_DIM]
        for c in range(3)
    )
    scores = back_dot(queries, keys) * (HEAD_DIM ** (-0.5))
    scores = jnp.where(allowed[image] > 0, scores, NEGATIVE)
    top = jnp.max(scores, axis=-1, keepdims=True)
    powers = jnp.exp(scores - top)
    total = jnp.sum(powers, axis=-1, keepdims=True)
    return (queries, keys, values, powers * (1.0 / total))


def each_image(qkv, body, begin=0, end=4):
    images = qkv.shape[1] // P_SIZE

    def step(index, carry):
        t, image = index // images, index % images
        body(t, image, pl.ds(pl.multiple_of(image * P_SIZE, P_SIZE), P_SIZE))
        return carry

    lax.fori_loop(begin * images, end * images, step, 0)


def attend_into(qkv, allowed, mixed, begin=0, end=4):
    def body(t, image, rows):
        blocks = []
        for head in range(qkv.shape[2] // (3 * HEAD_DIM)):
            queries, keys, values, probs = head_probs(qkv, allowed, t, rows, image, head)
            blocks.append(product(probs.astype(jnp.bfloat16), values))
        mixed[t, rows] = jnp.concatenate(blocks, axis=1).astype(mixed.dtype)

    each_image(qkv, body, begin, end)


def attend_back_into(qkv, allowed, grad_mixed, grad_qkv, begin=0, end=4):
    def body(t, image, rows):
        parts = ([], [], [])
        for head in range(qkv.shape[2] // (3 * HEAD_DIM)):
            queries, keys, values, probs = head_probs(qkv, allowed, t, rows, image, head)
            above = grad_mixed[t, rows, head * HEAD_DIM : (head + 1) * HEAD_DIM]
            grad_values = contract_rows(probs.astype(jnp.bfloat16), above)
            grad_probs = back_dot(above, values)
            inner = jnp.sum(probs * grad_probs, axis=-1, keepdims=True)
            grad_scores = (probs * (grad_probs - inner)).astype(jnp.bfloat16)
            scaling = HEAD_DIM ** (-0.5)
            parts[0].append(product(grad_scores, keys) * scaling)
            parts[1].append(contract_rows(grad_scores, queries) * scaling)
            parts[2].append(grad_values)
        grad_qkv[t, rows] = jnp.concatenate(parts[0] + parts[1] + parts[2], axis=1).astype(
            grad_qkv.dtype
        )

    each_image(qkv, body, begin, end)


def each_part(body, begin=0, end=4):
    def step(t, carry):
        body(t)
        return carry

    lax.fori_loop(begin, end, step, 0)


def layer_forward_chunks(
    hidden, allowed, gains, weights, bias, normed, qkv, mixed, hidden_mid, normed_mlp, slope, active,
    hidden_next,
):
    attend_w, merge_w, up_w, down_w = weights

    def start():
        norm_into(hidden, gains[0:1], gains[1:2], normed)

        def project(t):
            qkv[t] = back_dot(normed[...], attend_w[t]).astype(qkv.dtype)

        each_part(project)

    def attention():
        attend_into(qkv, allowed, mixed)

    def merge():
        total = hidden[...]
        for t in range(4):
            total = total + product(mixed[t], merge_w[t])
        hidden_mid[...] = total
        norm_into(hidden_mid, gains[2:3], gains[3:4], normed_mlp)

    def up(t):
        inner = product(normed_mlp[...], up_w[t]) + bias[pl.ds(t, 1)]
        value, rise = gelu_parts(inner)
        active[t] = value.astype(active.dtype)
        slope[t] = rise.astype(slope.dtype)

    def down():
        total = hidden_mid[...] + gains[4:5]
        for t in range(4):
            total = total + product(active[t], down_w[t])
        hidden_next[...] = total

    return [start, attention, merge, lambda: each_part(up), down]


def layer_forward_kernel(*refs):
    hidden, allowed, gains, bias = refs[:4]
    weights = refs[4:8]
    for chunk in layer_forward_chunks(hidden, allowed, gains, weights, bias, *refs[8:]):
        chunk()


def layer_shapes(rows, heads):
    low, full = jnp.bfloat16, jnp.float32
    return [
        jax.ShapeDtypeStruct((rows, D), low),
        jax.ShapeDtypeStruct((4, rows, heads * 3 * HEAD_DIM), low),
        jax.ShapeDtypeStruct((4, rows, heads * HEAD_DIM), low),
        jax.ShapeDtypeStruct((rows, D), full),
        jax.ShapeDtypeStruct((rows, D), low),
        jax.ShapeDtypeStruct((4, rows, D), low),
        jax.ShapeDtypeStruct((4, rows, D), low),
        jax.ShapeDtypeStruct((rows, D), full),
    ]


VMEM_LIMIT = 62 * 1024 * 1024


def layer_forward(hidden, allowed, gains, bias, weights):
    rows, heads = hidden.shape[0], weights[0].shape[1] // (3 * HEAD_DIM)
    vmem = pl.BlockSpec(memory_space=pltpu.VMEM)
    outs = layer_shapes(rows, heads)
    return pl.pallas_call(
        layer_forward_kernel,
        out_shape=outs,
        in_specs=[vmem] * 8,
        out_specs=[vmem] * len(outs),
        compiler_params=pltpu.CompilerParams(vmem_limit_bytes=VMEM_LIMIT),
        name="layer_forward",
    )(hidden, allowed, gains, bias, *weights)


def layer_backward_chunks(
    grad, allowed, gains, weights, stored, low, grad_inner, grad_mixed, grad_qkv, upstream, rows_out,
    attend_grad, merge_grad, up_grad, down_grad,
):
    attend_w, merge_w, up_w, down_w = weights
    hidden, normed, qkv, mixed, hidden_mid, normed_mlp, slope, active = stored

    def start():
        low[...] = grad[...].astype(low.dtype)
        rows_out[4:5] = jnp.sum(low[...].astype(jnp.float32), axis=0, keepdims=True)
        upstream[...] = jnp.zeros_like(upstream)

    def mlp(t):
        inner = (back_dot(low[...], down_w[t]) * slope[t]).astype(jnp.bfloat16)
        grad_inner[...] = inner
        rows_out[pl.ds(8 + t, 1)] = jnp.sum(inner.astype(jnp.float32), axis=0, keepdims=True)
        up_grad[t] = contract_rows(normed_mlp[...], grad_inner[...]).astype(jnp.bfloat16)
        down_grad[t] = contract_rows(active[t], low[...]).astype(jnp.bfloat16)
        upstream[...] += back_dot(grad_inner[...], up_w[t])

    def middle():
        sums = norm_back_into(grad, hidden_mid, upstream, gains[2:3])
        rows_out[2:3], rows_out[3:4] = sums
        low[...] = grad[...].astype(low.dtype)

        def part(t):
            merge_grad[t] = contract_rows(mixed[t], low[...]).astype(jnp.bfloat16)
            grad_mixed[t] = back_dot(low[...], merge_w[t]).astype(jnp.bfloat16)

        each_part(part)

    def attention():
        attend_back_into(qkv, allowed, grad_mixed, grad_qkv)

    def finish():
        upstream[...] = jnp.zeros_like(upstream)

        def part(t):
            attend_grad[t] = contract_rows(grad_qkv[t], normed[...]).astype(jnp.bfloat16)
            upstream[...] += product(grad_qkv[t], attend_w[t])

        each_part(part)
        sums = norm_back_into(grad, hidden, upstream, gains[0:1])
        rows_out[0:1], rows_out[1:2] = sums

    return [start, lambda: each_part(mlp), middle, attention, finish]


def layer_backward_kernel(*refs):
    grad_in, allowed, gains = refs[:3]
    weights, stored = refs[3:7], refs[7:15]
    grad, rows_out, attend_grad, merge_grad, up_grad, down_grad = refs[15:21]
    low, grad_inner, grad_mixed, grad_qkv, upstream = refs[21:]
    grad[...] = grad_in[...]
    rows_out[...] = jnp.zeros_like(rows_out)
    for chunk in layer_backward_chunks(
        grad, allowed, gains, weights, stored, low, grad_inner, grad_mixed, grad_qkv, upstream,
        rows_out, attend_grad, merge_grad, up_grad, down_grad,
    ):
        chunk()


def layer_backward(grad, allowed, gains, weights, stored):
    rows, heads = grad.shape[0], weights[0].shape[1] // (3 * HEAD_DIM)
    vmem = pl.BlockSpec(memory_space=pltpu.VMEM)
    low, full = jnp.bfloat16, jnp.float32
    outs = [jax.ShapeDtypeStruct((rows, D), full), jax.ShapeDtypeStruct((16, D), full)]
    outs += [jax.ShapeDtypeStruct(weight.shape, low) for weight in weights]
    return pl.pallas_call(
        layer_backward_kernel,
        out_shape=outs,
        in_specs=[vmem] * 15,
        out_specs=[vmem] * len(outs),
        scratch_shapes=[
            pltpu.VMEM((rows, D), low),
            pltpu.VMEM((rows, D), low),
            pltpu.VMEM((4, rows, heads * HEAD_DIM), low),
            pltpu.VMEM((4, rows, heads * 3 * HEAD_DIM), low),
            pltpu.VMEM((rows, D), full),
        ],
        compiler_params=pltpu.CompilerParams(vmem_limit_bytes=VMEM_LIMIT),
        name="layer_backward",
    )(grad, allowed, gains, *weights, *stored)


ATTEND_GROUP, MLP_GROUP, SMALL_GROUP = (0, 1), (2, 3), (4,)
POSITION_ROW, EMBED_ROW, LAYER_ROW, IMAGE_ROW, OTHER_ROW, SMALL_ROWS = 0, 256, 304, 320, 384, 512


def layer_back_kernel(last, *refs):
    grad_in, hidden, hidden_mid, normed, normed_mlp, slope, active, up_w, down_w = refs[:9]
    qkv, mixed, allowed, gains, attend_w, merge_w = refs[9:15]
    refs = refs[15:]
    if last:
        extra, patches = refs[:2]
        refs = refs[2:]
    grad, rows_out = refs[:2]
    refs = refs[2:]
    units = 5 if last else 4
    outs = refs[:units]
    refs = refs[units:]
    grads, got_core, got_one, got_two, got_z, result = (
        refs[units * entry : units * (entry + 1)] for entry in range(6)
    )
    refs = refs[6 * units :]
    if last:
        small_v = refs[0]
        refs = refs[1:]
    low, grad_inner, grad_mixed, grad_qkv, upstream, values, rounded = refs[:7]
    slopes, actives, ups, downs = refs[7:11]
    send_sems, step_sems, z_sems, spread_sems, core_sems, spare, load_sems, stream_sems = refs[11:19]
    total_sems = refs[19]
    if last:
        all_sems = refs[20]
    y, x, core, z = place()
    at_x = device_at(y, 1 - x, core, z)
    at_y = device_at(1 - y, x, core, z)
    at_core = device_at(y, x, 1 - core, z)

    def load(source, target, sem):
        copy = pltpu.make_async_copy(source, target, load_sems.at[sem])
        copy.start()
        return copy

    def stream(step):
        t, slot = ITEM_ORDER[step], step % 2
        pairs = ((down_w, downs), (slope, slopes), (active, actives), (up_w, ups))
        copies = []
        for entry, (source, target) in enumerate(pairs):
            copy = pltpu.make_async_copy(
                source.at[t], target.at[slot], stream_sems.at[slot, entry]
            )
            copy.start()
            copies.append(copy)
        return copies

    first_loads = [load(grad_in, grad, 0)]
    streams = [stream(0), stream(1)]
    first_loads += [load(normed_mlp, rounded, 1), load(hidden_mid, values, 2)]
    greet(partners())
    copies = Copies(send_sems)
    sent_of = {unit: [] for unit in range(len(grads))}
    conditional_of = {unit: [] for unit in range(len(grads))}

    def send_own(unit, *args):
        sent_of[unit].append(copies.send(*args))

    def put(unit, t, value):
        target = grads[unit]
        target[t] = value.reshape(target.shape[1:]).astype(target.dtype)

    def share(group, step):
        t = ITEM_ORDER[step]
        for unit in group:
            copies.send(
                grads[unit].at[t, :, :, :, 1 - core],
                got_core[unit].at[t],
                step_sems.at[unit, 0, t],
                at_core,
            )

    def core_sum(group, step):
        t = ITEM_ORDER[step]
        for unit in group:
            mine, other = grads[unit], got_core[unit]
            wait_arrival(other.at[t], step_sems.at[unit, 0, t], spare.at[0], at_core)

            for spot in ((0, 0), (0, 1), (1, 0), (1, 1)):
                where = (t, slice(None), *spot)
                add_slab(mine.at[(*where, core)], other.at[where])
            if t < 2:
                source, device = mine.at[t, :, :, 1 - x, core], at_x
            else:
                source, device = mine.at[t, :, 1 - y, :, core], at_y
            send_own(unit, source, got_one[unit].at[t], step_sems.at[unit, 1, t], device, False)

    def one(group, step):
        t = ITEM_ORDER[step]
        for unit in group:
            mine, other = grads[unit], got_one[unit]
            wait_arrival(
                other.at[t], step_sems.at[unit, 1, t], spare.at[0], at_x if t < 2 else at_y
            )

            for entry in range(2):
                spot = (entry, x, core) if t < 2 else (y, entry, core)
                add_slab(mine.at[(t, slice(None), *spot)], other.at[t, :, entry])
            if t < 2:
                source, device = mine.at[t, :, 1 - y, x, core], at_y
            else:
                source, device = mine.at[t, :, y, 1 - x, core], at_x
            send_own(unit, source, got_two[unit].at[t], step_sems.at[unit, 2, t], device, False)

    def two(group, step):
        t = ITEM_ORDER[step]
        for unit in group:
            mine, other = grads[unit], got_two[unit]
            wait_arrival(
                other.at[t], step_sems.at[unit, 2, t], spare.at[0], at_y if t < 2 else at_x
            )

            add_slab(mine.at[t, :, y, x, core], other.at[t])
            copy = pltpu.make_async_remote_copy(
                src_ref=mine.at[t, :, y, x, core],
                dst_ref=got_z[unit].at[z],
                send_sem=send_sems.at[copies.count],
                recv_sem=z_sems.at[unit, z],
                device_id=device_at(y, x, core, t),
                device_id_type=MESH,
            )
            copies.count += 1

            @pl.when(z != t)
            def _():
                copy.start()

            conditional_of[unit].append((t, copy))

    def place_of(unit):
        return outs[unit].at[z] if unit in SMALL_GROUP else outs[unit]

    def spot_of(unit, where):
        return place_of(unit).at[(slice(None), *where)]

    def half_spot(unit, where, side):
        spot = place_of(unit)
        count = spot.shape[0]
        if count > 1:
            return spot.at[(halves(count)[side], *where)]
        return spot.at[(slice(None), *where, halves(spot.shape[4])[side])]

    def over_z(group):
        for unit in group:
            mine, other, total = grads[unit], got_z[unit], result[unit]
            for bits in SWAP_TENSOR:
                t = flipped(z, bits)
                wait_arrival(
                    other.at[t], z_sems.at[unit, t], spare.at[0], device_at(y, x, core, t)
                )

            value = mine[z, :, y, x, core].astype(jnp.float32)
            for bits in SWAP_TENSOR:
                value = value + other[flipped(z, bits)].astype(jnp.float32)
            total[...] = value.astype(total.dtype)
            spot = spot_of(unit, (y, x, core))
            pltpu.make_async_copy(total, spot, total_sems.at[unit]).start()
            copies.send(total, spot, spread_sems.at[unit, 0], at_x)
            copies.send(total, spot, spread_sems.at[unit, 1], at_y)
            copies.send(total, spot, core_sems.at[unit, 0], at_core)

    def spread(group):
        for unit in group:
            spot = spot_of(unit, (y, 1 - x, core))
            wait_arrival(spot, spread_sems.at[unit, 0], spare.at[0], at_x)
            first = half_spot(unit, (y, 1 - x, core), 0)
            copies.send(first, first, spread_sems.at[unit, 2], at_y)
            copies.send(spot, spot, core_sems.at[unit, 1], at_core)
            spot = spot_of(unit, (1 - y, x, core))
            wait_arrival(spot, spread_sems.at[unit, 1], spare.at[0], at_y)
            second = half_spot(unit, (1 - y, x, core), 1)
            copies.send(second, second, spread_sems.at[unit, 3], at_x)
            copies.send(spot, spot, core_sems.at[unit, 2], at_core)

    def corner(group):
        for unit in group:
            where = (1 - y, 1 - x, core)
            wait_arrival(half_spot(unit, where, 0), spread_sems.at[unit, 2], spare.at[0], at_y)
            wait_arrival(half_spot(unit, where, 1), spread_sems.at[unit, 3], spare.at[0], at_x)
            spot = spot_of(unit, where)
            copies.send(spot, spot, core_sems.at[unit, 3], at_core)

    def finish(group):
        for unit in group:
            pltpu.make_async_copy(
                result[unit], spot_of(unit, (y, x, core)), total_sems.at[unit]
            ).wait()
            for entry, where in enumerate(((y, x), (y, 1 - x), (1 - y, x), (1 - y, 1 - x))):
                spot = spot_of(unit, (*where, 1 - core))
                wait_arrival(spot, core_sems.at[unit, entry], spare.at[0], at_core)

    def mlp(step):
        t, slot = ITEM_ORDER[step], step % 2
        for copy in streams[step]:
            copy.wait()
        inner = (back_dot(low[...], downs[slot]) * slopes[slot]).astype(jnp.bfloat16)
        grad_inner[...] = inner
        rows_out[8 + t : 9 + t] = jnp.sum(inner.astype(jnp.float32), axis=0, keepdims=True)
        put(2, t, contract_rows(rounded[...], grad_inner[...]))
        put(3, t, contract_rows(actives[slot], low[...]))
        upstream[...] += back_dot(grad_inner[...], ups[slot])
        if step < 2:
            streams.append(stream(step + 2))
        share(MLP_GROUP, step)

    def project(step):
        t = ITEM_ORDER[step]
        put(0, t, contract_rows(grad_qkv[t], rounded[...]))
        put(1, t, contract_rows(mixed[t], low[...]))
        upstream[...] += product(grad_qkv[t], attend_w[t])
        share(ATTEND_GROUP, step)

    def collect_small():
        rows_out[5:6] = jnp.sum(grad[...], axis=0, keepdims=True)
        small_v[LAYER_ROW : LAYER_ROW + 16] = rows_out[...]
        images = grad.shape[0] // P_SIZE
        total = grad[:P_SIZE]
        for image in range(1, images):
            total = total + grad[image * P_SIZE : (image + 1) * P_SIZE]
        small_v[POSITION_ROW : POSITION_ROW + P_SIZE] = total
        first = grad[...].astype(jnp.bfloat16)
        second = (grad[...] - first.astype(jnp.float32)).astype(jnp.bfloat16)
        small_v[EMBED_ROW : EMBED_ROW + PV] = contract_rows(patches[...], first) + contract_rows(
            patches[...], second
        )
        device_index = lax.axis_index("batch") * 4 + z
        for image in range(images):
            rows = grad[image * P_SIZE : (image + 1) * P_SIZE]
            spot = IMAGE_ROW + device_index * images + image
            small_v[pl.ds(spot, 1)] = jnp.sum(rows, axis=0, keepdims=True)
        for t in range(4):
            part = small_v.shape[0] // 4
            put(4, t, small_v[t * part : (t + 1) * part])

    rows_out[...] = jnp.zeros_like(rows_out)
    if last:
        extra_load = load(extra, small_v, 3)
    for copy in first_loads:
        copy.wait()
    low[...] = grad[...].astype(low.dtype)
    rows_out[4:5] = jnp.sum(low[...].astype(jnp.float32), axis=0, keepdims=True)
    upstream[...] = jnp.zeros_like(upstream)
    mlp(0)
    mlp(1)
    core_sum(MLP_GROUP, 0)
    mlp(2)
    core_sum(MLP_GROUP, 1)
    mlp(3)
    core_sum(MLP_GROUP, 2)
    one(MLP_GROUP, 0)
    rows_out[2:3], rows_out[3:4] = norm_back_into(grad, values, upstream, gains[2:3])
    later_loads = [load(hidden, values, 2), load(normed, rounded, 1)]
    low[...] = grad[...].astype(low.dtype)
    for t in range(4):
        grad_mixed[t] = back_dot(low[...], merge_w[t]).astype(grad_mixed.dtype)
    core_sum(MLP_GROUP, 3)
    one(MLP_GROUP, 1)
    attend_back_into(qkv, allowed, grad_mixed, grad_qkv, 0, 2)
    one(MLP_GROUP, 2)
    two(MLP_GROUP, 0)
    attend_back_into(qkv, allowed, grad_mixed, grad_qkv, 2, 4)
    one(MLP_GROUP, 3)
    two(MLP_GROUP, 1)
    upstream[...] = jnp.zeros_like(upstream)
    for copy in later_loads:
        copy.wait()
    project(0)
    project(1)
    core_sum(ATTEND_GROUP, 0)
    two(MLP_GROUP, 2)
    project(2)
    core_sum(ATTEND_GROUP, 1)
    two(MLP_GROUP, 3)
    project(3)
    core_sum(ATTEND_GROUP, 2)
    one(ATTEND_GROUP, 0)
    rows_out[0:1], rows_out[1:2] = norm_back_into(grad, values, upstream, gains[0:1])
    if last:
        extra_load.wait()
        collect_small()
        for step in range(4):
            share(SMALL_GROUP, step)
    core_sum(ATTEND_GROUP, 3)
    one(ATTEND_GROUP, 1)
    over_z(MLP_GROUP)
    two(ATTEND_GROUP, 0)
    if last:
        for step in range(4):
            core_sum(SMALL_GROUP, step)
    one(ATTEND_GROUP, 2)
    two(ATTEND_GROUP, 1)
    if last:
        for step in range(4):
            one(SMALL_GROUP, step)
    one(ATTEND_GROUP, 3)
    spread(MLP_GROUP)
    two(ATTEND_GROUP, 2)
    if last:
        for step in range(4):
            two(SMALL_GROUP, step)
    corner(MLP_GROUP)
    two(ATTEND_GROUP, 3)
    over_z(ATTEND_GROUP)
    if last:
        over_z(SMALL_GROUP)
    spread(ATTEND_GROUP)
    if last:
        spread(SMALL_GROUP)
    corner(ATTEND_GROUP)
    if last:
        corner(SMALL_GROUP)
        finish(SMALL_GROUP)
        (unit,) = SMALL_GROUP
        for bits in SWAP_TENSOR:
            at_t = device_at(y, x, core, flipped(z, bits))
            copies.send(outs[unit].at[z], outs[unit].at[z], all_sems.at[bits], at_t)
    finish(MLP_GROUP)
    finish(ATTEND_GROUP)
    if last:
        for bits in SWAP_TENSOR:
            t = flipped(z, bits)
            wait_arrival(
                outs[unit].at[t], all_sems.at[bits], spare.at[0], device_at(y, x, core, t)
            )
    copies.finish()
    for unit in sent_of:
        for copy in sent_of[unit]:
            copy.wait_send()
        for t, copy in conditional_of[unit]:

            @pl.when(z != t)
            def _(copy=copy):
                copy.wait_send()


def owner_shape(weight):
    count = 1 if weight.shape[1] == D else weight.shape[1] // 64
    return (count, 2, 2, 2, weight.shape[1] // (8 * count), D)


def layer_back_reduce(layer_index, grad, allowed, gains, weights, stored, extra=None, patches=None):
    hidden, normed, qkv, mixed, hidden_mid, normed_mlp, slope, active = stored
    attend_w, merge_w, up_w, down_w = weights
    last = layer_index == 0
    rows, heads = grad.shape[0], attend_w.shape[1] // (3 * HEAD_DIM)
    low, full = jnp.bfloat16, jnp.float32
    vmem = pl.BlockSpec(memory_space=pltpu.VMEM)
    anywhere = pl.BlockSpec(memory_space=pl.ANY)
    shapes = [owner_shape(weight) for weight in weights]
    if last:
        shapes.append((1, 2, 2, 2, SMALL_ROWS // 32, D))
    scratch = []
    for lead in ((4, 2, 2, 2), (4, 2, 2), (4, 2), (4,), (4,), ()):
        for shape in shapes:
            whole = lead[:1] + shape[:1] + lead[1:] + shape[4:]
            scratch.append(pltpu.VMEM(whole, low))
    count = len(shapes)
    if last:
        scratch.append(pltpu.VMEM((SMALL_ROWS, D), full))
    dma = pltpu.SemaphoreType.DMA
    scratch += [
        pltpu.VMEM((rows, D), low),
        pltpu.VMEM((rows, D), low),
        pltpu.VMEM((4, rows, heads * HEAD_DIM), low),
        pltpu.VMEM((4, rows, heads * 3 * HEAD_DIM), low),
        pltpu.VMEM((rows, D), full),
        pltpu.VMEM((rows, D), full),
        pltpu.VMEM((rows, D), low),
        pltpu.VMEM((2, rows, D), slope.dtype),
        pltpu.VMEM((2, rows, D), low),
        pltpu.VMEM((2, D, D), low),
        pltpu.VMEM((2, D, D), low),
        dma((count * 24 + 3,)),
        dma((count, 3, 4)),
        dma((count, 4)),
        dma((count, 4)),
        dma((count, 4)),
        dma((1,)),
        dma((4,)),
        dma((2, 4)),
        dma((count,)),
    ]
    if last:
        scratch.append(dma((4,)))
    outs = [jax.ShapeDtypeStruct((rows, D), full), jax.ShapeDtypeStruct((16, D), full)]
    outs += [jax.ShapeDtypeStruct(shape, low) for shape in shapes[:4]]
    if last:
        outs.append(jax.ShapeDtypeStruct((4, *shapes[4]), low))
    inputs = [grad, hidden, hidden_mid, normed, normed_mlp, slope, active, up_w, down_w]
    specs = [anywhere] * 9 + [vmem] * 6
    inputs += [qkv, mixed, allowed, gains, attend_w, merge_w]
    if last:
        inputs += [extra, patches]
        specs += [anywhere, vmem]
    return pl.pallas_call(
        functools.partial(layer_back_kernel, last),
        out_shape=outs,
        in_specs=specs,
        out_specs=[vmem] * 2 + [anywhere] * (len(outs) - 2),
        scratch_shapes=scratch,
        compiler_params=pltpu.CompilerParams(
            collective_id=2 + layer_index, has_side_effects=True, vmem_limit_bytes=BACK_LIMIT
        ),
        name="layer_back_reduce",
    )(*inputs)


BACK_LIMIT = 66 * 1000 * 1000


def shards(
    patches,
    valid_mask,
    class_ids,
    embed_weight,
    embed_bias,
    position_table,
    class_table,
    attn_gain,
    attn_offset,
    attend_weight,
    merge_weight,
    mlp_gain,
    mlp_offset,
    up_weight,
    up_bias,
    down_weight,
    down_bias,
    final_gain,
    final_offset,
    head_weight,
    head_bias,
    latent_cot,
    logdet_cot,
):
    shard_count = patches.shape[0]
    local_images = shard_count // P_SIZE
    tensor_index = lax.axis_index("tensor")
    tensor_count = lax.axis_size("tensor")
    batch_count = lax.axis_size("batch")
    device_index = lax.axis_index("batch") * tensor_count + tensor_index
    device_count = batch_count * tensor_count
    patch_values = patches.astype(jnp.float32)
    local_valid = lax.dynamic_slice_in_dim(valid_mask, tensor_index * shard_count, shard_count, 0)
    live_mask = local_valid.astype(jnp.float32)[:, None]
    allowed = build_allowed(local_valid, P_SIZE).astype(jnp.float32)
    embed_full = embed_weight.astype(jnp.float32)
    shards = []
    for layer_index in range(NL):
        shards.append(jnp.swapaxes(attend_weight[layer_index], 1, 2).reshape(-1, D))
        shards.append(merge_weight[layer_index])
        shards.append(up_weight[layer_index])
        shards.append(down_weight[layer_index])
    gains = [
        jnp.stack(
            [attn_gain[layer_index], attn_offset[layer_index], mlp_gain[layer_index]]
            + [mlp_offset[layer_index], down_bias[layer_index]]
        )
        for layer_index in range(NL)
    ]
    choose = class_ids[:, None] == lax.broadcasted_iota(jnp.int32, (local_images, CLASSES), 1)
    class_rows = product(choose.astype(jnp.bfloat16), class_table)
    embedding = (patches, embed_weight, embed_bias[None], position_table, class_rows)
    valid_rows = local_valid.astype(jnp.float32).reshape(local_images, P_SIZE)
    wholes, stored, hidden = forward_layers(
        shards, up_bias, embedding, valid_rows, allowed, gains
    )
    final = layer_norm(hidden, final_gain, final_offset)
    final_low = final.astype(jnp.bfloat16)
    head_out = product(final_low, head_weight) + head_bias
    position = lax.broadcasted_iota(jnp.int32, (shard_count, 1), 0) % P_SIZE
    starts = position == 0
    previous = jnp.concatenate([jnp.zeros((1, 2 * PV), jnp.float32), head_out[:-1]], axis=0)
    previous = jnp.where(starts, 0.0, previous)
    shift_part = previous[:, :PV]
    log_scale = previous[:, PV:]
    scale_factor = jnp.exp(-log_scale)
    latents = (
        live_mask * (patch_values - shift_part) * scale_factor + (1.0 - live_mask) * patch_values
    )
    log_det = -jnp.sum((live_mask * log_scale).reshape(local_images, P_SIZE * PV), axis=1)
    image_cot = jnp.repeat(logdet_cot, P_SIZE)[:, None]
    direct_grad = latent_cot * (live_mask * scale_factor + (1.0 - live_mask))
    grad_shift = -live_mask * latent_cot * scale_factor
    grad_scale = -live_mask * (latent_cot * (patch_values - shift_part) * scale_factor + image_cot)
    grad_previous = jnp.where(starts, 0.0, jnp.concatenate([grad_shift, grad_scale], axis=1))
    grad_head = jnp.concatenate([grad_previous[1:], jnp.zeros((1, 2 * PV), jnp.float32)], axis=0)
    grad_head_low = grad_head.astype(jnp.bfloat16)
    head_weight_grad = contract_rows(grad_head_low, final_low)
    head_bias_grad = jnp.sum(grad_head_low.astype(jnp.float32), axis=0)
    grad_final = back_dot(grad_head_low, head_weight)
    grad_hidden, final_gain_grad, final_offset_grad = norm_backward(
        hidden, final_gain, final_offset, grad_final
    )
    image_count = device_count * local_images
    image_index = device_index * local_images
    id_rows = jnp.stack([class_ids // 32, class_ids % 32]).astype(jnp.float32)
    id_rows = lax.dynamic_update_slice(jnp.zeros((2, D), jnp.float32), id_rows, (0, image_index))
    other = [
        head_weight_grad,
        final_gain_grad[None],
        final_offset_grad[None],
        jnp.pad(head_bias_grad, (0, D - 2 * PV))[None],
        id_rows,
    ]
    if fast_mesh():
        grad_hidden, layer_rows, *later_sums = layer_back_reduce(
            1, grad_hidden, allowed, gains[1], wholes[4:], stored[1]
        )
        other = jnp.concatenate([jnp.zeros((OTHER_ROW, D), jnp.float32), layer_rows] + other)
        other = jnp.pad(other, ((0, SMALL_ROWS - other.shape[0]), (0, 0)))
        grad_hidden, layer_rows, *sums = layer_back_reduce(
            0, grad_hidden, allowed, gains[0], wholes[:4], stored[0], other, patches
        )
        small_sum = sums[4].reshape(-1, D)
        sums = [entry.reshape(-1, D) for entry in sums[:4] + later_sums]
    else:
        rows_of = {}
        split_list = [None] * NL
        for layer_index in reversed(range(NL)):
            weights = wholes[4 * layer_index : 4 * layer_index + 4]
            grad_hidden, rows_of[layer_index], *split_list[layer_index] = layer_backward(
                grad_hidden, allowed, gains[layer_index], weights, stored[layer_index]
            )
        per_image = grad_hidden.reshape(local_images, P_SIZE, D)
        image_rows = lax.dynamic_update_slice_in_dim(
            jnp.zeros((image_count, D), jnp.float32), jnp.sum(per_image, axis=1), image_index, 0
        )
        first_rows = lax.dynamic_update_slice_in_dim(
            rows_of[0], jnp.sum(grad_hidden, axis=0)[None], 5, 0
        )
        small = [
            jnp.sum(per_image, axis=0),
            precise_rows(patch_values, grad_hidden),
            first_rows,
            image_rows,
            rows_of[1],
        ]
        joined = jnp.concatenate(small + other, axis=0)
        joined = jnp.pad(joined, ((0, -joined.shape[0] % (8 * device_count)), (0, 0)))
        grads = [grad.reshape(-1, D) for grad in split_list[0] + split_list[1]]
        sums = reduce_rows([to_batch_major(grad) for grad in grads] + [split_blocks(joined)])
        small_sum = lax.all_gather(sums[-1], "tensor", axis=1).reshape(-1, D)
        sums = [entry.reshape(-1, D) for entry in sums[:-1]]
    split_list = [None] * NL
    for layer_index in range(NL):
        attend_sum, merge_sum, up_sum, down_sum = sums[4 * layer_index : 4 * layer_index + 4]
        split_list[layer_index] = (
            jnp.swapaxes(attend_sum.reshape(3, -1, D), 1, 2).astype(jnp.float32),
            merge_sum.astype(jnp.float32),
            up_sum.astype(jnp.float32),
            down_sum.astype(jnp.float32),
        )
    patches_grad = direct_grad + lax.dot_general(
        grad_hidden,
        embed_full,
        (((1,), (1,)), ((), ())),
        precision=HIGHEST,
        preferred_element_type=jnp.float32,
    )
    small_sum = small_sum.astype(jnp.float32)
    other_row = IMAGE_ROW + image_count
    row = other_row + 16 + 2 * PV
    id_sums = small_sum[row + 3 : row + 5, :image_count].astype(jnp.int32)
    all_ids = id_sums[0] * 32 + id_sums[1]
    choose_all = all_ids[:, None] == lax.broadcasted_iota(
        jnp.int32, (image_count, CLASSES), 1
    )
    class_grad = precise_rows(
        choose_all.astype(jnp.float32), small_sum[IMAGE_ROW:other_row]
    )
    layer_rows = [small_sum[LAYER_ROW : LAYER_ROW + 16], small_sum[other_row : other_row + 16]]
    own_bias = [lax.dynamic_slice_in_dim(entry, 8 + tensor_index, 1, 0) for entry in layer_rows]
    split_stack = [jnp.stack([entry[member] for entry in split_list]) for member in range(4)]
    shared_stack = [
        jnp.stack([entry[member] for entry in layer_rows]) for member in range(5)
    ]
    return (
        latents,
        log_det,
        patches_grad,
        small_sum[EMBED_ROW : EMBED_ROW + PV],
        layer_rows[0][5],
        small_sum[:P_SIZE],
        class_grad,
        shared_stack[0],
        shared_stack[1],
        split_stack[0],
        split_stack[1],
        shared_stack[2],
        shared_stack[3],
        split_stack[2],
        jnp.concatenate(own_bias, axis=0),
        split_stack[3],
        shared_stack[4],
        small_sum[row],
        small_sum[row + 1],
        jnp.swapaxes(small_sum[other_row + 16 : row], 0, 1),
        small_sum[row + 2, : 2 * PV],
    )


def solution(mesh):
    return jax.shard_map(
        shards,
        mesh=mesh,
        in_specs=(
            P(("batch", "tensor"), None),
            P("batch"),
            P(("batch", "tensor")),
            P(),
            P(),
            P(),
            P(),
            P(),
            P(),
            P(None, None, None, "tensor"),
            P(None, "tensor", None),
            P(),
            P(),
            P(None, None, "tensor"),
            P(None, "tensor"),
            P(None, "tensor", None),
            P(),
            P(),
            P(),
            P(),
            P(),
            P(("batch", "tensor"), None),
            P(("batch", "tensor")),
        ),
        out_specs=(
            P(("batch", "tensor"), None),
            P(("batch", "tensor")),
            P(("batch", "tensor"), None),
            P(),
            P(),
            P(),
            P(),
            P(),
            P(),
            P(None, None, None, "tensor"),
            P(None, "tensor", None),
            P(),
            P(),
            P(None, None, "tensor"),
            P(None, "tensor"),
            P(None, "tensor", None),
            P(),
            P(),
            P(),
            P(),
            P(),
        ),
        check_vma=False,
    )
```
